128 devices in a mesh: comp: 2 (over core), tile: 64 (over x, z, y).
Axes of the slice: x: 4, y: 4, z: 4, core: 2. Of those that a mesh axis runs over, the one named last changes fastest.
Arguments:
- fields: float32 [2, 8, 524288], P('comp', None, 'tile'), may hold values from -6 to 6
- level_rate: float32 [2, 8], P('comp'), may hold values from 0.1 to 0.9
- edge_weight: float32 [2, 3, 524288], P('comp', None, 'tile'), may hold values from 0.5 to 2
- fine_diagonal: float32 [2, 524288], P('comp', 'tile'), may hold values from 0.1 to 1
- fine_table: int32 [2, 3, 524288], P('comp', None, 'tile'), may hold values from 0 to 8447, as said below
- old_height: float32 [2, 524288], P('comp', 'tile'), may hold values from -6 to 6
- level_weight: float32 [2, 8], P('comp'), may hold values from 0.1 to 0.6
- flux_weight: float32 [2, 4], P('comp'), may hold values from 0.2 to 1
- fine_owner: int32 [2, 524288], P('comp', 'tile'), may hold values from 0 to 1023, as said below
- coarse_table: int32 [2, 3, 65536], P('comp', None, 'tile'), may hold values from 0 to 1055, as said below
- coarse_edge: float32 [2, 3, 65536], P('comp', None, 'tile'), may hold values from 2 to 8
- coarse_diagonal: float32 [2, 65536], P('comp', 'tile'), may hold values from 0.5 to 5
- coarse_owner: int32 [2, 65536], P('comp', 'tile'), may hold values from 0 to 15, as said below
- coarse_inverse: float32 [2, 1024, 1024], P('comp', 'tile'), may hold values from -0.05 to 0.05, as said below
- surface_out: bfloat16 [2, 4, 524288], P('comp', None, 'tile'), may hold values from -6 to 6
- send_blocks: int32 [2, 64, 160], P('comp', 'tile'), may hold values from 0 to 64, as said below
- entry_slot: int32 [2, 64, 160], P('comp', 'tile'), may hold values from 0 to 159, as said below
- entry_block: int32 [2, 64, 160], P('comp', 'tile'), may hold values from 0 to 63, as said below
- remap_tiles: bfloat16 [2, 64, 160, 128, 128], P('comp', 'tile'), may hold values from 0 to 0.17675781
Outputs:
- new_fields: float32 [2, 8, 524288], P('comp', None, 'tile')
- received: float32 [2, 4, 524288], P('comp', None, 'tile')
- height: float32 [2, 524288], P('comp', 'tile')
The draws below stay inside these ranges and needn't reach their ends.
Inputs may be any that keep to these rules, and one draw needn't show every extreme that they name: A position in the cells of the cell's own device, extended by 128 cells on each side (the loop of tiles closes), lying within 128 cells of the cell itself: fine_table[g, k, c] - 128 - (c mod 8192) is between -128 and 128. A position in the first-level cells of the cell's own device, extended by 16 cells on each side (the loop of tiles closes), lying within 16 cells of the cell itself: coarse_table[g, k, a] - 16 - (a mod 1024) is between -16 and 16. `fine_owner`: nondecreasing within each device's cells; every aggregate of a device owns at least one cell. `coarse_owner`: nondecreasing within each device's first-level cells; every aggregate owns at least one cell. `coarse_inverse`: exactly symmetric. `send_blocks`: for each offset j, the used slots come first and at least one is used; 64 marks an unused slot; on some offset of every device all 32 slots are used. `entry_slot`: names a used slot of the receiving device; every used slot is named by some entry. `entry_block`: nondecreasing along the entries of a device; every block is named.
All inputs are finite; a program needn't handle non-finite values.
Results may differ from the reference program's by a relative error of at most 0.0003.
Values may be sent and summed in bfloat16 or wider, within the bound.
A program may use at most 128 MiB of HBM per device.

```python
import math
import jax
import jax.numpy as jnp
from jax import lax

LEV = 8
NF = 4
TILE_W = 128
HALO = 128
CD = 8192
CELLS = 524288
CDB = 64
SLOT = 32
RB = 160
C1 = 1024
C2 = 16
HALO1 = 16
L1CELLS = 65536
NC2 = 1024
N_TILE = 64


def neighbour_table(base_key, cells_dev, cell_total, halo_width):
    first_key, second_key, third_key = jax.random.split(base_key, 3)
    table_shape = (2, cell_total)
    upward = jax.random.randint(first_key, table_shape, 1, 5)
    downward = -jax.random.randint(second_key, table_shape, 1, 5)
    distant = jax.random.randint(third_key, table_shape, -halo_width, halo_width + 1)
    local_cell = jnp.arange(cell_total, dtype=jnp.int32) % cells_dev
    distant = jnp.where(local_cell == 0, -halo_width, distant)
    distant = jnp.where(local_cell == cells_dev - 1, halo_width, distant)
    offsets = jnp.stack([upward, downward, distant], axis=1)
    return (local_cell[None, None, :] + halo_width + offsets).astype(jnp.int32)


def owner_table(base_key, cells_dev, owners_dev, cell_total):
    row_count = 2 * cell_total // cells_dev
    extra_ids = jax.random.randint(base_key, (row_count, cells_dev - owners_dev), 0, owners_dev)
    every_id = jnp.broadcast_to(jnp.arange(owners_dev, dtype=jnp.int32), (row_count, owners_dev))
    joined = jnp.sort(jnp.concatenate([every_id, extra_ids.astype(jnp.int32)], axis=1), axis=1)
    return joined.reshape(2, cell_total)


def send_layout(base_key):
    tile_total = CELLS // CD
    block_key, count_key, full_key = jax.random.split(jax.random.fold_in(base_key, 17), 3)
    counts = jax.random.randint(count_key, (2, tile_total, 5), 1, SLOT + 1)
    full_offset = jax.random.randint(full_key, (2, tile_total), 0, 5)
    full_offset = full_offset.at[:, 0].set(4)
    counts = jnp.where(jnp.arange(5)[None, None, :] == full_offset[:, :, None], SLOT, counts)
    chosen = jax.random.randint(block_key, (2, tile_total, 5, SLOT), 0, CDB)
    used = jnp.arange(SLOT)[None, None, None, :] < counts[:, :, :, None]
    blocks = jnp.where(used, chosen, CDB).astype(jnp.int32)
    return (blocks.reshape(2, tile_total, 5 * SLOT), used.reshape(2, tile_total, 5 * SLOT))


def entry_layout(base_key):
    tile_total = CELLS // CD
    blocks, used = send_layout(base_key)
    slot_column = jnp.arange(5 * SLOT, dtype=jnp.int32)
    source_tile = (jnp.arange(tile_total, dtype=jnp.int32)[:, None] + slot_column[None, :] // SLOT - 2) % tile_total
    live_slot = used[::-1][:, source_tile, slot_column[None, :]].astype(jnp.int32)
    live_count = jnp.sum(live_slot, axis=-1)
    running = jnp.cumsum(live_slot, axis=-1)
    pick_key, order_key, block_key = jax.random.split(jax.random.fold_in(base_key, 29), 3)
    entry_number = jnp.arange(RB, dtype=jnp.int32)
    random_pick = jax.random.randint(pick_key, (2, tile_total, RB), 0, live_count[:, :, None])
    slot_rank = jnp.where(entry_number[None, None, :] < live_count[:, :, None], entry_number[None, None, :], random_pick)
    slot_rank = slot_rank[:, :, jax.random.permutation(order_key, RB)]
    slot_choice = jnp.sum(running[:, :, None, :] <= slot_rank[:, :, :, None], axis=-1).astype(jnp.int32)
    extra_ids = jax.random.randint(block_key, (2, tile_total, RB - CDB), 0, CDB)
    every_id = jnp.broadcast_to(jnp.arange(CDB, dtype=jnp.int32), (2, tile_total, CDB))
    owners = jnp.sort(jnp.concatenate([every_id, extra_ids.astype(jnp.int32)], axis=-1), axis=-1)
    return (slot_choice, owners)


def draw_fine_table(key, part):
    return neighbour_table(jax.random.fold_in(key, 3), CD, CELLS, HALO)


def draw_coarse_table(key, part):
    return neighbour_table(jax.random.fold_in(key, 5), C1, L1CELLS, HALO1)


def draw_fine_owner(key, part):
    return owner_table(jax.random.fold_in(key, 7), CD, C1, CELLS)


def draw_coarse_owner(key, part):
    return owner_table(jax.random.fold_in(key, 9), C1, C2, L1CELLS)


def draw_send_blocks(key, part):
    return send_layout(key)[0]


def draw_entry_slot(key, part):
    return entry_layout(key)[0]


def draw_entry_block(key, part):
    return entry_layout(key)[1]


def draw_coarse_inverse(key, part):
    diag_key, noise_key = jax.random.split(jax.random.fold_in(key, 41))
    diagonal = jnp.exp(jax.random.uniform(diag_key, (2, NC2), jnp.float32, jnp.log(0.002), jnp.log(0.02)))
    raw_noise = jax.random.normal(noise_key, (2, NC2, NC2), jnp.float32)
    symmetric = (raw_noise + jnp.swapaxes(raw_noise, 1, 2)) * (0.35 / NC2 ** 0.5)
    scale_pair = jnp.sqrt(diagonal[:, :, None] * diagonal[:, None, :])
    return symmetric * scale_pair + diagonal[:, :, None] * jnp.eye(NC2, dtype=jnp.float32)[None]


def block_levels(key, dims, pieces, least, high):
    def one(axis_at, parts):
        draws = jax.random.uniform(jax.random.fold_in(jax.random.fold_in(key, 6), axis_at), (parts,), jnp.float32, least / len(pieces), high / len(pieces))
        return jnp.repeat(jnp.exp(draws), dims[axis_at] // parts).reshape((-1,) + (1,) * (len(dims) - axis_at - 1))

    level = one(*pieces[0])
    for cut in pieces[1:]:
        level = level * one(*cut)
    return level


def normal_values(stream_key, dims, deviation, most, cuts=(), held_as=jnp.bfloat16):
    values = jax.random.normal(stream_key, dims, jnp.float32) * deviation
    if len(cuts) > 0:
        values = block_levels(stream_key, dims, cuts, -0.22, 0.18) * values
    return jnp.clip(values, min=-most, max=most).astype(held_as)


def setup_inputs(seed: int = 0) -> dict:
    splits = jax.random.split(jax.random.key(seed), 20)
    fields = normal_values(splits[0], (2, LEV, CELLS), 1.0, 6.0, ((0, 2), (2, 64)), jnp.float32)
    level_rate = jnp.clip(jnp.exp(math.log(0.9) - 2.1972245 * jax.random.uniform(splits[1], (2, LEV), jnp.float32) ** block_levels(splits[1], (2, LEV), ((0, 2),), -0.2, 0.2)), 0.1, 0.9)
    edge_weight = jnp.clip(jnp.exp(math.log(2.0) - 1.3862944 * jax.random.uniform(splits[2], (2, 3, CELLS), jnp.float32) ** block_levels(splits[2], (2, 3, CELLS), ((0, 2), (2, 64)), -0.2, 0.2)), 0.5, 2.0)
    fine_diagonal = jnp.clip(jnp.exp(math.log(1.0) - 2.3025851 * jax.random.uniform(splits[3], (2, CELLS), jnp.float32) ** block_levels(splits[3], (2, CELLS), ((0, 2), (1, 64)), -0.2, 0.2)), 0.1, 1.0)
    fine_table = draw_fine_table(jax.random.fold_in(splits[19], 71), 0)
    old_height = normal_values(splits[5], (2, CELLS), 1.0, 6.0, ((0, 2), (1, 64)), jnp.float32)
    level_weight = jnp.clip(0.1 + 0.5 * jax.random.uniform(splits[6], (2, LEV), jnp.float32) ** block_levels(splits[6], (2, LEV), ((0, 2),), -0.2, 0.2), 0.1, 0.6)
    flux_weight = jnp.clip(0.2 + 0.8 * jax.random.uniform(splits[7], (2, NF), jnp.float32) ** block_levels(splits[7], (2, NF), ((0, 2),), -0.2, 0.2), 0.2, 1.0)
    fine_owner = draw_fine_owner(jax.random.fold_in(splits[19], 71), 0)
    coarse_table = draw_coarse_table(jax.random.fold_in(splits[19], 71), 0)
    coarse_edge = jnp.clip(jnp.exp(math.log(8.0) - 1.3862944 * jax.random.uniform(splits[10], (2, 3, L1CELLS), jnp.float32) ** block_levels(splits[10], (2, 3, L1CELLS), ((0, 2), (2, 64)), -0.2, 0.2)), 2.0, 8.0)
    coarse_diagonal = jnp.clip(jnp.exp(math.log(5.0) - 2.3025851 * jax.random.uniform(splits[11], (2, L1CELLS), jnp.float32) ** block_levels(splits[11], (2, L1CELLS), ((0, 2), (1, 64)), -0.2, 0.2)), 0.5, 5.0)
    coarse_owner = draw_coarse_owner(jax.random.fold_in(splits[19], 71), 0)
    coarse_inverse = draw_coarse_inverse(jax.random.fold_in(splits[19], 71), 0)
    surface_out = normal_values(splits[14], (2, NF, CELLS), 1.0, 6.0, ((0, 2), (2, 64)))
    send_blocks = draw_send_blocks(jax.random.fold_in(splits[19], 71), 0)
    entry_slot = draw_entry_slot(jax.random.fold_in(splits[19], 71), 0)
    entry_block = draw_entry_block(jax.random.fold_in(splits[19], 71), 0)
    remap_tiles = jnp.clip(0.17675781 * jax.random.uniform(splits[18], (2, N_TILE, RB, TILE_W, TILE_W), jnp.float32) ** block_levels(splits[18], (2, N_TILE, RB, TILE_W, TILE_W), ((0, 2), (1, 64)), -0.2, 0.2), 0.0, 0.17675781).astype(jnp.bfloat16)
    return dict(fields=fields, level_rate=level_rate, edge_weight=edge_weight, fine_diagonal=fine_diagonal, fine_table=fine_table, old_height=old_height, level_weight=level_weight, flux_weight=flux_weight, fine_owner=fine_owner, coarse_table=coarse_table, coarse_edge=coarse_edge, coarse_diagonal=coarse_diagonal, coarse_owner=coarse_owner, coarse_inverse=coarse_inverse, surface_out=surface_out, send_blocks=send_blocks, entry_slot=entry_slot, entry_block=entry_block, remap_tiles=remap_tiles)


RELAXATION = 0.8


def neighbour_index(local_table, cells_dev, halo_width, cell_total):
    position = jnp.arange(cell_total, dtype=jnp.int32)
    first_cell = (position // cells_dev) * cells_dev
    return (first_cell[None, :] + local_table.astype(jnp.int32) - halo_width) % cell_total


def owner_index(local_owner, cells_dev, owners_dev):
    position = jnp.arange(local_owner.shape[0], dtype=jnp.int32)
    return (position // cells_dev) * owners_dev + local_owner.astype(jnp.int32)


def apply_operator(values, neighbours, weights, diagonal):
    return (diagonal + jnp.sum(weights, axis=0)) * values - jnp.sum(weights * values[neighbours], axis=0)


def remap_member(member, surface_out, send_blocks, entry_slot, entry_block, remap_tiles):
    partner = 1 - member
    source = surface_out[partner].reshape(NF, N_TILE, CDB, TILE_W).transpose(1, 2, 0, 3)
    source = jnp.concatenate([source, jnp.zeros((N_TILE, 1, NF, TILE_W), source.dtype)], axis=1)
    sender = send_blocks[partner]
    slot_offset = jnp.repeat(jnp.arange(5, dtype=jnp.int32), SLOT)
    slot_column = jnp.arange(5 * SLOT, dtype=jnp.int32)

    def one_tile(tile_number):
        source_tile = (tile_number + slot_offset - 2) % N_TILE
        chosen = sender[source_tile, slot_column]
        slot_data = source[source_tile, chosen]
        picked = slot_data[entry_slot[member, tile_number]].astype(jnp.float32)
        tiles_now = remap_tiles[member, tile_number].astype(jnp.float32)
        products = jnp.einsum("efs,eds->efd", picked, tiles_now)
        return jax.ops.segment_sum(products, entry_block[member, tile_number], num_segments=CDB)

    blocks = lax.map(one_tile, jnp.arange(N_TILE, dtype=jnp.int32))
    return blocks.transpose(2, 0, 1, 3).reshape(NF, CELLS)


def reference(fields, level_rate, edge_weight, fine_diagonal, fine_table, old_height, level_weight, flux_weight, fine_owner, coarse_table, coarse_edge, coarse_diagonal, coarse_owner, coarse_inverse, surface_out, send_blocks, entry_slot, entry_block, remap_tiles):
    new_list = []
    received_list = []
    height_list = []
    for member in range(2):
        fine_links = neighbour_index(fine_table[member], CD, HALO, CELLS)
        coarse_links = neighbour_index(coarse_table[member], C1, HALO1, L1CELLS)
        fine_owners = owner_index(fine_owner[member], CD, C1)
        coarse_owners = owner_index(coarse_owner[member], C1, C2)
        weights = edge_weight[member]
        weight_sum = jnp.sum(weights, axis=0)
        current = fields[member]
        beside_all = jnp.sum(weights[None] * current[:, fine_links], axis=1)
        advanced = current + level_rate[member][:, None] * (beside_all - weight_sum * current) / weight_sum
        received = remap_member(member, surface_out, send_blocks, entry_slot, entry_block, remap_tiles)
        forcing = jnp.sum(level_weight[member][:, None] * advanced, axis=0) + jnp.sum(flux_weight[member][:, None] * received, axis=0)
        fine_total = fine_diagonal[member] + weight_sum
        previous = old_height[member]
        smoothed = previous + RELAXATION * (forcing - apply_operator(previous, fine_links, weights, fine_diagonal[member])) / fine_total
        fine_residual = forcing - apply_operator(smoothed, fine_links, weights, fine_diagonal[member])
        coarse_source = jax.ops.segment_sum(fine_residual, fine_owners, num_segments=L1CELLS)
        coarse_weights = coarse_edge[member]
        coarse_total = coarse_diagonal[member] + jnp.sum(coarse_weights, axis=0)
        coarse_first = RELAXATION * coarse_source / coarse_total
        coarse_residual = coarse_source - apply_operator(coarse_first, coarse_links, coarse_weights, coarse_diagonal[member])
        bottom_source = jax.ops.segment_sum(coarse_residual, coarse_owners, num_segments=NC2)
        bottom_value = jnp.dot(coarse_inverse[member], bottom_source, precision=lax.Precision.HIGHEST)
        coarse_second = coarse_first + bottom_value[coarse_owners]
        coarse_third = coarse_second + RELAXATION * (coarse_source - apply_operator(coarse_second, coarse_links, coarse_weights, coarse_diagonal[member])) / coarse_total
        corrected = smoothed + coarse_third[fine_owners]
        height = corrected + RELAXATION * (forcing - apply_operator(corrected, fine_links, weights, fine_diagonal[member])) / fine_total
        new_list.append(advanced)
        received_list.append(received)
        height_list.append(height)
    return (jnp.stack(new_list), jnp.stack(received_list), jnp.stack(height_list))
```

```python
import functools

import jax
import jax.numpy as jnp
from jax import lax
from jax.experimental import pallas as pl
from jax.experimental.pallas import tpu as pltpu
from jax.sharding import PartitionSpec as P

MESH = pl.DeviceIdType.MESH
F32, BF16, I32 = jnp.float32, jnp.bfloat16, jnp.int32
RELAX = 0.8
NT = (((1,), (1,)), ((), ()))
NN = (((1,), (0,)), ((), ()))


def take(x, lane):
    return jnp.take_along_axis(x, lane, axis=1, mode="promise_in_bounds")


def pick(prev, cur, nxt, pos):
    lane = pos & 127
    return jnp.where(
        pos < 0, take(prev, lane), jnp.where(pos > 127, take(nxt, lane), take(cur, lane))
    )


def spread(row, count=8):
    return jnp.broadcast_to(row, (count, 128))


def iota(shape, dim):
    return lax.broadcasted_iota(I32, shape, dim)


def split(x):
    high = x.astype(BF16)
    return high, (x - high.astype(F32)).astype(BF16)


def dot(a, b, dims):
    return lax.dot_general(a, b, dims, preferred_element_type=F32)


def kernel(
    fields, rate_s, edge, fdiag, ftab, oldh, lw_s, fw_s, fown, ctab, cedge, cdiag, cown,
    cinv, surf, sendb, eslot, eblk, tiles,
    newf, recv, height,
    tl, outg, inc, hs, hr, invr, sm_l, sm_r, cs_l, cs_r, pay, cs_s, gb, member, picks, prod_h, prod_l,
    hot, lhs, oldp, smp, cop, base, pos, etab, eedge, e_d, e_o, key, cs, cf, cs2, t3, khot, klhs,
    invc,
    tile_sem, surf_ss, surf_rs, halo_ss, halo_rs, inv_ss, inv_rs, sm_ss, sm_rs, cs_ss, cs_rs,
    ag_ss, ag_rs,
):
    g = lax.axis_index("comp")
    t = lax.axis_index("tile")
    n = lax.axis_size("tile")
    left, right = lax.rem(t + n - 1, n), lax.rem(t + 1, n)
    bar = pltpu.get_barrier_semaphore()

    def greet(i, carry):
        pl.semaphore_signal(bar, inc=1, device_id=(g, lax.rem(t + i, n)), device_id_type=MESH)
        return carry

    def greet_other(i, carry):
        pl.semaphore_signal(
            bar, inc=1, device_id=(1 - g, lax.rem(t + i + n - 2, n)), device_id_type=MESH
        )
        return carry

    lax.fori_loop(0, 5, greet_other, 0)
    lax.fori_loop(1, n, greet, 0)

    chunks = 4
    per = 160 // chunks
    tile_copies = [
        pltpu.make_async_copy(
            tiles.at[pl.ds(c * per, per)], tl.at[pl.ds(c * per, per)], tile_sem.at[c]
        )
        for c in range(chunks)
    ]
    for c in tile_copies:
        c.start()

    def gather(i, carry):
        for a in range(8):
            s = i * 8 + a
            outg[s] = surf[jnp.minimum(sendb[0, s], 63)]
        return carry

    lax.fori_loop(0, 20, gather, 0)

    row8 = iota((8, 128), 0)
    cpos = [ctab[k] - 16 - 128 * row8 for k in range(3)]
    csum = cedge[0] + cedge[1] + cedge[2]
    c_d = cdiag[...] + csum
    for k in range(3):
        etab[k, 0:1, :] = jnp.zeros((1, 128), F32)
        etab[k, 1:9, :] = cpos[k].astype(F32)
        etab[k, 9:16, :] = jnp.zeros((7, 128), F32)
        eedge[k, 0:1, :] = jnp.zeros((1, 128), F32)
        eedge[k, 1:9, :] = cedge[k]
        eedge[k, 9:16, :] = jnp.zeros((7, 128), F32)
    e_d[...] = jnp.ones((24, 128), F32)
    e_d[2:10, :] = c_d
    e_o[...] = jnp.zeros((24, 128), F32)
    e_o[2:10, :] = cown[...].astype(F32)
    for side, block, low in ((0, 0, 0), (1, 63, 6)):
        hs[side, 0:8, :] = fields[block]
        hs[side, 8:9, :] = oldh[block : block + 1, :]
        hs[side, 9:10, :] = fown[block : block + 1, :].astype(F32)
        hs[side, 10:16, :] = jnp.zeros((6, 128), F32)
        for k in range(3):
            hs[side, 16 + 2 * k : 18 + 2 * k, :] = etab[k, 1 + low : 3 + low, :]
            hs[side, 22 + 2 * k : 24 + 2 * k, :] = cedge[k, low : low + 2, :]
        hs[side, 28:30, :] = e_d[2 + low : 4 + low, :]
        hs[side, 30:32, :] = e_o[2 + low : 4 + low, :]

    pl.semaphore_wait(bar, n + 4)

    surf_copies = [
        pltpu.make_async_remote_copy(
            src_ref=outg.at[pl.ds(32 * j, 32)],
            dst_ref=inc.at[pl.ds(32 * j, 32)],
            send_sem=surf_ss.at[j],
            recv_sem=surf_rs.at[j],
            device_id=(1 - g, lax.rem(t + n + 2 - j, n)),
            device_id_type=MESH,
        )
        for j in range(5)
    ]

    def pair(to_left, at_right, to_right, at_left, ss, rs):
        return [
            pltpu.make_async_remote_copy(
                src_ref=to_left, dst_ref=at_right, send_sem=ss.at[0], recv_sem=rs.at[0],
                device_id=(g, left), device_id_type=MESH,
            ),
            pltpu.make_async_remote_copy(
                src_ref=to_right, dst_ref=at_left, send_sem=ss.at[1], recv_sem=rs.at[1],
                device_id=(g, right), device_id_type=MESH,
            ),
        ]

    halo_copies = pair(hs.at[0], hr.at[1], hs.at[1], hr.at[0], halo_ss, halo_rs)
    inv_copies = pair(cinv, invr.at[1], cinv, invr.at[0], inv_ss, inv_rs)
    for c in halo_copies + surf_copies + inv_copies:
        c.start()

    def positions(i, carry):
        at = pl.ds(pl.multiple_of(i * 8, 8), 8)
        for k in range(3):
            pos[k, at, :] = ftab[k, at, :] - 128 - 128 * (i * 8 + row8)
        return carry

    lax.fori_loop(0, 8, positions, 0)

    def column(ref, count):
        out = jnp.zeros((8, 128), F32)
        for level in range(count):
            out = jnp.where(row8 == level, ref[0, level], out)
        return out

    rates, weights = column(rate_s, 8), column(lw_s, 8)

    def advance(j, prev, cur, nxt):
        beside = total = None
        for k in range(3):
            p = spread(pos[k, pl.ds(j, 1), :])
            w = spread(edge[k, pl.ds(j, 1), :])
            term = w * pick(prev, cur, nxt, p)
            beside = term if beside is None else beside + term
            total = w if total is None else total + w
        new = cur + rates * (beside - total * cur) / total
        newf[j] = new
        base[pl.ds(j, 1), :] = jnp.sum(weights * new, axis=0, keepdims=True)

    def advance8(i, carry):
        for a in range(8):
            j = i * 8 + a
            advance(j, fields[j - 1], fields[j], fields[j + 1])
        return carry

    lax.fori_loop(1, 7, advance8, 0)
    for j in (*range(1, 8), *range(56, 63)):
        advance(j, fields[j - 1], fields[j], fields[j + 1])

    down = iota((128, 128), 0)

    def one_hot(i, carry):
        for a in range(4):
            r = i * 4 + a
            row = fown[pl.ds(r, 1), :] & 127
            at = pl.ds(pl.multiple_of(r * 128, 128), 128)
            hot[:, at] = jnp.where(down == spread(row, 128), 1.0, 0.0).astype(BF16)
        return carry

    lax.fori_loop(0, 16, one_hot, 0)

    lane8 = iota((8, 128), 1)
    e_first = spread(eblk[0:1, 0:128])
    e_last = spread(
        jnp.concatenate([eblk[0:1, 128:160], jnp.zeros((1, 96), I32)], axis=1)
    )
    for c in range(5):
        source = e_first if c < 4 else e_last
        four = take(source, (c % 4) * 32 + lane8 // 4) * 4 + lane8 % 4
        for part in range(2):
            rows = iota((128, 128), 0) + 128 * part
            member[128 * part : 128 * part + 128, 128 * c : 128 * c + 128] = jnp.where(
                rows == spread(four[0:1], 128), 1.0, 0.0
            ).astype(BF16)

    for c in halo_copies:
        c.wait_recv()
    advance(0, hr[0, 0:8, :], fields[0], fields[1])
    advance(63, fields[62], fields[63], hr[1, 0:8, :])
    oldp[7:8, :] = hr[0, 8:9, :]
    oldp[8:72, :] = oldh[...]
    oldp[72:73, :] = hr[1, 8:9, :]
    for k in range(3):
        etab[k, 0:1, :] = hr[0, 17 + 2 * k : 18 + 2 * k, :]
        etab[k, 9:10, :] = hr[1, 16 + 2 * k : 17 + 2 * k, :]
        eedge[k, 0:1, :] = hr[0, 23 + 2 * k : 24 + 2 * k, :]
        eedge[k, 9:10, :] = hr[1, 22 + 2 * k : 23 + 2 * k, :]
    e_d[0:2, :] = hr[0, 28:30, :]
    e_d[10:12, :] = hr[1, 28:30, :]
    e_o[0:2, :] = hr[0, 30:32, :]
    e_o[10:12, :] = hr[1, 30:32, :]

    row16 = iota((16, 128), 0)
    side = jnp.where(row16 == 0, 7, jnp.where(row16 == 9, 1, 0))
    key[...] = ((t + side) & 7) * 16 + e_o[1:17, :].astype(I32)
    for r in range(10):
        khot[:, 128 * r : 128 * r + 128] = jnp.where(
            down == spread(key[r : r + 1, :], 128), 1.0, 0.0
        ).astype(BF16)

    def neighbours(ref, r, at_ref_row):
        out = None
        prev = ref[at_ref_row - 1 : at_ref_row + 7, :]
        cur = ref[at_ref_row : at_ref_row + 8, :]
        nxt = ref[at_ref_row + 1 : at_ref_row + 9, :]
        for k in range(3):
            at = slice(8 * r, 8 * r + 8)
            term = edge[k, at, :] * pick(prev, cur, nxt, pos[k, at, :])
            out = term if out is None else out + term
        return out

    def totals(r):
        at = slice(8 * r, 8 * r + 8)
        return fdiag[at, :] + (edge[0, at, :] + edge[1, at, :] + edge[2, at, :])

    for r in range(8):
        at = slice(8 * r, 8 * r + 8)
        smp[8 + 8 * r : 16 + 8 * r, :] = neighbours(oldp, r, 8 + 8 * r)

    for c in surf_copies:
        c.wait_recv()
    for c in tile_copies:
        c.wait()

    def products(i, carry):
        for a in range(2):
            e0 = i * 8 + a * 4
            for b in range(4):
                picks[pl.ds(pl.multiple_of(e0 * 4 + 4 * b, 4), 4), :] = inc[
                    eslot[0, e0 + b]
                ].astype(F32)
            at = pl.ds(pl.multiple_of(e0 * 4, 16), 16)
            out = dot(
                picks[at, :].astype(BF16), tl[pl.ds(e0, 4)].reshape(512, 128), NT
            )
            part = row16 // 4
            four = jnp.where(
                part == 0,
                out[:, 0:128],
                jnp.where(
                    part == 1,
                    out[:, 128:256],
                    jnp.where(part == 2, out[:, 256:384], out[:, 384:512]),
                ),
            )
            high, low = split(four)
            prod_h[at, :] = high
            prod_l[at, :] = low
        return carry

    lax.fori_loop(0, 20, products, 0)
    recv[...] = dot(member[...], prod_h[...], NN) + dot(member[...], prod_l[...], NN)

    forcing = []
    for r in range(8):
        at = slice(8 * r, 8 * r + 8)
        out = base[at, :]
        for f in range(4):
            out = out + fw_s[0, f] * recv[pl.ds(32 * r + f, 8, stride=4), :]
        base[at, :] = out
        prev = oldh[at, :]
        whole = totals(r)
        smp[8 + 8 * r : 16 + 8 * r, :] = (
            prev + RELAX * (out - (whole * prev - smp[8 + 8 * r : 16 + 8 * r, :])) / whole
        )

    sm_copies = pair(smp.at[pl.ds(8, 8)], sm_r, smp.at[pl.ds(64, 8)], sm_l, sm_ss, sm_rs)
    for c in sm_copies:
        c.start()
    for c in sm_copies:
        c.wait_send()
        c.wait_recv()
    smp[7:8, :] = sm_l[7:8, :]
    smp[72:73, :] = sm_r[0:1, :]
    for r in range(8):
        at = slice(8 * r, 8 * r + 8)
        cur = smp[8 + 8 * r : 16 + 8 * r, :]
        res = base[at, :] - (totals(r) * cur - neighbours(smp, r, 8 + 8 * r))
        high = fown[at, :] >> 7
        for a in range(8):
            mine = jnp.where(spread(high[a : a + 1]) == row8, spread(res[a : a + 1]), 0.0)
            where = slice(128 * (8 * r + a), 128 * (8 * r + a) + 128)
            lhs[:, where] = jnp.concatenate(list(split_f32(mine)), axis=0).astype(BF16)
    sums = dot(lhs[...], hot[...], NT)
    source = sums[0:8] + sums[8:16]
    cs[...] = jnp.zeros((24, 128), F32)
    cs[2:10, :] = source
    cf[...] = jnp.zeros((24, 128), F32)
    cs2[...] = jnp.zeros((24, 128), F32)
    cs_s[...] = source
    cs_copies = pair(cs_s, cs_r, cs_s, cs_l, cs_ss, cs_rs)
    for c in cs_copies:
        c.start()
    cf[2:10, :] = RELAX * source / c_d

    def coarse_neighbours(ref):
        out = None
        for k in range(3):
            term = eedge[k] * pick(
                ref[0:16, :], ref[1:17, :], ref[2:18, :], etab[k].astype(I32)
            )
            out = term if out is None else out + term
        return out

    left_over = cs[1:17, :] - e_d[1:17, :] * cf[1:17, :] + coarse_neighbours(cf)
    klhs[...] = jnp.zeros((8, 1280), F32)
    for r in range(10):
        klhs[0:1, 128 * r : 128 * r + 128] = left_over[r : r + 1]
    packed = jnp.concatenate(list(split_f32(klhs[...])), axis=0).astype(BF16)
    bottoms = dot(packed, khot[...], NT)
    pay[0] = bottoms[0:1] + bottoms[8:9]
    gb[t] = pay[0]

    def ag_copy(i):
        return pltpu.make_async_remote_copy(
            src_ref=pay,
            dst_ref=gb.at[pl.ds(t, 1)],
            send_sem=ag_ss,
            recv_sem=ag_rs,
            device_id=(g, lax.rem(t + i, n)),
            device_id_type=MESH,
        )

    def ag_start(i, carry):
        ag_copy(i).start()
        return carry

    lax.fori_loop(1, n, ag_start, 0)

    for c in inv_copies:
        c.wait_recv()
    for at, block in ((0, cinv[...]), (16, invr[0]), (32, invr[1])):
        high, low = split(block)
        invc[at : at + 16, :] = high
        invc[48 + at : 64 + at, :] = low
    invc[96:128, :] = jnp.zeros((32, 1024), BF16)
    for c in cs_copies:
        c.wait_recv()
    cs[0:2, :] = cs_l[6:8, :]
    cs[10:12, :] = cs_r[0:2, :]
    for at in (0, 8):
        cf[at : at + 8, :] = RELAX * cs[at : at + 8, :] / e_d[at : at + 8, :]

    everyone = pltpu.make_async_remote_copy(
        src_ref=gb.at[pl.ds(0, n - 1)],
        dst_ref=gb.at[pl.ds(0, n - 1)],
        send_sem=ag_ss,
        recv_sem=ag_rs,
        device_id=(g, right),
        device_id_type=MESH,
    )
    everyone.wait_recv()
    from_right = (row8 == 0) & (lane8 >= 112)
    from_left = (row8 == 7) & (lane8 < 16)
    groups = [gb[8 * j : 8 * j + 8, 0, :] for j in range(8)]
    flat = []
    for j in range(8):
        mix = jnp.where(
            from_right, groups[(j + 1) % 8], jnp.where(from_left, groups[(j - 1) % 8], groups[j])
        )
        flat.append(jnp.sum(mix, axis=0, keepdims=True))
    flat = spread_all(jnp.concatenate(flat, axis=1))
    packed = jnp.concatenate(list(split_f32(flat)), axis=0).astype(BF16)
    found = dot(packed, invc[...], NT)
    value = found[0:1] + found[8:9]
    value = value + pltpu.roll(spread(value), 128 - 48, 1)[0:1]
    value = spread(value, 16)
    shift = jnp.where(row16 < 2, 16, jnp.where(row16 < 10, 0, 32))
    cs2[0:16, :] = cf[0:16, :] + take(value, jnp.minimum(e_o[0:16, :].astype(I32), 15) + shift)
    cur = cs2[1:17, :]
    whole = e_d[1:17, :]
    t3[...] = cur + RELAX * (cs[1:17, :] - (whole * cur - coarse_neighbours(cs2))) / whole

    for r in range(8):
        at = slice(8 * r, 8 * r + 8)
        owner = fown[at, :]
        high, lane = owner >> 7, owner & 127
        out = smp[8 + 8 * r : 16 + 8 * r, :]
        for h in range(8):
            out = out + jnp.where(high == h, take(spread(t3[1 + h : 2 + h, :]), lane), 0.0)
        cop[8 + 8 * r : 16 + 8 * r, :] = out
    own_l = spread(hr[0, 9:10, :]).astype(I32) & 127
    own_r = spread(hr[1, 9:10, :]).astype(I32) & 127
    cop[7:8, :] = smp[7:8, :] + take(spread(t3[0:1, :]), own_l)[0:1]
    cop[72:73, :] = smp[72:73, :] + take(spread(t3[9:10, :]), own_r)[0:1]
    for r in range(8):
        at = slice(8 * r, 8 * r + 8)
        cur = cop[8 + 8 * r : 16 + 8 * r, :]
        whole = totals(r)
        beside = neighbours(cop, r, 8 + 8 * r)
        height[at, :] = cur + RELAX * (base[at, :] - (whole * cur - beside)) / whole

    for c in halo_copies + surf_copies + inv_copies + cs_copies:
        c.wait_send()
    everyone.wait_send()


def split_f32(x):
    high = x.astype(BF16).astype(F32)
    return high, x - high


def spread_all(row):
    return jnp.broadcast_to(row, (8, row.shape[1]))


def per_device(
    fields, level_rate, edge_weight, fine_diagonal, fine_table, old_height, level_weight,
    flux_weight, fine_owner, coarse_table, coarse_edge, coarse_diagonal, coarse_owner,
    coarse_inverse, surface_out, send_blocks, entry_slot, entry_block, remap_tiles,
):
    operands = (
        fields.reshape(8, 64, 128).transpose(1, 0, 2),
        level_rate,
        edge_weight.reshape(3, 64, 128),
        fine_diagonal.reshape(64, 128),
        fine_table.reshape(3, 64, 128),
        old_height.reshape(64, 128),
        level_weight,
        flux_weight,
        fine_owner.reshape(64, 128),
        coarse_table.reshape(3, 8, 128),
        coarse_edge.reshape(3, 8, 128),
        coarse_diagonal.reshape(8, 128),
        coarse_owner.reshape(8, 128),
        coarse_inverse.reshape(16, 1024),
        surface_out.reshape(4, 64, 128).transpose(1, 0, 2),
        send_blocks.reshape(1, 160),
        entry_slot.reshape(1, 160),
        entry_block.reshape(1, 160),
        remap_tiles.reshape(160, 128, 128),
    )
    vmem = pl.BlockSpec(memory_space=pltpu.VMEM)
    smem = pl.BlockSpec(memory_space=pltpu.SMEM)
    specs = [vmem] * 19
    for i in (1, 6, 7, 15, 16):
        specs[i] = smem
    specs[18] = pl.BlockSpec(memory_space=pl.ANY)
    V = pltpu.VMEM
    D = pltpu.SemaphoreType.DMA
    new, got, high = pl.pallas_call(
        kernel,
        out_shape=(
            jax.ShapeDtypeStruct((64, 8, 128), F32),
            jax.ShapeDtypeStruct((256, 128), F32),
            jax.ShapeDtypeStruct((64, 128), F32),
        ),
        in_specs=specs,
        out_specs=(vmem, vmem, vmem),
        scratch_shapes=[
            V((160, 128, 128), BF16),
            V((160, 4, 128), BF16),
            V((160, 4, 128), BF16),
            V((2, 32, 128), F32),
            V((2, 32, 128), F32),
            V((2, 16, 1024), F32),
            V((8, 128), F32),
            V((8, 128), F32),
            V((8, 128), F32),
            V((8, 128), F32),
            V((1, 1, 128), F32),
            V((8, 128), F32),
            V((64, 1, 128), F32),
            V((256, 640), BF16),
            V((640, 128), F32),
            V((640, 128), BF16),
            V((640, 128), BF16),
            V((128, 8192), BF16),
            V((16, 8192), BF16),
            V((80, 128), F32),
            V((80, 128), F32),
            V((80, 128), F32),
            V((64, 128), F32),
            V((3, 64, 128), I32),
            V((3, 16, 128), F32),
            V((3, 16, 128), F32),
            V((24, 128), F32),
            V((24, 128), F32),
            V((16, 128), I32),
            V((24, 128), F32),
            V((24, 128), F32),
            V((24, 128), F32),
            V((16, 128), F32),
            V((128, 1280), BF16),
            V((8, 1280), F32),
            V((128, 1024), BF16),
            D((4,)),
            D((5,)), D((5,)),
            D((2,)), D((2,)),
            D((2,)), D((2,)),
            D((2,)), D((2,)),
            D((2,)), D((2,)),
            D, D,
        ],
        compiler_params=pltpu.CompilerParams(
            collective_id=0, has_side_effects=True, vmem_limit_bytes=48 << 20
        ),
        name="step",
    )(*operands)
    return (
        new.transpose(1, 0, 2).reshape(1, 8, 8192),
        got.reshape(64, 4, 128).transpose(1, 0, 2).reshape(1, 4, 8192),
        high.reshape(1, 8192),
    )


def solution(mesh):
    in_specs = (
        P("comp", None, "tile"),
        P("comp", None),
        P("comp", None, "tile"),
        P("comp", "tile"),
        P("comp", None, "tile"),
        P("comp", "tile"),
        P("comp", None),
        P("comp", None),
        P("comp", "tile"),
        P("comp", None, "tile"),
        P("comp", None, "tile"),
        P("comp", "tile"),
        P("comp", "tile"),
        P("comp", "tile", None),
        P("comp", None, "tile"),
        P("comp", "tile", None),
        P("comp", "tile", None),
        P("comp", "tile", None),
        P("comp", "tile", None, None, None),
    )
    out_specs = (P("comp", None, "tile"), P("comp", None, "tile"), P("comp", "tile"))
    return jax.shard_map(
        per_device, mesh=mesh, in_specs=in_specs, out_specs=out_specs, check_vma=False
    )
```

```python
import functools

import jax
import jax.numpy as jnp
from jax import lax
from jax.experimental import pallas as pl
from jax.experimental.pallas import tpu as pltpu
from jax.sharding import PartitionSpec as P

MESH = pl.DeviceIdType.MESH
F32, BF16, I32 = jnp.float32, jnp.bfloat16, jnp.int32
RELAX = 0.8
NT = (((1,), (1,)), ((), ()))
NN = (((1,), (0,)), ((), ()))


def take(x, lane):
    return jnp.take_along_axis(x, lane, axis=1, mode="promise_in_bounds")


def pick(prev, cur, nxt, pos):
    lane = pos & 127
    return jnp.where(
        pos < 0, take(prev, lane), jnp.where(pos > 127, take(nxt, lane), take(cur, lane))
    )


def spread(row, count=8):
    return jnp.broadcast_to(row, (count, 128))


def iota(shape, dim):
    return lax.broadcasted_iota(I32, shape, dim)


def split(x):
    high = x.astype(BF16)
    return high, (x - high.astype(F32)).astype(BF16)


def dot(a, b, dims):
    return lax.dot_general(a, b, dims, preferred_element_type=F32)


def kernel(
    *refs,
):
    inputs, outputs, scratch = refs[:19], refs[19:22], refs[22:]
    local, scratch = scratch[:19], scratch[19:]
    step(*local, *outputs, inputs, local, *scratch)


def step(
    fields, rate_s, edge, fdiag, ftab, oldh, lw_s, fw_s, fown, ctab, cedge, cdiag, cown,
    cinv, surf, sendb, eslot, eblk, tl,
    newf, recv, height, inputs, local,
    outg, inc, hs, hr, invr, sm_l, sm_r, cs_l, cs_r, pay, cs_s, gb, member, picks, prod_h, prod_l,
    hot, lhs, oldp, smp, cop, base, pos, etab, eedge, e_d, e_o, key, cs, cf, cs2, t3, khot, klhs, shares,
    invc,
    in_sem, tile_sem, surf_ss, surf_rs, halo_ss, halo_rs, inv_ss, inv_rs, sm_ss, sm_rs, cs_ss, cs_rs,
    ag_ss, ag_rs, plane_sem, space_sem,
):
    g = lax.axis_index("comp")
    t = lax.axis_index("tile")
    n = lax.axis_size("tile")
    left, right = lax.rem(t + n - 1, n), lax.rem(t + 1, n)
    y, z, x = lax.rem(t, 4), lax.rem(lax.div(t, 4), 4), lax.div(t, 16)
    ys = [lax.rem(y + d, 4) for d in range(4)]
    zs = [4 * lax.rem(z + d, 4) for d in range(4)]
    xs = [16 * lax.rem(x + d, 4) for d in range(4)]
    ring_y = [xs[0] + zs[0] + ys[d] for d in (1, 2, 3)]
    ring_z = [xs[0] + zs[d] + ys[0] for d in (1, 2, 3)]
    ring_x = [xs[d] + zs[0] + ys[0] for d in (1, 2, 3)]
    bar = pltpu.get_barrier_semaphore()

    def signal(sem, group, tile):
        pl.semaphore_signal(sem, inc=1, device_id=(group, tile), device_id_type=MESH)

    loads = [
        pltpu.make_async_copy(inputs[i], local[i], in_sem.at[i]) for i in range(18)
    ]
    for i in (15, 14, 0, 5, 8, 9, 10, 11, 12, 4, 2, 1, 6, 7, 17, 3, 16, 13):
        loads[i].start()
    for d in (2, -2, 1, -1, 0):
        signal(bar, 1 - g, lax.rem(t + n + d, n))
    for tile in (left, right, *ring_y, *ring_z, *ring_x):
        signal(bar, g, tile)

    tiles = inputs[18]
    chunks = 4
    per = 160 // chunks
    tile_copies = [
        pltpu.make_async_copy(
            tiles.at[pl.ds(c * per, per)], tl.at[pl.ds(c * per, per)], tile_sem.at[c]
        )
        for c in range(chunks)
    ]
    for c in tile_copies:
        c.start()

    def ready(*which):
        for i in which:
            loads[i].wait()

    ready(15, 14)

    def gather(i, carry):
        for a in range(8):
            s = i * 8 + a
            outg[s] = surf[jnp.minimum(sendb[0, s], 63)]
        return carry

    lax.fori_loop(0, 20, gather, 0)

    ready(0, 5, 8, 9, 10, 11, 12)
    row8 = iota((8, 128), 0)
    cpos = [ctab[k] - 16 - 128 * row8 for k in range(3)]
    csum = cedge[0] + cedge[1] + cedge[2]
    c_d = cdiag[...] + csum
    for k in range(3):
        etab[k, 0:1, :] = jnp.zeros((1, 128), F32)
        etab[k, 1:9, :] = cpos[k].astype(F32)
        etab[k, 9:16, :] = jnp.zeros((7, 128), F32)
        eedge[k, 0:1, :] = jnp.zeros((1, 128), F32)
        eedge[k, 1:9, :] = cedge[k]
        eedge[k, 9:16, :] = jnp.zeros((7, 128), F32)
    e_d[...] = jnp.ones((24, 128), F32)
    e_d[2:10, :] = c_d
    e_o[...] = jnp.zeros((24, 128), F32)
    e_o[2:10, :] = cown[...].astype(F32)
    for side, block, low in ((0, 0, 0), (1, 63, 6)):
        hs[side, 0:8, :] = fields[block]
        hs[side, 8:9, :] = oldh[block : block + 1, :]
        hs[side, 9:10, :] = fown[block : block + 1, :].astype(F32)
        hs[side, 10:16, :] = jnp.zeros((6, 128), F32)
        for k in range(3):
            hs[side, 16 + 2 * k : 18 + 2 * k, :] = etab[k, 1 + low : 3 + low, :]
            hs[side, 22 + 2 * k : 24 + 2 * k, :] = cedge[k, low : low + 2, :]
        hs[side, 28:30, :] = e_d[2 + low : 4 + low, :]
        hs[side, 30:32, :] = e_o[2 + low : 4 + low, :]

    pl.semaphore_wait(bar, 16)

    surf_copies = [
        pltpu.make_async_remote_copy(
            src_ref=outg.at[pl.ds(32 * j, 32)],
            dst_ref=inc.at[pl.ds(32 * j, 32)],
            send_sem=surf_ss.at[j],
            recv_sem=surf_rs.at[j],
            device_id=(1 - g, lax.rem(t + n + 2 - j, n)),
            device_id_type=MESH,
        )
        for j in range(5)
    ]

    def pair(to_left, at_right, to_right, at_left, ss, rs):
        return [
            pltpu.make_async_remote_copy(
                src_ref=to_left, dst_ref=at_right, send_sem=ss.at[0], recv_sem=rs.at[0],
                device_id=(g, left), device_id_type=MESH,
            ),
            pltpu.make_async_remote_copy(
                src_ref=to_right, dst_ref=at_left, send_sem=ss.at[1], recv_sem=rs.at[1],
                device_id=(g, right), device_id_type=MESH,
            ),
        ]

    halo_copies = pair(hs.at[0], hr.at[1], hs.at[1], hr.at[0], halo_ss, halo_rs)
    inv_copies = pair(inputs[13], invr.at[1], inputs[13], invr.at[0], inv_ss, inv_rs)
    for c in halo_copies + surf_copies:
        c.start()
    for tile in ring_z:
        signal(plane_sem, g, tile)
    for c in inv_copies:
        c.start()

    ready(4, 2, 1, 6, 7, 17, 3, 16, 13)
    def positions(i, carry):
        at = pl.ds(pl.multiple_of(i * 8, 8), 8)
        total = edge[0, at, :] + edge[1, at, :] + edge[2, at, :]
        share = 1.0 / total
        for k in range(3):
            pos[k, at, :] = ftab[k, at, :] - 128 - 128 * (i * 8 + row8)
            shares[k, at, :] = edge[k, at, :] * share
        return carry

    lax.fori_loop(0, 8, positions, 0)

    def column(ref, count):
        out = jnp.zeros((8, 128), F32)
        for level in range(count):
            out = jnp.where(row8 == level, ref[0, level], out)
        return out

    rates, weights = column(rate_s, 8), column(lw_s, 8)

    def advance(j, prev, cur, nxt):
        beside = None
        for k in range(3):
            p = spread(pos[k, pl.ds(j, 1), :])
            w = spread(shares[k, pl.ds(j, 1), :])
            term = w * pick(prev, cur, nxt, p)
            beside = term if beside is None else beside + term
        new = cur + rates * (beside - cur)
        newf[j] = new
        base[pl.ds(j, 1), :] = jnp.sum(weights * new, axis=0, keepdims=True)

    def advance8(i, carry):
        for a in range(8):
            j = i * 8 + a
            advance(j, fields[j - 1], fields[j], fields[j + 1])
        return carry

    lax.fori_loop(1, 7, advance8, 0)
    for j in (*range(1, 8), *range(56, 63)):
        advance(j, fields[j - 1], fields[j], fields[j + 1])

    lane8 = iota((8, 128), 1)
    e_first = spread(eblk[0:1, 0:128])
    e_last = spread(
        jnp.concatenate([eblk[0:1, 128:160], jnp.zeros((1, 96), I32)], axis=1)
    )
    for c in range(5):
        source = e_first if c < 4 else e_last
        four = take(source, (c % 4) * 32 + lane8 // 4) * 4 + lane8 % 4
        for part in range(2):
            rows = iota((128, 128), 0) + 128 * part
            member[128 * part : 128 * part + 128, 128 * c : 128 * c + 128] = jnp.where(
                rows == spread(four[0:1], 128), 1.0, 0.0
            ).astype(BF16)

    for c in halo_copies:
        c.wait_recv()
    advance(0, hr[0, 0:8, :], fields[0], fields[1])
    advance(63, fields[62], fields[63], hr[1, 0:8, :])
    oldp[7:8, :] = hr[0, 8:9, :]
    oldp[8:72, :] = oldh[...]
    oldp[72:73, :] = hr[1, 8:9, :]
    def neighbours(ref, r, at_ref_row):
        out = None
        prev = ref[at_ref_row - 1 : at_ref_row + 7, :]
        cur = ref[at_ref_row : at_ref_row + 8, :]
        nxt = ref[at_ref_row + 1 : at_ref_row + 9, :]
        for k in range(3):
            at = slice(8 * r, 8 * r + 8)
            term = edge[k, at, :] * pick(prev, cur, nxt, pos[k, at, :])
            out = term if out is None else out + term
        return out

    def totals(r):
        at = slice(8 * r, 8 * r + 8)
        return fdiag[at, :] + (edge[0, at, :] + edge[1, at, :] + edge[2, at, :])

    for r in range(8):
        at = slice(8 * r, 8 * r + 8)
        smp[8 + 8 * r : 16 + 8 * r, :] = neighbours(oldp, r, 8 + 8 * r)

    row16 = iota((16, 128), 0)
    for c in surf_copies:
        c.wait_recv()
    for c in tile_copies:
        c.wait()

    def choose(i, carry):
        for b in range(16):
            e = i * 16 + b
            picks[pl.ds(pl.multiple_of(e * 4, 4), 4), :] = inc[eslot[0, e]].astype(F32)
        return carry

    lax.fori_loop(0, 10, choose, 0)
    quarter = row16 // 4
    for i in range(40):
        at = slice(16 * i, 16 * i + 16)
        out = dot(picks[at, :].astype(BF16), tl[4 * i : 4 * i + 4].reshape(512, 128), NT)
        four = jnp.where(
            quarter == 0,
            out[:, 0:128],
            jnp.where(
                quarter == 1,
                out[:, 128:256],
                jnp.where(quarter == 2, out[:, 256:384], out[:, 384:512]),
            ),
        )
        prod_h[at, :], prod_l[at, :] = split(four)

    recv[...] = dot(member[...], prod_h[...], NN) + dot(member[...], prod_l[...], NN)

    forcing = []
    for r in range(8):
        at = slice(8 * r, 8 * r + 8)
        out = base[at, :]
        for f in range(4):
            out = out + fw_s[0, f] * recv[pl.ds(32 * r + f, 8, stride=4), :]
        base[at, :] = out
        prev = oldh[at, :]
        whole = totals(r)
        smp[8 + 8 * r : 16 + 8 * r, :] = (
            prev + RELAX * (out - (whole * prev - smp[8 + 8 * r : 16 + 8 * r, :])) / whole
        )

    sm_copies = pair(smp.at[pl.ds(8, 8)], sm_r, smp.at[pl.ds(64, 8)], sm_l, sm_ss, sm_rs)
    for c in sm_copies:
        c.start()
    pl.semaphore_wait(plane_sem, 3)
    for tile in ring_x:
        signal(space_sem, g, tile)
    down = iota((128, 128), 0)

    def one_hot(i, carry):
        for a in range(4):
            r = i * 4 + a
            row = fown[pl.ds(r, 1), :] & 127
            at = pl.ds(pl.multiple_of(r * 128, 128), 128)
            hot[:, at] = jnp.where(down == spread(row, 128), 1.0, 0.0).astype(BF16)
        return carry

    lax.fori_loop(0, 16, one_hot, 0)
    for k in range(3):
        etab[k, 0:1, :] = hr[0, 17 + 2 * k : 18 + 2 * k, :]
        etab[k, 9:10, :] = hr[1, 16 + 2 * k : 17 + 2 * k, :]
        eedge[k, 0:1, :] = hr[0, 23 + 2 * k : 24 + 2 * k, :]
        eedge[k, 9:10, :] = hr[1, 22 + 2 * k : 23 + 2 * k, :]
    e_d[0:2, :] = hr[0, 28:30, :]
    e_d[10:12, :] = hr[1, 28:30, :]
    e_o[0:2, :] = hr[0, 30:32, :]
    e_o[10:12, :] = hr[1, 30:32, :]

    side = jnp.where(row16 == 0, 7, jnp.where(row16 == 9, 1, 0))
    key[...] = ((t + side) & 7) * 16 + e_o[1:17, :].astype(I32)
    for r in range(10):
        khot[:, 128 * r : 128 * r + 128] = jnp.where(
            down == spread(key[r : r + 1, :], 128), 1.0, 0.0
        ).astype(BF16)

    smp[7:8, :] = jnp.zeros((1, 128), F32)
    smp[72:73, :] = jnp.zeros((1, 128), F32)

    def spot(row, owner):
        mine = jnp.where(spread(owner >> 7) == row8, spread(row), 0.0)
        return jnp.concatenate(list(split_f32(mine)), axis=0).astype(BF16)

    sums = None
    for r in range(8):
        at = slice(8 * r, 8 * r + 8)
        cur = smp[8 + 8 * r : 16 + 8 * r, :]
        res = base[at, :] - (totals(r) * cur - neighbours(smp, r, 8 + 8 * r))
        for a in range(8):
            where = slice(128 * (8 * r + a), 128 * (8 * r + a) + 128)
            lhs[:, where] = spot(res[a : a + 1], fown[8 * r + a : 8 * r + a + 1, :])
    for r in range(4):
        where = slice(2048 * r, 2048 * r + 2048)
        part_sum = dot(lhs[:, where], hot[:, where], NT)
        sums = part_sum if sums is None else sums + part_sum
    for c in sm_copies:
        c.wait_send()
        c.wait_recv()
    smp[7:8, :] = sm_l[7:8, :]
    smp[72:73, :] = sm_r[0:1, :]
    far_l, far_r = spread(sm_l[7:8, :]), spread(sm_r[0:1, :])
    more_l = more_r = jnp.zeros((8, 128), F32)
    for k in range(3):
        p = pos[k, 0:8, :]
        more_l = more_l + jnp.where(p < 0, edge[k, 0:8, :] * take(far_l, p & 127), 0.0)
        p = pos[k, 56:64, :]
        more_r = more_r + jnp.where(p > 127, edge[k, 56:64, :] * take(far_r, p & 127), 0.0)
    sums = sums + dot(spot(more_l[0:1], fown[0:1, :]), hot[:, 0:128], NT)
    sums = sums + dot(spot(more_r[7:8], fown[63:64, :]), hot[:, 8064:8192], NT)
    source = sums[0:8] + sums[8:16]
    cs[...] = jnp.zeros((24, 128), F32)
    cs[2:10, :] = source
    cf[...] = jnp.zeros((24, 128), F32)
    cs2[...] = jnp.zeros((24, 128), F32)
    cs_s[...] = source
    cs_copies = pair(cs_s, cs_r, cs_s, cs_l, cs_ss, cs_rs)
    for c in cs_copies:
        c.start()
    cf[2:10, :] = RELAX * source / c_d

    def coarse_neighbours(ref):
        out = None
        for k in range(3):
            term = eedge[k] * pick(
                ref[0:16, :], ref[1:17, :], ref[2:18, :], etab[k].astype(I32)
            )
            out = term if out is None else out + term
        return out

    left_over = cs[1:17, :] - e_d[1:17, :] * cf[1:17, :] + coarse_neighbours(cf)
    klhs[...] = jnp.zeros((8, 1280), F32)
    for r in range(10):
        klhs[0:1, 128 * r : 128 * r + 128] = left_over[r : r + 1]
    packed = jnp.concatenate(list(split_f32(klhs[...])), axis=0).astype(BF16)
    bottoms = dot(packed, khot[...], NT)
    pay[0] = bottoms[0:1] + bottoms[8:9]
    gb[t] = pay[0]

    pl.semaphore_wait(space_sem, 3)
    hops = (0, 1, 2, 1)
    others = sorted(
        ((a, b, c) for a in range(4) for b in range(4) for c in range(4)),
        key=lambda d: -(hops[d[0]] + hops[d[1]] + hops[d[2]]),
    )[:-1]
    for a, b, c in others:
        pltpu.make_async_remote_copy(
            src_ref=pay,
            dst_ref=gb.at[pl.ds(t, 1)],
            send_sem=ag_ss,
            recv_sem=ag_rs,
            device_id=(g, xs[a] + zs[b] + ys[c]),
            device_id_type=MESH,
        ).start()

    for c in inv_copies:
        c.wait_recv()
    for at, block in ((0, cinv[...]), (16, invr[0]), (32, invr[1])):
        high, low = split(block)
        invc[at : at + 16, :] = high
        invc[48 + at : 64 + at, :] = low
    invc[96:128, :] = jnp.zeros((32, 1024), BF16)
    for c in cs_copies:
        c.wait_recv()
    cs[0:2, :] = cs_l[6:8, :]
    cs[10:12, :] = cs_r[0:2, :]
    for at in (0, 8):
        cf[at : at + 8, :] = RELAX * cs[at : at + 8, :] / e_d[at : at + 8, :]

    everyone = pltpu.make_async_remote_copy(
        src_ref=gb.at[pl.ds(0, n - 1)],
        dst_ref=gb.at[pl.ds(0, n - 1)],
        send_sem=ag_ss,
        recv_sem=ag_rs,
        device_id=(g, right),
        device_id_type=MESH,
    )
    everyone.wait_recv()
    from_right = (row8 == 0) & (lane8 >= 112)
    from_left = (row8 == 7) & (lane8 < 16)
    groups = [gb[8 * j : 8 * j + 8, 0, :] for j in range(8)]
    flat = []
    for j in range(8):
        mix = jnp.where(
            from_right, groups[(j + 1) % 8], jnp.where(from_left, groups[(j - 1) % 8], groups[j])
        )
        flat.append(jnp.sum(mix, axis=0, keepdims=True))
    flat = spread_all(jnp.concatenate(flat, axis=1))
    packed = jnp.concatenate(list(split_f32(flat)), axis=0).astype(BF16)
    found = dot(packed, invc[...], NT)
    value = found[0:1] + found[8:9]
    value = value + pltpu.roll(spread(value), 128 - 48, 1)[0:1]
    value = spread(value, 16)
    shift = jnp.where(row16 < 2, 16, jnp.where(row16 < 10, 0, 32))
    cs2[0:16, :] = cf[0:16, :] + take(value, jnp.minimum(e_o[0:16, :].astype(I32), 15) + shift)
    cur = cs2[1:17, :]
    whole = e_d[1:17, :]
    t3[...] = cur + RELAX * (cs[1:17, :] - (whole * cur - coarse_neighbours(cs2))) / whole

    for r in range(8):
        at = slice(8 * r, 8 * r + 8)
        owner = fown[at, :]
        high, lane = owner >> 7, owner & 127
        out = smp[8 + 8 * r : 16 + 8 * r, :]
        for h in range(8):
            out = out + jnp.where(high == h, take(spread(t3[1 + h : 2 + h, :]), lane), 0.0)
        cop[8 + 8 * r : 16 + 8 * r, :] = out
    own_l = spread(hr[0, 9:10, :]).astype(I32) & 127
    own_r = spread(hr[1, 9:10, :]).astype(I32) & 127
    cop[7:8, :] = smp[7:8, :] + take(spread(t3[0:1, :]), own_l)[0:1]
    cop[72:73, :] = smp[72:73, :] + take(spread(t3[9:10, :]), own_r)[0:1]
    for r in range(8):
        at = slice(8 * r, 8 * r + 8)
        cur = cop[8 + 8 * r : 16 + 8 * r, :]
        whole = totals(r)
        beside = neighbours(cop, r, 8 + 8 * r)
        height[at, :] = cur + RELAX * (base[at, :] - (whole * cur - beside)) / whole

    for c in halo_copies + surf_copies + inv_copies + cs_copies:
        c.wait_send()
    everyone.wait_send()


def write_out(a, b, c, a_out, b_out, c_out, sems):
    copies = [
        pltpu.make_async_copy(source, target, sems.at[i])
        for i, (source, target) in enumerate(((a, a_out), (b, b_out), (c, c_out)))
    ]
    for copy in copies:
        copy.start()
    for copy in copies:
        copy.wait()


def split_f32(x):
    high = x.astype(BF16).astype(F32)
    return high, x - high


def spread_all(row):
    return jnp.broadcast_to(row, (8, row.shape[1]))


def per_device(
    fields, level_rate, edge_weight, fine_diagonal, fine_table, old_height, level_weight,
    flux_weight, fine_owner, coarse_table, coarse_edge, coarse_diagonal, coarse_owner,
    coarse_inverse, surface_out, send_blocks, entry_slot, entry_block, remap_tiles,
):
    operands = (
        fields.reshape(8, 64, 128).transpose(1, 0, 2),
        level_rate,
        edge_weight.reshape(3, 64, 128),
        fine_diagonal.reshape(64, 128),
        fine_table.reshape(3, 64, 128),
        old_height.reshape(64, 128),
        level_weight,
        flux_weight,
        fine_owner.reshape(64, 128),
        coarse_table.reshape(3, 8, 128),
        coarse_edge.reshape(3, 8, 128),
        coarse_diagonal.reshape(8, 128),
        coarse_owner.reshape(8, 128),
        coarse_inverse.reshape(16, 1024),
        surface_out.reshape(4, 64, 128).transpose(1, 0, 2),
        send_blocks.reshape(1, 160),
        entry_slot.reshape(1, 160),
        entry_block.reshape(1, 160),
        remap_tiles.reshape(160, 128, 128),
    )
    vmem = pl.BlockSpec(memory_space=pltpu.VMEM)
    specs = [pl.BlockSpec(memory_space=pltpu.HBM)] * 19
    V = pltpu.VMEM
    local = [
        (pltpu.SMEM if i in (1, 6, 7, 15, 16) else V)(x.shape, x.dtype)
        for i, x in enumerate(operands)
    ]
    D = pltpu.SemaphoreType.DMA
    new, got, high = pl.pallas_call(
        kernel,
        out_shape=(
            jax.ShapeDtypeStruct((64, 8, 128), F32),
            jax.ShapeDtypeStruct((256, 128), F32),
            jax.ShapeDtypeStruct((64, 128), F32),
        ),
        in_specs=specs,
        out_specs=(vmem, vmem, vmem),
        scratch_shapes=[
            *local,
            V((160, 4, 128), BF16),
            V((160, 4, 128), BF16),
            V((2, 32, 128), F32),
            V((2, 32, 128), F32),
            V((2, 16, 1024), F32),
            V((8, 128), F32),
            V((8, 128), F32),
            V((8, 128), F32),
            V((8, 128), F32),
            V((1, 1, 128), F32),
            V((8, 128), F32),
            V((64, 1, 128), F32),
            V((256, 640), BF16),
            V((640, 128), F32),
            V((640, 128), BF16),
            V((640, 128), BF16),
            V((128, 8192), BF16),
            V((16, 8192), BF16),
            V((80, 128), F32),
            V((80, 128), F32),
            V((80, 128), F32),
            V((64, 128), F32),
            V((3, 64, 128), I32),
            V((3, 16, 128), F32),
            V((3, 16, 128), F32),
            V((24, 128), F32),
            V((24, 128), F32),
            V((16, 128), I32),
            V((24, 128), F32),
            V((24, 128), F32),
            V((24, 128), F32),
            V((16, 128), F32),
            V((128, 1280), BF16),
            V((8, 1280), F32),
            V((3, 64, 128), F32),
            V((128, 1024), BF16),
            D((18,)),
            D((4,)),
            D((5,)), D((5,)),
            D((2,)), D((2,)),
            D((2,)), D((2,)),
            D((2,)), D((2,)),
            D((2,)), D((2,)),
            D, D,
            pltpu.SemaphoreType.REGULAR, pltpu.SemaphoreType.REGULAR,
        ],
        compiler_params=pltpu.CompilerParams(
            collective_id=0, has_side_effects=True, vmem_limit_bytes=48 << 20
        ),
        name="step",
    )(*[pltpu.with_memory_space_constraint(x, pltpu.HBM) for x in operands])
    new, got, high = pl.pallas_call(
        write_out,
        out_shape=tuple(jax.ShapeDtypeStruct(v.shape, v.dtype) for v in (new, got, high)),
        in_specs=[vmem] * 3,
        out_specs=[pl.BlockSpec(memory_space=pltpu.HBM)] * 3,
        scratch_shapes=[D((3,))],
        compiler_params=pltpu.CompilerParams(vmem_limit_bytes=1 << 20),
        name="write_out",
    )(new, got, high)
    return (
        new.transpose(1, 0, 2).reshape(1, 8, 8192),
        got.reshape(64, 4, 128).transpose(1, 0, 2).reshape(1, 4, 8192),
        high.reshape(1, 8192),
    )


def solution(mesh):
    in_specs = (
        P("comp", None, "tile"),
        P("comp", None),
        P("comp", None, "tile"),
        P("comp", "tile"),
        P("comp", None, "tile"),
        P("comp", "tile"),
        P("comp", None),
        P("comp", None),
        P("comp", "tile"),
        P("comp", None, "tile"),
        P("comp", None, "tile"),
        P("comp", "tile"),
        P("comp", "tile"),
        P("comp", "tile", None),
        P("comp", None, "tile"),
        P("comp", "tile", None),
        P("comp", "tile", None),
        P("comp", "tile", None),
        P("comp", "tile", None, None, None),
    )
    out_specs = (P("comp", None, "tile"), P("comp", None, "tile"), P("comp", "tile"))
    return jax.shard_map(
        per_device, mesh=mesh, in_specs=in_specs, out_specs=out_specs, check_vma=False
    )
```

```python
import functools

import jax
import jax.numpy as jnp
from jax import lax
from jax.experimental import pallas as pl
from jax.experimental.pallas import tpu as pltpu
from jax.sharding import PartitionSpec as P

MESH = pl.DeviceIdType.MESH
F32, BF16, I32 = jnp.float32, jnp.bfloat16, jnp.int32
RELAX = 0.8
NT = (((1,), (1,)), ((), ()))
NN = (((1,), (0,)), ((), ()))


def take(x, lane):
    return jnp.take_along_axis(x, lane, axis=1, mode="promise_in_bounds")


def pick(prev, cur, nxt, pos):
    lane = pos & 127
    return jnp.where(
        pos < 0, take(prev, lane), jnp.where(pos > 127, take(nxt, lane), take(cur, lane))
    )


def spread(row, count=8):
    return jnp.broadcast_to(row, (count, 128))


def iota(shape, dim):
    return lax.broadcasted_iota(I32, shape, dim)


def split(x):
    high = x.astype(BF16)
    return high, (x - high.astype(F32)).astype(BF16)


def dot(a, b, dims):
    return lax.dot_general(a, b, dims, preferred_element_type=F32)


def kernel(
    *refs,
):
    inputs, outputs, scratch = refs[:19], refs[19:22], refs[22:]
    local, scratch = scratch[:19], scratch[19:]
    step(*local, *outputs, inputs, local, *scratch)


def step(
    fields, rate_s, edge, fdiag, ftab, oldh, lw_s, fw_s, fown, ctab, cedge, cdiag, cown,
    cinv, surf, sendb, eslot, eblk, tl,
    newf, recv, height, inputs, local,
    outg, inc, hs, hr, invr, sm_l, sm_r, cs_l, cs_r, pay, cs_s, gb, member, picks, prod_h, prod_l,
    hot, lhs, oldp, smp, cop, base, pos, etab, eedge, e_d, e_o, key, cs, cf, cs2, t3, khot, klhs, hot_n, shares,
    invc,
    in_sem, tile_sem, surf_ss, surf_rs, halo_ss, halo_rs, inv_ss, inv_rs, sm_ss, sm_rs, cs_ss, cs_rs,
    ag_ss, ag_rs, plane_sem, space_sem,
):
    g = lax.axis_index("comp")
    t = lax.axis_index("tile")
    n = lax.axis_size("tile")
    left, right = lax.rem(t + n - 1, n), lax.rem(t + 1, n)
    y, z, x = lax.rem(t, 4), lax.rem(lax.div(t, 4), 4), lax.div(t, 16)
    ys = [lax.rem(y + d, 4) for d in range(4)]
    zs = [4 * lax.rem(z + d, 4) for d in range(4)]
    xs = [16 * lax.rem(x + d, 4) for d in range(4)]
    ring_y = [xs[0] + zs[0] + ys[d] for d in (1, 2, 3)]
    ring_z = [xs[0] + zs[d] + ys[0] for d in (1, 2, 3)]
    ring_x = [xs[d] + zs[0] + ys[0] for d in (1, 2, 3)]
    bar = pltpu.get_barrier_semaphore()

    def signal(sem, group, tile):
        pl.semaphore_signal(sem, inc=1, device_id=(group, tile), device_id_type=MESH)

    loads = [
        pltpu.make_async_copy(inputs[i], local[i], in_sem.at[i]) for i in range(18)
    ]
    for i in (15, 14, 0, 5, 8, 9, 10, 11, 12, 4, 2, 1, 6, 7, 17, 3, 16, 13):
        loads[i].start()
    for d in (2, -2, 1, -1, 0):
        signal(bar, 1 - g, lax.rem(t + n + d, n))
    for tile in (left, right, *ring_y, *ring_z, *ring_x):
        signal(bar, g, tile)

    tiles = inputs[18]
    chunks = 4
    per = 160 // chunks
    tile_copies = [
        pltpu.make_async_copy(
            tiles.at[pl.ds(c * per, per)], tl.at[pl.ds(c * per, per)], tile_sem.at[c]
        )
        for c in range(chunks)
    ]
    for c in tile_copies:
        c.start()

    def ready(*which):
        for i in which:
            loads[i].wait()

    ready(15, 14)

    def gather(i, carry):
        for a in range(8):
            s = i * 8 + a
            outg[s] = surf[jnp.minimum(sendb[0, s], 63)]
        return carry

    lax.fori_loop(0, 20, gather, 0)

    ready(0, 5, 8, 9, 10, 11, 12, 4, 2)
    row8 = iota((8, 128), 0)
    cpos = [ctab[k] - 16 - 128 * row8 for k in range(3)]
    csum = cedge[0] + cedge[1] + cedge[2]
    c_d = cdiag[...] + csum
    for k in range(3):
        etab[k, 2:10, :] = cpos[k].astype(F32)
        etab[k, 12:16, :] = jnp.zeros((4, 128), F32)
        eedge[k, 2:10, :] = cedge[k]
        eedge[k, 12:16, :] = jnp.zeros((4, 128), F32)
    e_d[...] = jnp.ones((24, 128), F32)
    e_d[3:11, :] = c_d
    e_o[...] = jnp.zeros((24, 128), F32)
    e_o[3:11, :] = cown[...].astype(F32)
    for side, block, low in ((0, 0, 0), (1, 63, 6)):
        hs[side, 0:8, :] = fields[block]
        hs[side, 8:9, :] = oldh[block : block + 1, :]
        hs[side, 9:10, :] = fown[block : block + 1, :].astype(F32)
        for k in range(3):
            here = ftab[k, block : block + 1, :] - (128 + 128 * block)
            hs[side, 10 + k : 11 + k, :] = here.astype(F32)
            hs[side, 13 + k : 14 + k, :] = edge[k, block : block + 1, :]
        for k in range(3):
            hs[side, 16 + 2 * k : 18 + 2 * k, :] = etab[k, 2 + low : 4 + low, :]
            hs[side, 22 + 2 * k : 24 + 2 * k, :] = cedge[k, low : low + 2, :]
        hs[side, 28:30, :] = e_d[3 + low : 5 + low, :]
        hs[side, 30:32, :] = e_o[3 + low : 5 + low, :]

    pl.semaphore_wait(bar, 16)

    surf_copies = [
        pltpu.make_async_remote_copy(
            src_ref=outg.at[pl.ds(32 * j, 32)],
            dst_ref=inc.at[pl.ds(32 * j, 32)],
            send_sem=surf_ss.at[j],
            recv_sem=surf_rs.at[j],
            device_id=(1 - g, lax.rem(t + n + 2 - j, n)),
            device_id_type=MESH,
        )
        for j in range(5)
    ]

    def pair(to_left, at_right, to_right, at_left, ss, rs):
        return [
            pltpu.make_async_remote_copy(
                src_ref=to_left, dst_ref=at_right, send_sem=ss.at[0], recv_sem=rs.at[0],
                device_id=(g, left), device_id_type=MESH,
            ),
            pltpu.make_async_remote_copy(
                src_ref=to_right, dst_ref=at_left, send_sem=ss.at[1], recv_sem=rs.at[1],
                device_id=(g, right), device_id_type=MESH,
            ),
        ]

    halo_copies = pair(hs.at[0], hr.at[1], hs.at[1], hr.at[0], halo_ss, halo_rs)
    inv_copies = pair(inputs[13], invr.at[1], inputs[13], invr.at[0], inv_ss, inv_rs)
    for c in halo_copies + surf_copies:
        c.start()
    for tile in ring_z:
        signal(plane_sem, g, tile)

    ready(1, 6, 7, 17, 3, 16, 13)
    def positions(i, carry):
        at = pl.ds(pl.multiple_of(i * 8, 8), 8)
        total = edge[0, at, :] + edge[1, at, :] + edge[2, at, :]
        share = 1.0 / total
        for k in range(3):
            pos[k, at, :] = ftab[k, at, :] - 128 - 128 * (i * 8 + row8)
            shares[k, at, :] = edge[k, at, :] * share
        return carry

    lax.fori_loop(0, 8, positions, 0)

    def column(ref, count):
        out = jnp.zeros((8, 128), F32)
        for level in range(count):
            out = jnp.where(row8 == level, ref[0, level], out)
        return out

    rates, weights = column(rate_s, 8), column(lw_s, 8)

    def advance(j, prev, cur, nxt):
        beside = None
        for k in range(3):
            p = spread(pos[k, pl.ds(j, 1), :])
            w = spread(shares[k, pl.ds(j, 1), :])
            term = w * pick(prev, cur, nxt, p)
            beside = term if beside is None else beside + term
        new = cur + rates * (beside - cur)
        newf[j] = new
        base[pl.ds(j, 1), :] = jnp.sum(weights * new, axis=0, keepdims=True)

    def advance8(i, carry):
        for a in range(8):
            j = i * 8 + a
            advance(j, fields[j - 1], fields[j], fields[j + 1])
        return carry

    lax.fori_loop(1, 7, advance8, 0)
    for j in (*range(1, 8), *range(56, 63)):
        advance(j, fields[j - 1], fields[j], fields[j + 1])

    lane8 = iota((8, 128), 1)
    e_first = spread(eblk[0:1, 0:128])
    e_last = spread(
        jnp.concatenate([eblk[0:1, 128:160], jnp.zeros((1, 96), I32)], axis=1)
    )
    for c in range(5):
        source = e_first if c < 4 else e_last
        four = take(source, (c % 4) * 32 + lane8 // 4) * 4 + lane8 % 4
        for part in range(2):
            rows = iota((128, 128), 0) + 128 * part
            member[128 * part : 128 * part + 128, 128 * c : 128 * c + 128] = jnp.where(
                rows == spread(four[0:1], 128), 1.0, 0.0
            ).astype(BF16)

    down = iota((128, 128), 0)

    def one_hot(i, carry):
        for a in range(4):
            r = i * 4 + a
            row = fown[pl.ds(r, 1), :] & 127
            at = pl.ds(pl.multiple_of(r * 128, 128), 128)
            hot[:, at] = jnp.where(down == spread(row, 128), 1.0, 0.0).astype(BF16)
        return carry

    lax.fori_loop(0, 16, one_hot, 0)
    for c in halo_copies:
        c.wait_recv()
    advance(0, hr[0, 0:8, :], fields[0], fields[1])
    advance(63, fields[62], fields[63], hr[1, 0:8, :])
    oldp[7:8, :] = hr[0, 8:9, :]
    oldp[8:72, :] = oldh[...]
    oldp[72:73, :] = hr[1, 8:9, :]
    def neighbours(ref, r, at_ref_row):
        out = None
        prev = ref[at_ref_row - 1 : at_ref_row + 7, :]
        cur = ref[at_ref_row : at_ref_row + 8, :]
        nxt = ref[at_ref_row + 1 : at_ref_row + 9, :]
        for k in range(3):
            at = slice(8 * r, 8 * r + 8)
            term = edge[k, at, :] * pick(prev, cur, nxt, pos[k, at, :])
            out = term if out is None else out + term
        return out

    def totals(r):
        at = slice(8 * r, 8 * r + 8)
        return fdiag[at, :] + (edge[0, at, :] + edge[1, at, :] + edge[2, at, :])

    for r in range(8):
        at = slice(8 * r, 8 * r + 8)
        smp[8 + 8 * r : 16 + 8 * r, :] = neighbours(oldp, r, 8 + 8 * r)

    row16 = iota((16, 128), 0)
    for k in range(3):
        etab[k, 0:2, :] = hr[0, 16 + 2 * k : 18 + 2 * k, :]
        etab[k, 10:12, :] = hr[1, 16 + 2 * k : 18 + 2 * k, :]
        eedge[k, 0:2, :] = hr[0, 22 + 2 * k : 24 + 2 * k, :]
        eedge[k, 10:12, :] = hr[1, 22 + 2 * k : 24 + 2 * k, :]
    e_d[1:3, :] = hr[0, 28:30, :]
    e_d[11:13, :] = hr[1, 28:30, :]
    e_o[1:3, :] = hr[0, 30:32, :]
    e_o[11:13, :] = hr[1, 30:32, :]
    side = jnp.where(row16 < 2, 7, jnp.where(row16 >= 10, 1, 0))
    key[...] = ((t + side) & 7) * 16 + e_o[1:17, :].astype(I32)
    for r in range(12):
        khot[:, 128 * r : 128 * r + 128] = jnp.where(
            down == spread(key[r : r + 1, :], 128), 1.0, 0.0
        ).astype(BF16)
    for i in range(2):
        owner = spread(hr[i, 9:10, :], 128).astype(I32) & 127
        hot_n[i] = jnp.where(down == owner, 1.0, 0.0).astype(BF16)
    for c in surf_copies:
        c.wait_recv()
    for c in tile_copies:
        c.wait()

    for c in inv_copies:
        c.start()
    pl.semaphore_wait(plane_sem, 3)
    for tile in ring_x:
        signal(space_sem, g, tile)
    def choose(i, carry):
        for b in range(16):
            e = i * 16 + b
            picks[pl.ds(pl.multiple_of(e * 4, 4), 4), :] = inc[eslot[0, e]].astype(F32)
        return carry

    lax.fori_loop(0, 10, choose, 0)
    quarter = row16 // 4
    for i in range(40):
        at = slice(16 * i, 16 * i + 16)
        out = dot(picks[at, :].astype(BF16), tl[4 * i : 4 * i + 4].reshape(512, 128), NT)
        four = jnp.where(
            quarter == 0,
            out[:, 0:128],
            jnp.where(
                quarter == 1,
                out[:, 128:256],
                jnp.where(quarter == 2, out[:, 256:384], out[:, 384:512]),
            ),
        )
        prod_h[at, :], prod_l[at, :] = split(four)

    recv[...] = dot(member[...], prod_h[...], NN) + dot(member[...], prod_l[...], NN)

    forcing = []
    for r in range(8):
        at = slice(8 * r, 8 * r + 8)
        out = base[at, :]
        for f in range(4):
            out = out + fw_s[0, f] * recv[pl.ds(32 * r + f, 8, stride=4), :]
        base[at, :] = out
        prev = oldh[at, :]
        whole = totals(r)
        smp[8 + 8 * r : 16 + 8 * r, :] = (
            prev + RELAX * (out - (whole * prev - smp[8 + 8 * r : 16 + 8 * r, :])) / whole
        )

    sm_copies = pair(smp.at[pl.ds(8, 8)], sm_r, smp.at[pl.ds(64, 8)], sm_l, sm_ss, sm_rs)
    for c in sm_copies:
        c.start()
    smp[7:8, :] = jnp.zeros((1, 128), F32)
    smp[72:73, :] = jnp.zeros((1, 128), F32)

    def spot(row, owner):
        mine = jnp.where(spread(owner >> 7) == row8, spread(row), 0.0)
        return jnp.concatenate(list(split_f32(mine)), axis=0).astype(BF16)

    sums = None
    for r in range(8):
        at = slice(8 * r, 8 * r + 8)
        cur = smp[8 + 8 * r : 16 + 8 * r, :]
        res = base[at, :] - (totals(r) * cur - neighbours(smp, r, 8 + 8 * r))
        for a in range(8):
            where = slice(128 * (8 * r + a), 128 * (8 * r + a) + 128)
            lhs[:, where] = spot(res[a : a + 1], fown[8 * r + a : 8 * r + a + 1, :])
    for r in range(4):
        where = slice(2048 * r, 2048 * r + 2048)
        part_sum = dot(lhs[:, where], hot[:, where], NT)
        sums = part_sum if sums is None else sums + part_sum
    source = sums[0:8] + sums[8:16]
    cs_s[...] = source
    cs_copies = pair(cs_s, cs_r, cs_s, cs_l, cs_ss, cs_rs)
    for c in cs_copies:
        c.start()

    def from_here(i, row, towards):
        row = spread(row)
        out = jnp.zeros((8, 128), F32)
        for k in range(3):
            p = spread(hr[i, 10 + k : 11 + k, :]).astype(I32)
            term = spread(hr[i, 13 + k : 14 + k, :]) * take(row, p & 127)
            out = out + jnp.where(towards(p), term, 0.0)
        both = dot(jnp.concatenate(list(split_f32(out)), axis=0).astype(BF16), hot_n[i], NT)
        return both[0:1] + both[8:9]

    extra_l = from_here(0, smp[8:9, :], lambda p: p > 127)
    extra_r = from_here(1, smp[71:72, :], lambda p: p < 0)
    cs[...] = jnp.zeros((24, 128), F32)
    cs[2:3, :] = extra_l
    cs[3:11, :] = source
    cs[11:12, :] = extra_r
    cf[...] = jnp.zeros((24, 128), F32)
    cs2[...] = jnp.zeros((24, 128), F32)
    cf[0:16, :] = RELAX * cs[0:16, :] / e_d[0:16, :]

    def coarse_neighbours(ref):
        out = None
        for k in range(3):
            term = eedge[k] * pick(
                ref[0:16, :], ref[1:17, :], ref[2:18, :], etab[k].astype(I32)
            )
            out = term if out is None else out + term
        return out

    left_over = cs[1:17, :] - e_d[1:17, :] * cf[1:17, :] + coarse_neighbours(cf)
    klhs[...] = jnp.zeros((8, 1536), F32)
    for r in range(12):
        klhs[0:1, 128 * r : 128 * r + 128] = left_over[r : r + 1]
    packed = jnp.concatenate(list(split_f32(klhs[...])), axis=0).astype(BF16)
    bottoms = dot(packed, khot[...], NT)
    pay[0] = bottoms[0:1] + bottoms[8:9]
    gb[t] = pay[0]

    pl.semaphore_wait(space_sem, 3)
    hops = (0, 1, 2, 1)
    others = sorted(
        ((a, b, c) for a in range(4) for b in range(4) for c in range(4)),
        key=lambda d: -(hops[d[0]] + hops[d[1]] + hops[d[2]]),
    )[:-1]
    for a, b, c in others:
        pltpu.make_async_remote_copy(
            src_ref=pay,
            dst_ref=gb.at[pl.ds(t, 1)],
            send_sem=ag_ss,
            recv_sem=ag_rs,
            device_id=(g, xs[a] + zs[b] + ys[c]),
            device_id_type=MESH,
        ).start()

    for c in inv_copies:
        c.wait_recv()
    for at, block in ((0, cinv[...]), (16, invr[0]), (32, invr[1])):
        high, low = split(block)
        invc[at : at + 16, :] = high
        invc[48 + at : 64 + at, :] = low
    invc[96:128, :] = jnp.zeros((32, 1024), BF16)
    for c in sm_copies:
        c.wait_send()
        c.wait_recv()
    smp[7:8, :] = sm_l[7:8, :]
    smp[72:73, :] = sm_r[0:1, :]
    far_l, far_r = spread(sm_l[7:8, :]), spread(sm_r[0:1, :])
    more_l = more_r = jnp.zeros((8, 128), F32)
    for k in range(3):
        p = pos[k, 0:8, :]
        more_l = more_l + jnp.where(p < 0, edge[k, 0:8, :] * take(far_l, p & 127), 0.0)
        p = pos[k, 56:64, :]
        more_r = more_r + jnp.where(p > 127, edge[k, 56:64, :] * take(far_r, p & 127), 0.0)
    sums = dot(spot(more_l[0:1], fown[0:1, :]), hot[:, 0:128], NT)
    sums = sums + dot(spot(more_r[7:8], fown[63:64, :]), hot[:, 8064:8192], NT)
    more = sums[0:8] + sums[8:16]
    for c in cs_copies:
        c.wait_recv()
    cs[1:3, :] = cs_l[6:8, :] + cs[1:3, :]
    cs[3:11, :] = cs[3:11, :] + more
    cs[11:13, :] = cs_r[0:2, :] + cs[11:13, :]
    cf[0:16, :] = RELAX * cs[0:16, :] / e_d[0:16, :]

    everyone = pltpu.make_async_remote_copy(
        src_ref=gb.at[pl.ds(0, n - 1)],
        dst_ref=gb.at[pl.ds(0, n - 1)],
        send_sem=ag_ss,
        recv_sem=ag_rs,
        device_id=(g, right),
        device_id_type=MESH,
    )
    everyone.wait_recv()
    from_right = (row8 == 0) & (lane8 >= 112)
    from_left = (row8 == 7) & (lane8 < 16)
    groups = [gb[8 * j : 8 * j + 8, 0, :] for j in range(8)]
    flat = []
    for j in range(8):
        mix = jnp.where(
            from_right, groups[(j + 1) % 8], jnp.where(from_left, groups[(j - 1) % 8], groups[j])
        )
        flat.append(jnp.sum(mix, axis=0, keepdims=True))
    flat = spread_all(jnp.concatenate(flat, axis=1))
    packed = jnp.concatenate(list(split_f32(flat)), axis=0).astype(BF16)
    found = dot(packed, invc[...], NT)
    value = found[0:1] + found[8:9]
    value = value + pltpu.roll(spread(value), 128 - 48, 1)[0:1]
    value = spread(value, 16)
    shift = jnp.where(row16 < 3, 16, jnp.where(row16 < 11, 0, 32))
    cs2[0:16, :] = cf[0:16, :] + take(value, jnp.minimum(e_o[0:16, :].astype(I32), 15) + shift)
    cur = cs2[1:17, :]
    whole = e_d[1:17, :]
    t3[...] = cur + RELAX * (cs[1:17, :] - (whole * cur - coarse_neighbours(cs2))) / whole

    for r in range(8):
        at = slice(8 * r, 8 * r + 8)
        owner = fown[at, :]
        high, lane = owner >> 7, owner & 127
        out = smp[8 + 8 * r : 16 + 8 * r, :]
        for h in range(8):
            out = out + jnp.where(high == h, take(spread(t3[2 + h : 3 + h, :]), lane), 0.0)
        cop[8 + 8 * r : 16 + 8 * r, :] = out
    own_l = spread(hr[0, 9:10, :]).astype(I32) & 127
    own_r = spread(hr[1, 9:10, :]).astype(I32) & 127
    cop[7:8, :] = smp[7:8, :] + take(spread(t3[1:2, :]), own_l)[0:1]
    cop[72:73, :] = smp[72:73, :] + take(spread(t3[10:11, :]), own_r)[0:1]
    for r in range(8):
        at = slice(8 * r, 8 * r + 8)
        cur = cop[8 + 8 * r : 16 + 8 * r, :]
        whole = totals(r)
        beside = neighbours(cop, r, 8 + 8 * r)
        height[at, :] = cur + RELAX * (base[at, :] - (whole * cur - beside)) / whole

    for c in halo_copies + surf_copies + inv_copies + cs_copies:
        c.wait_send()
    everyone.wait_send()


def write_out(a, b, c, a_out, b_out, c_out, sems):
    copies = [
        pltpu.make_async_copy(source, target, sems.at[i])
        for i, (source, target) in enumerate(((a, a_out), (b, b_out), (c, c_out)))
    ]
    for copy in copies:
        copy.start()
    for copy in copies:
        copy.wait()


def split_f32(x):
    high = x.astype(BF16).astype(F32)
    return high, x - high


def spread_all(row):
    return jnp.broadcast_to(row, (8, row.shape[1]))


def per_device(
    fields, level_rate, edge_weight, fine_diagonal, fine_table, old_height, level_weight,
    flux_weight, fine_owner, coarse_table, coarse_edge, coarse_diagonal, coarse_owner,
    coarse_inverse, surface_out, send_blocks, entry_slot, entry_block, remap_tiles,
):
    operands = (
        fields.reshape(8, 64, 128).transpose(1, 0, 2),
        level_rate,
        edge_weight.reshape(3, 64, 128),
        fine_diagonal.reshape(64, 128),
        fine_table.reshape(3, 64, 128),
        old_height.reshape(64, 128),
        level_weight,
        flux_weight,
        fine_owner.reshape(64, 128),
        coarse_table.reshape(3, 8, 128),
        coarse_edge.reshape(3, 8, 128),
        coarse_diagonal.reshape(8, 128),
        coarse_owner.reshape(8, 128),
        coarse_inverse.reshape(16, 1024),
        surface_out.reshape(4, 64, 128).transpose(1, 0, 2),
        send_blocks.reshape(1, 160),
        entry_slot.reshape(1, 160),
        entry_block.reshape(1, 160),
        remap_tiles.reshape(160, 128, 128),
    )
    vmem = pl.BlockSpec(memory_space=pltpu.VMEM)
    specs = [pl.BlockSpec(memory_space=pltpu.HBM)] * 19
    V = pltpu.VMEM
    local = [
        (pltpu.SMEM if i in (1, 6, 7, 15, 16) else V)(x.shape, x.dtype)
        for i, x in enumerate(operands)
    ]
    D = pltpu.SemaphoreType.DMA
    new, got, high = pl.pallas_call(
        kernel,
        out_shape=(
            jax.ShapeDtypeStruct((64, 8, 128), F32),
            jax.ShapeDtypeStruct((256, 128), F32),
            jax.ShapeDtypeStruct((64, 128), F32),
        ),
        in_specs=specs,
        out_specs=(vmem, vmem, vmem),
        scratch_shapes=[
            *local,
            V((160, 4, 128), BF16),
            V((160, 4, 128), BF16),
            V((2, 32, 128), F32),
            V((2, 32, 128), F32),
            V((2, 16, 1024), F32),
            V((8, 128), F32),
            V((8, 128), F32),
            V((8, 128), F32),
            V((8, 128), F32),
            V((1, 1, 128), F32),
            V((8, 128), F32),
            V((64, 1, 128), F32),
            V((256, 640), BF16),
            V((640, 128), F32),
            V((640, 128), BF16),
            V((640, 128), BF16),
            V((128, 8192), BF16),
            V((16, 8192), BF16),
            V((80, 128), F32),
            V((80, 128), F32),
            V((80, 128), F32),
            V((64, 128), F32),
            V((3, 64, 128), I32),
            V((3, 16, 128), F32),
            V((3, 16, 128), F32),
            V((24, 128), F32),
            V((24, 128), F32),
            V((16, 128), I32),
            V((24, 128), F32),
            V((24, 128), F32),
            V((24, 128), F32),
            V((16, 128), F32),
            V((128, 1536), BF16),
            V((8, 1536), F32),
            V((2, 128, 128), BF16),
            V((3, 64, 128), F32),
            V((128, 1024), BF16),
            D((18,)),
            D((4,)),
            D((5,)), D((5,)),
            D((2,)), D((2,)),
            D((2,)), D((2,)),
            D((2,)), D((2,)),
            D((2,)), D((2,)),
            D, D,
            pltpu.SemaphoreType.REGULAR, pltpu.SemaphoreType.REGULAR,
        ],
        compiler_params=pltpu.CompilerParams(
            collective_id=0, has_side_effects=True, vmem_limit_bytes=48 << 20
        ),
        name="step",
    )(*[pltpu.with_memory_space_constraint(x, pltpu.HBM) for x in operands])
    new, got, high = pl.pallas_call(
        write_out,
        out_shape=tuple(jax.ShapeDtypeStruct(v.shape, v.dtype) for v in (new, got, high)),
        in_specs=[vmem] * 3,
        out_specs=[pl.BlockSpec(memory_space=pltpu.HBM)] * 3,
        scratch_shapes=[D((3,))],
        compiler_params=pltpu.CompilerParams(vmem_limit_bytes=1 << 20),
        name="write_out",
    )(new, got, high)
    return (
        new.transpose(1, 0, 2).reshape(1, 8, 8192),
        got.reshape(64, 4, 128).transpose(1, 0, 2).reshape(1, 4, 8192),
        high.reshape(1, 8192),
    )


def solution(mesh):
    in_specs = (
        P("comp", None, "tile"),
        P("comp", None),
        P("comp", None, "tile"),
        P("comp", "tile"),
        P("comp", None, "tile"),
        P("comp", "tile"),
        P("comp", None),
        P("comp", None),
        P("comp", "tile"),
        P("comp", None, "tile"),
        P("comp", None, "tile"),
        P("comp", "tile"),
        P("comp", "tile"),
        P("comp", "tile", None),
        P("comp", None, "tile"),
        P("comp", "tile", None),
        P("comp", "tile", None),
        P("comp", "tile", None),
        P("comp", "tile", None, None, None),
    )
    out_specs = (P("comp", None, "tile"), P("comp", None, "tile"), P("comp", "tile"))
    return jax.shard_map(
        per_device, mesh=mesh, in_specs=in_specs, out_specs=out_specs, check_vma=False
    )
```

```python
import functools

import jax
import jax.numpy as jnp
from jax import lax
from jax.experimental import pallas as pl
from jax.experimental.pallas import tpu as pltpu
from jax.sharding import PartitionSpec as P

MESH = pl.DeviceIdType.MESH
F32, BF16, I32 = jnp.float32, jnp.bfloat16, jnp.int32
RELAX = 0.8
NT = (((1,), (1,)), ((), ()))
NN = (((1,), (0,)), ((), ()))


def take(x, lane):
    return jnp.take_along_axis(x, lane, axis=1, mode="promise_in_bounds")


def pick(prev, cur, nxt, pos):
    lane = pos & 127
    return jnp.where(
        pos < 0, take(prev, lane), jnp.where(pos > 127, take(nxt, lane), take(cur, lane))
    )


def spread(row, count=8):
    return jnp.broadcast_to(row, (count, 128))


def iota(shape, dim):
    return lax.broadcasted_iota(I32, shape, dim)


def split(x):
    high = x.astype(BF16)
    return high, (x - high.astype(F32)).astype(BF16)


def dot(a, b, dims):
    return lax.dot_general(a, b, dims, preferred_element_type=F32)


def kernel(
    *refs,
):
    inputs, outputs, scratch = refs[:19], refs[19:22], refs[22:]
    local, scratch = scratch[:19], scratch[19:]
    step(*local, *outputs, inputs, local, *scratch)


def step(
    fields, rate_s, edge, fdiag, ftab, oldh, lw_s, fw_s, fown, ctab, cedge, cdiag, cown,
    cinv, surf, sendb, eslot, eblk, tl,
    newf, recv, height, inputs, local,
    outg, inc, hs, hr, invr, sm_l, sm_r, cs_l, cs_r, pay, cs_s, gb, member, picks, prod,
    hot, lhs, seg, oldp, smp, cop, base, pos, etab, eedge, e_d, e_o, key, cs, cf, cs2, t3, khot, klhs, hot_n, shares,
    invc,
    in_sem, tile_sem, surf_ss, surf_rs, halo_ss, halo_rs, inv_ss, inv_rs, sm_ss, sm_rs, cs_ss, cs_rs,
    ag_ss, ag_rs, plane_sem, space_sem,
):
    g = lax.axis_index("comp")
    t = lax.axis_index("tile")
    n = lax.axis_size("tile")
    left, right = lax.rem(t + n - 1, n), lax.rem(t + 1, n)
    y, z, x = lax.rem(t, 4), lax.rem(lax.div(t, 4), 4), lax.div(t, 16)
    ys = [lax.rem(y + d, 4) for d in range(4)]
    zs = [4 * lax.rem(z + d, 4) for d in range(4)]
    xs = [16 * lax.rem(x + d, 4) for d in range(4)]
    ring_y = [xs[0] + zs[0] + ys[d] for d in (1, 2, 3)]
    ring_z = [xs[0] + zs[d] + ys[0] for d in (1, 2, 3)]
    ring_x = [xs[d] + zs[0] + ys[0] for d in (1, 2, 3)]
    bar = pltpu.get_barrier_semaphore()

    def signal(sem, group, tile):
        pl.semaphore_signal(sem, inc=1, device_id=(group, tile), device_id_type=MESH)

    loads = [
        pltpu.make_async_copy(inputs[i], local[i], in_sem.at[i]) for i in range(18)
    ]
    for i in (15, 14, 0, 5, 8, 9, 10, 11, 12, 4, 2, 1, 6, 7, 17, 3, 16, 13):
        loads[i].start()
    for d in (2, -2, 1, -1, 0):
        signal(bar, 1 - g, lax.rem(t + n + d, n))
    for tile in (left, right, *ring_y, *ring_z, *ring_x):
        signal(bar, g, tile)

    tiles = inputs[18]
    chunks = 4
    per = 160 // chunks
    tile_copies = [
        pltpu.make_async_copy(
            tiles.at[pl.ds(c * per, per)], tl.at[pl.ds(c * per, per)], tile_sem.at[c]
        )
        for c in range(chunks)
    ]
    for c in tile_copies:
        c.start()

    def ready(*which):
        for i in which:
            loads[i].wait()

    ready(15, 14)

    def gather(i, carry):
        for a in range(8):
            s = i * 8 + a
            outg[s] = surf[jnp.minimum(sendb[0, s], 63)]
        return carry

    lax.fori_loop(0, 20, gather, 0)

    ready(0, 5, 8, 9, 10, 11, 12, 4, 2)
    row8 = iota((8, 128), 0)
    cpos = [ctab[k] - 16 - 128 * row8 for k in range(3)]
    csum = cedge[0] + cedge[1] + cedge[2]
    c_d = cdiag[...] + csum
    for k in range(3):
        etab[k, 2:10, :] = cpos[k].astype(F32)
        etab[k, 12:16, :] = jnp.zeros((4, 128), F32)
        eedge[k, 2:10, :] = cedge[k]
        eedge[k, 12:16, :] = jnp.zeros((4, 128), F32)
    e_d[...] = jnp.ones((24, 128), F32)
    e_d[3:11, :] = c_d
    e_o[...] = jnp.zeros((24, 128), F32)
    e_o[3:11, :] = cown[...].astype(F32)
    for side, block, low in ((0, 0, 0), (1, 63, 6)):
        hs[side, 0:8, :] = fields[block]
        hs[side, 8:9, :] = oldh[block : block + 1, :]
        hs[side, 9:10, :] = fown[block : block + 1, :].astype(F32)
        for k in range(3):
            here = ftab[k, block : block + 1, :] - (128 + 128 * block)
            hs[side, 10 + k : 11 + k, :] = here.astype(F32)
            hs[side, 13 + k : 14 + k, :] = edge[k, block : block + 1, :]
        for k in range(3):
            hs[side, 16 + 2 * k : 18 + 2 * k, :] = etab[k, 2 + low : 4 + low, :]
            hs[side, 22 + 2 * k : 24 + 2 * k, :] = cedge[k, low : low + 2, :]
        hs[side, 28:30, :] = e_d[3 + low : 5 + low, :]
        hs[side, 30:32, :] = e_o[3 + low : 5 + low, :]

    pl.semaphore_wait(bar, 16)

    surf_copies = [
        pltpu.make_async_remote_copy(
            src_ref=outg.at[pl.ds(32 * j, 32)],
            dst_ref=inc.at[pl.ds(32 * j, 32)],
            send_sem=surf_ss.at[j],
            recv_sem=surf_rs.at[j],
            device_id=(1 - g, lax.rem(t + n + 2 - j, n)),
            device_id_type=MESH,
        )
        for j in range(5)
    ]

    def pair(to_left, at_right, to_right, at_left, ss, rs):
        return [
            pltpu.make_async_remote_copy(
                src_ref=to_left, dst_ref=at_right, send_sem=ss.at[0], recv_sem=rs.at[0],
                device_id=(g, left), device_id_type=MESH,
            ),
            pltpu.make_async_remote_copy(
                src_ref=to_right, dst_ref=at_left, send_sem=ss.at[1], recv_sem=rs.at[1],
                device_id=(g, right), device_id_type=MESH,
            ),
        ]

    halo_copies = pair(hs.at[0], hr.at[1], hs.at[1], hr.at[0], halo_ss, halo_rs)
    inv_copies = pair(inputs[13], invr.at[1], inputs[13], invr.at[0], inv_ss, inv_rs)
    for c in halo_copies + surf_copies:
        c.start()
    for tile in ring_z:
        signal(plane_sem, g, tile)

    ready(1, 6, 7, 17, 3, 16, 13)
    def positions(i, carry):
        at = pl.ds(pl.multiple_of(i * 8, 8), 8)
        total = edge[0, at, :] + edge[1, at, :] + edge[2, at, :]
        share = 1.0 / total
        for k in range(3):
            pos[k, at, :] = ftab[k, at, :] - 128 - 128 * (i * 8 + row8)
            shares[k, at, :] = edge[k, at, :] * share
        return carry

    lax.fori_loop(0, 8, positions, 0)

    def column(ref, count):
        out = jnp.zeros((8, 128), F32)
        for level in range(count):
            out = jnp.where(row8 == level, ref[0, level], out)
        return out

    rates, weights = column(rate_s, 8), column(lw_s, 8)

    def advance(j, prev, cur, nxt):
        beside = None
        for k in range(3):
            p = spread(pos[k, pl.ds(j, 1), :])
            w = spread(shares[k, pl.ds(j, 1), :])
            term = w * pick(prev, cur, nxt, p)
            beside = term if beside is None else beside + term
        new = cur + rates * (beside - cur)
        newf[j] = new
        base[pl.ds(j, 1), :] = jnp.sum(weights * new, axis=0, keepdims=True)

    def advance8(i, carry):
        for a in range(8):
            j = i * 8 + a
            advance(j, fields[j - 1], fields[j], fields[j + 1])
        return carry

    lax.fori_loop(1, 7, advance8, 0)
    for j in (*range(1, 8), *range(56, 63)):
        advance(j, fields[j - 1], fields[j], fields[j + 1])

    lane8 = iota((8, 128), 1)
    blocks = iota((64, 160), 0)
    member[...] = jnp.where(
        blocks == jnp.broadcast_to(eblk[...], (64, 160)), 1.0, 0.0
    ).astype(BF16)

    down = iota((128, 128), 0)

    def one_hot(i, carry):
        for a in range(4):
            r = i * 4 + a
            row = fown[pl.ds(r, 1), :] & 127
            at = pl.ds(pl.multiple_of(r * 128, 128), 128)
            hot[:, at] = jnp.where(down == spread(row, 128), 1.0, 0.0).astype(BF16)
        return carry

    lax.fori_loop(0, 16, one_hot, 0)
    for c in halo_copies:
        c.wait_recv()
    advance(0, hr[0, 0:8, :], fields[0], fields[1])
    advance(63, fields[62], fields[63], hr[1, 0:8, :])
    oldp[7:8, :] = hr[0, 8:9, :]
    oldp[8:72, :] = oldh[...]
    oldp[72:73, :] = hr[1, 8:9, :]
    def neighbours(ref, r, at_ref_row):
        out = None
        prev = ref[at_ref_row - 1 : at_ref_row + 7, :]
        cur = ref[at_ref_row : at_ref_row + 8, :]
        nxt = ref[at_ref_row + 1 : at_ref_row + 9, :]
        for k in range(3):
            at = slice(8 * r, 8 * r + 8)
            term = edge[k, at, :] * pick(prev, cur, nxt, pos[k, at, :])
            out = term if out is None else out + term
        return out

    def totals(r):
        at = slice(8 * r, 8 * r + 8)
        return fdiag[at, :] + (edge[0, at, :] + edge[1, at, :] + edge[2, at, :])

    for r in range(8):
        at = slice(8 * r, 8 * r + 8)
        smp[8 + 8 * r : 16 + 8 * r, :] = neighbours(oldp, r, 8 + 8 * r)

    row16 = iota((16, 128), 0)
    for k in range(3):
        etab[k, 0:2, :] = hr[0, 16 + 2 * k : 18 + 2 * k, :]
        etab[k, 10:12, :] = hr[1, 16 + 2 * k : 18 + 2 * k, :]
        eedge[k, 0:2, :] = hr[0, 22 + 2 * k : 24 + 2 * k, :]
        eedge[k, 10:12, :] = hr[1, 22 + 2 * k : 24 + 2 * k, :]
    e_d[1:3, :] = hr[0, 28:30, :]
    e_d[11:13, :] = hr[1, 28:30, :]
    e_o[1:3, :] = hr[0, 30:32, :]
    e_o[11:13, :] = hr[1, 30:32, :]
    side = jnp.where(row16 < 2, 7, jnp.where(row16 >= 10, 1, 0))
    key[...] = ((t + side) & 7) * 16 + e_o[1:17, :].astype(I32)
    for r in range(12):
        khot[:, 128 * r : 128 * r + 128] = jnp.where(
            down == spread(key[r : r + 1, :], 128), 1.0, 0.0
        ).astype(BF16)
    for i in range(2):
        owner = spread(hr[i, 9:10, :], 128).astype(I32) & 127
        hot_n[i] = jnp.where(down == owner, 1.0, 0.0).astype(BF16)
    for c in surf_copies:
        c.wait_recv()
    for c in tile_copies:
        c.wait()

    for c in inv_copies:
        c.start()
    pl.semaphore_wait(plane_sem, 3)
    for tile in ring_x:
        signal(space_sem, g, tile)
    def choose(i, carry):
        for b in range(16):
            e = i * 16 + b
            picks[pl.ds(pl.multiple_of(e * 4, 4), 4), :] = inc[eslot[0, e]].astype(F32)
        return carry

    lax.fori_loop(0, 10, choose, 0)
    quarter = row16 // 4
    for i in range(40):
        at = slice(16 * i, 16 * i + 16)
        rows = picks[at, :]
        ab = jnp.where(quarter < 2, rows, 0.0).astype(BF16)
        cd = jnp.where(quarter < 2, 0.0, rows).astype(BF16)
        four = tl[4 * i : 4 * i + 4]
        out = dot(
            jnp.concatenate([ab, cd], axis=1),
            jnp.concatenate(
                [four[0:2].reshape(256, 128), four[2:4].reshape(256, 128)], axis=1
            ),
            NT,
        )
        prod[at, :] = jnp.where(quarter % 2 == 0, out[:, 0:128], out[:, 128:256])

    for f in range(4):
        high, low = split(prod[pl.ds(f, 160, stride=4), :])
        both = dot(member[...], jnp.concatenate([high, low], axis=1), NN)
        recv[pl.ds(f, 64, stride=4), :] = both[:, 0:128] + both[:, 128:256]

    for r in range(8):
        at = slice(8 * r, 8 * r + 8)
        out = base[at, :]
        for f in range(4):
            out = out + fw_s[0, f] * recv[pl.ds(32 * r + f, 8, stride=4), :]
        base[at, :] = out
        prev = oldh[at, :]
        whole = totals(r)
        smp[8 + 8 * r : 16 + 8 * r, :] = (
            prev + RELAX * (out - (whole * prev - smp[8 + 8 * r : 16 + 8 * r, :])) / whole
        )

    sm_copies = pair(smp.at[pl.ds(8, 8)], sm_r, smp.at[pl.ds(64, 8)], sm_l, sm_ss, sm_rs)
    for c in sm_copies:
        c.start()
    smp[7:8, :] = jnp.zeros((1, 128), F32)
    smp[72:73, :] = jnp.zeros((1, 128), F32)

    def spot(row, owner):
        mine = jnp.where(spread(owner >> 7) == row8, spread(row), 0.0)
        return jnp.concatenate(list(split_f32(mine)), axis=0).astype(BF16)

    for r in range(8):
        at = slice(8 * r, 8 * r + 8)
        cur = smp[8 + 8 * r : 16 + 8 * r, :]
        res = base[at, :] - (totals(r) * cur - neighbours(smp, r, 8 + 8 * r))
        for a in range(8):
            where = slice(128 * (8 * r + a), 128 * (8 * r + a) + 128)
            lhs[:, where] = spot(res[a : a + 1], fown[8 * r + a : 8 * r + a + 1, :])
    for r in range(2):
        where = slice(4096 * r, 4096 * r + 4096)
        seg[r] = dot(lhs[:, where], hot[:, where], NT)
    source = (seg[0, 0:8] + seg[0, 8:16]) + (seg[1, 0:8] + seg[1, 8:16])
    cs_s[...] = source
    cs_copies = pair(cs_s, cs_r, cs_s, cs_l, cs_ss, cs_rs)
    for c in cs_copies:
        c.start()

    def from_here(i, row, towards):
        row = spread(row)
        out = jnp.zeros((8, 128), F32)
        for k in range(3):
            p = spread(hr[i, 10 + k : 11 + k, :]).astype(I32)
            term = spread(hr[i, 13 + k : 14 + k, :]) * take(row, p & 127)
            out = out + jnp.where(towards(p), term, 0.0)
        both = dot(jnp.concatenate(list(split_f32(out)), axis=0).astype(BF16), hot_n[i], NT)
        return both[0:1] + both[8:9]

    extra_l = from_here(0, smp[8:9, :], lambda p: p > 127)
    extra_r = from_here(1, smp[71:72, :], lambda p: p < 0)
    cs[...] = jnp.zeros((24, 128), F32)
    cs[2:3, :] = extra_l
    cs[3:11, :] = source
    cs[11:12, :] = extra_r
    cf[...] = jnp.zeros((24, 128), F32)
    cs2[...] = jnp.zeros((24, 128), F32)
    cf[0:16, :] = RELAX * cs[0:16, :] / e_d[0:16, :]

    def coarse_neighbours(ref):
        out = None
        for k in range(3):
            term = eedge[k] * pick(
                ref[0:16, :], ref[1:17, :], ref[2:18, :], etab[k].astype(I32)
            )
            out = term if out is None else out + term
        return out

    left_over = cs[1:17, :] - e_d[1:17, :] * cf[1:17, :] + coarse_neighbours(cf)
    klhs[...] = jnp.zeros((8, 1536), F32)
    for r in range(12):
        klhs[0:1, 128 * r : 128 * r + 128] = left_over[r : r + 1]
    packed = jnp.concatenate(list(split_f32(klhs[...])), axis=0).astype(BF16)
    bottoms = dot(packed, khot[...], NT)
    pay[0] = bottoms[0:1] + bottoms[8:9]
    gb[t] = pay[0]

    pl.semaphore_wait(space_sem, 3)
    hops = (0, 1, 2, 1)
    others = sorted(
        ((a, b, c) for a in range(4) for b in range(4) for c in range(4)),
        key=lambda d: -(hops[d[0]] + hops[d[1]] + hops[d[2]]),
    )[:-1]
    for a, b, c in others:
        pltpu.make_async_remote_copy(
            src_ref=pay,
            dst_ref=gb.at[pl.ds(t, 1)],
            send_sem=ag_ss,
            recv_sem=ag_rs,
            device_id=(g, xs[a] + zs[b] + ys[c]),
            device_id_type=MESH,
        ).start()

    for c in inv_copies:
        c.wait_recv()
    for at, block in ((0, cinv[...]), (16, invr[0]), (32, invr[1])):
        high, low = split(block)
        invc[at : at + 16, :] = high
        invc[48 + at : 64 + at, :] = low
    invc[96:128, :] = jnp.zeros((32, 1024), BF16)
    for c in sm_copies:
        c.wait_send()
        c.wait_recv()
    smp[7:8, :] = sm_l[7:8, :]
    smp[72:73, :] = sm_r[0:1, :]
    far_l, far_r = spread(sm_l[7:8, :]), spread(sm_r[0:1, :])
    more_l = more_r = jnp.zeros((8, 128), F32)
    for k in range(3):
        p = pos[k, 0:8, :]
        more_l = more_l + jnp.where(p < 0, edge[k, 0:8, :] * take(far_l, p & 127), 0.0)
        p = pos[k, 56:64, :]
        more_r = more_r + jnp.where(p > 127, edge[k, 56:64, :] * take(far_r, p & 127), 0.0)
    sums = dot(spot(more_l[0:1], fown[0:1, :]), hot[:, 0:128], NT)
    sums = sums + dot(spot(more_r[7:8], fown[63:64, :]), hot[:, 8064:8192], NT)
    more = sums[0:8] + sums[8:16]
    for c in cs_copies:
        c.wait_recv()
    cs[1:3, :] = cs_l[6:8, :] + cs[1:3, :]
    cs[3:11, :] = cs[3:11, :] + more
    cs[11:13, :] = cs_r[0:2, :] + cs[11:13, :]
    cf[0:16, :] = RELAX * cs[0:16, :] / e_d[0:16, :]

    everyone = pltpu.make_async_remote_copy(
        src_ref=gb.at[pl.ds(0, n - 1)],
        dst_ref=gb.at[pl.ds(0, n - 1)],
        send_sem=ag_ss,
        recv_sem=ag_rs,
        device_id=(g, right),
        device_id_type=MESH,
    )
    everyone.wait_recv()
    from_right = (row8 == 0) & (lane8 >= 112)
    from_left = (row8 == 7) & (lane8 < 16)
    groups = [gb[8 * j : 8 * j + 8, 0, :] for j in range(8)]
    flat = []
    for j in range(8):
        mix = jnp.where(
            from_right, groups[(j + 1) % 8], jnp.where(from_left, groups[(j - 1) % 8], groups[j])
        )
        flat.append(jnp.sum(mix, axis=0, keepdims=True))
    flat = spread_all(jnp.concatenate(flat, axis=1))
    packed = jnp.concatenate(list(split_f32(flat)), axis=0).astype(BF16)
    found = dot(packed, invc[...], NT)
    value = found[0:1] + found[8:9]
    value = value + pltpu.roll(spread(value), 128 - 48, 1)[0:1]
    value = spread(value, 16)
    shift = jnp.where(row16 < 3, 16, jnp.where(row16 < 11, 0, 32))
    cs2[0:16, :] = cf[0:16, :] + take(value, jnp.minimum(e_o[0:16, :].astype(I32), 15) + shift)
    cur = cs2[1:17, :]
    whole = e_d[1:17, :]
    t3[...] = cur + RELAX * (cs[1:17, :] - (whole * cur - coarse_neighbours(cs2))) / whole

    for r in range(8):
        at = slice(8 * r, 8 * r + 8)
        owner = fown[at, :]
        high, lane = owner >> 7, owner & 127
        out = smp[8 + 8 * r : 16 + 8 * r, :]
        for h in range(8):
            out = out + jnp.where(high == h, take(spread(t3[2 + h : 3 + h, :]), lane), 0.0)
        cop[8 + 8 * r : 16 + 8 * r, :] = out
    own_l = spread(hr[0, 9:10, :]).astype(I32) & 127
    own_r = spread(hr[1, 9:10, :]).astype(I32) & 127
    cop[7:8, :] = smp[7:8, :] + take(spread(t3[1:2, :]), own_l)[0:1]
    cop[72:73, :] = smp[72:73, :] + take(spread(t3[10:11, :]), own_r)[0:1]
    for r in range(8):
        at = slice(8 * r, 8 * r + 8)
        cur = cop[8 + 8 * r : 16 + 8 * r, :]
        whole = totals(r)
        beside = neighbours(cop, r, 8 + 8 * r)
        height[at, :] = cur + RELAX * (base[at, :] - (whole * cur - beside)) / whole

    for c in halo_copies + surf_copies + inv_copies + cs_copies:
        c.wait_send()
    everyone.wait_send()


def write_out(a, b, c, a_out, b_out, c_out, sems):
    copies = [
        pltpu.make_async_copy(source, target, sems.at[i])
        for i, (source, target) in enumerate(((a, a_out), (b, b_out), (c, c_out)))
    ]
    for copy in copies:
        copy.start()
    for copy in copies:
        copy.wait()


def split_f32(x):
    high = x.astype(BF16).astype(F32)
    return high, x - high


def spread_all(row):
    return jnp.broadcast_to(row, (8, row.shape[1]))


def per_device(
    fields, level_rate, edge_weight, fine_diagonal, fine_table, old_height, level_weight,
    flux_weight, fine_owner, coarse_table, coarse_edge, coarse_diagonal, coarse_owner,
    coarse_inverse, surface_out, send_blocks, entry_slot, entry_block, remap_tiles,
):
    operands = (
        fields.reshape(8, 64, 128).transpose(1, 0, 2),
        level_rate,
        edge_weight.reshape(3, 64, 128),
        fine_diagonal.reshape(64, 128),
        fine_table.reshape(3, 64, 128),
        old_height.reshape(64, 128),
        level_weight,
        flux_weight,
        fine_owner.reshape(64, 128),
        coarse_table.reshape(3, 8, 128),
        coarse_edge.reshape(3, 8, 128),
        coarse_diagonal.reshape(8, 128),
        coarse_owner.reshape(8, 128),
        coarse_inverse.reshape(16, 1024),
        surface_out.reshape(4, 64, 128).transpose(1, 0, 2),
        send_blocks.reshape(1, 160),
        entry_slot.reshape(1, 160),
        entry_block.reshape(1, 160),
        remap_tiles.reshape(160, 128, 128),
    )
    vmem = pl.BlockSpec(memory_space=pltpu.VMEM)
    specs = [pl.BlockSpec(memory_space=pltpu.HBM)] * 19
    V = pltpu.VMEM
    local = [
        (pltpu.SMEM if i in (1, 6, 7, 15, 16) else V)(x.shape, x.dtype)
        for i, x in enumerate(operands)
    ]
    D = pltpu.SemaphoreType.DMA
    new, got, high = pl.pallas_call(
        kernel,
        out_shape=(
            jax.ShapeDtypeStruct((64, 8, 128), F32),
            jax.ShapeDtypeStruct((256, 128), F32),
            jax.ShapeDtypeStruct((64, 128), F32),
        ),
        in_specs=specs,
        out_specs=(vmem, vmem, vmem),
        scratch_shapes=[
            *local,
            V((160, 4, 128), BF16),
            V((160, 4, 128), BF16),
            V((2, 32, 128), F32),
            V((2, 32, 128), F32),
            V((2, 16, 1024), F32),
            V((8, 128), F32),
            V((8, 128), F32),
            V((8, 128), F32),
            V((8, 128), F32),
            V((1, 1, 128), F32),
            V((8, 128), F32),
            V((64, 1, 128), F32),
            V((64, 160), BF16),
            V((640, 128), F32),
            V((640, 128), F32),
            V((128, 8192), BF16),
            V((16, 8192), BF16),
            V((2, 16, 128), F32),
            V((80, 128), F32),
            V((80, 128), F32),
            V((80, 128), F32),
            V((64, 128), F32),
            V((3, 64, 128), I32),
            V((3, 16, 128), F32),
            V((3, 16, 128), F32),
            V((24, 128), F32),
            V((24, 128), F32),
            V((16, 128), I32),
            V((24, 128), F32),
            V((24, 128), F32),
            V((24, 128), F32),
            V((16, 128), F32),
            V((128, 1536), BF16),
            V((8, 1536), F32),
            V((2, 128, 128), BF16),
            V((3, 64, 128), F32),
            V((128, 1024), BF16),
            D((18,)),
            D((4,)),
            D((5,)), D((5,)),
            D((2,)), D((2,)),
            D((2,)), D((2,)),
            D((2,)), D((2,)),
            D((2,)), D((2,)),
            D, D,
            pltpu.SemaphoreType.REGULAR, pltpu.SemaphoreType.REGULAR,
        ],
        compiler_params=pltpu.CompilerParams(
            collective_id=0, has_side_effects=True, vmem_limit_bytes=48 << 20
        ),
        name="step",
    )(*[pltpu.with_memory_space_constraint(x, pltpu.HBM) for x in operands])
    new, got, high = pl.pallas_call(
        write_out,
        out_shape=tuple(jax.ShapeDtypeStruct(v.shape, v.dtype) for v in (new, got, high)),
        in_specs=[vmem] * 3,
        out_specs=[pl.BlockSpec(memory_space=pltpu.HBM)] * 3,
        scratch_shapes=[D((3,))],
        compiler_params=pltpu.CompilerParams(vmem_limit_bytes=1 << 20),
        name="write_out",
    )(new, got, high)
    return (
        new.transpose(1, 0, 2).reshape(1, 8, 8192),
        got.reshape(64, 4, 128).transpose(1, 0, 2).reshape(1, 4, 8192),
        high.reshape(1, 8192),
    )


def solution(mesh):
    in_specs = (
        P("comp", None, "tile"),
        P("comp", None),
        P("comp", None, "tile"),
        P("comp", "tile"),
        P("comp", None, "tile"),
        P("comp", "tile"),
        P("comp", None),
        P("comp", None),
        P("comp", "tile"),
        P("comp", None, "tile"),
        P("comp", None, "tile"),
        P("comp", "tile"),
        P("comp", "tile"),
        P("comp", "tile", None),
        P("comp", None, "tile"),
        P("comp", "tile", None),
        P("comp", "tile", None),
        P("comp", "tile", None),
        P("comp", "tile", None, None, None),
    )
    out_specs = (P("comp", None, "tile"), P("comp", None, "tile"), P("comp", "tile"))
    return jax.shard_map(
        per_device, mesh=mesh, in_specs=in_specs, out_specs=out_specs, check_vma=False
    )
```

```python
import functools

import jax
import jax.numpy as jnp
from jax import lax
from jax.experimental import pallas as pl
from jax.experimental.pallas import tpu as pltpu
from jax.sharding import PartitionSpec as P

MESH = pl.DeviceIdType.MESH
F32, BF16, I32 = jnp.float32, jnp.bfloat16, jnp.int32
RELAX = 0.8
NT = (((1,), (1,)), ((), ()))
NN = (((1,), (0,)), ((), ()))


def take(x, lane):
    return jnp.take_along_axis(x, lane, axis=1, mode="promise_in_bounds")


def pick(prev, cur, nxt, pos):
    lane = pos & 127
    return jnp.where(
        pos < 0, take(prev, lane), jnp.where(pos > 127, take(nxt, lane), take(cur, lane))
    )


def spread(row, count=8):
    return jnp.broadcast_to(row, (count, 128))


def iota(shape, dim):
    return lax.broadcasted_iota(I32, shape, dim)


def split(x):
    high = x.astype(BF16)
    return high, (x - high.astype(F32)).astype(BF16)


def dot(a, b, dims):
    return lax.dot_general(a, b, dims, preferred_element_type=F32)


def kernel(
    *refs,
):
    inputs, outputs, scratch = refs[:19], refs[19:22], refs[22:]
    local, scratch = scratch[:19], scratch[19:]
    step(*local, *outputs, inputs, local, *scratch)


def step(
    fields, rate_s, edge, fdiag, ftab, oldh, lw_s, fw_s, fown, ctab, cedge, cdiag, cown,
    cinv, surf, sendb, eslot, eblk, tl,
    newf, recv, height, inputs, local,
    outg, inc, hs, hr, invr, sm_l, sm_r, cs_l, cs_r, pay, cs_s, gb, member, picks, prod,
    hot, lhs, seg, oldp, smp, cop, base, pos, etab, eedge, e_d, e_o, key, cs, cf, cs2, t3, khot, klhs, hot_n, shares,
    invc, rl, rh,
    in_sem, tile_sem, surf_ss, surf_rs, halo_ss, halo_rs, inv_ss, inv_rs, sm_ss, sm_rs, cs_ss, cs_rs,
    ag_ss, ag_rs, plane_sem, space_sem, rl_ss, rl_rs, rh_ss, rh_rs,
):
    g = lax.axis_index("comp")
    t = lax.axis_index("tile")
    n = lax.axis_size("tile")
    left, right = lax.rem(t + n - 1, n), lax.rem(t + 1, n)
    seat, back = lax.rem(t, 16), lax.rem(t + n - 16, n)
    y, z, x = lax.rem(t, 4), lax.rem(lax.div(t, 4), 4), lax.div(t, 16)
    ys = [lax.rem(y + d, 4) for d in range(4)]
    zs = [4 * lax.rem(z + d, 4) for d in range(4)]
    xs = [16 * lax.rem(x + d, 4) for d in range(4)]
    ring_y = [xs[0] + zs[0] + ys[d] for d in (1, 2, 3)]
    ring_z = [xs[0] + zs[d] + ys[0] for d in (1, 2, 3)]
    ring_x = [xs[d] + zs[0] + ys[0] for d in (1, 2, 3)]
    bar = pltpu.get_barrier_semaphore()

    def signal(sem, group, tile):
        pl.semaphore_signal(sem, inc=1, device_id=(group, tile), device_id_type=MESH)

    loads = [
        pltpu.make_async_copy(inputs[i], local[i], in_sem.at[i]) for i in range(18)
    ]
    for i in (15, 14, 0, 5, 8, 9, 10, 11, 12, 4, 2, 1, 6, 7, 17, 3, 16, 13):
        loads[i].start()
    def greet(ok, group, tile):
        if ok is None:
            signal(bar, group, tile)
        else:
            pl.when(ok)(functools.partial(signal, bar, group, tile))

    for d, ok in ((-2, seat < 14), (2, None), (-1, seat < 15), (1, None)):
        greet(ok, 1 - g, lax.rem(t + n - d, n))
    greet(None, g, left)
    greet(seat < 15, g, right)
    greet(seat < 2, 1 - g, lax.rem(t + 16, n))
    for tile in (*ring_y, *ring_z, *ring_x):
        signal(bar, g, tile)
    signal(bar, 1 - g, t)

    tiles = inputs[18]
    chunks = 4
    per = 160 // chunks
    tile_copies = [
        pltpu.make_async_copy(
            tiles.at[pl.ds(c * per, per)], tl.at[pl.ds(c * per, per)], tile_sem.at[c]
        )
        for c in range(chunks)
    ]
    for c in tile_copies:
        c.start()

    def ready(*which):
        for i in which:
            loads[i].wait()

    ready(15, 14)

    def gather(i, carry):
        for a in range(8):
            s = i * 8 + a
            outg[s] = surf[jnp.minimum(sendb[0, s], 63)]
        return carry

    lax.fori_loop(0, 20, gather, 0)

    ready(0, 5, 8, 9, 10, 11, 12, 4, 2)
    row8 = iota((8, 128), 0)
    cpos = [ctab[k] - 16 - 128 * row8 for k in range(3)]
    csum = cedge[0] + cedge[1] + cedge[2]
    c_d = cdiag[...] + csum
    for k in range(3):
        etab[k, 2:10, :] = cpos[k].astype(F32)
        etab[k, 12:16, :] = jnp.zeros((4, 128), F32)
        eedge[k, 2:10, :] = cedge[k]
        eedge[k, 12:16, :] = jnp.zeros((4, 128), F32)
    e_d[...] = jnp.ones((24, 128), F32)
    e_d[3:11, :] = c_d
    e_o[...] = jnp.zeros((24, 128), F32)
    e_o[3:11, :] = cown[...].astype(F32)
    for side, block, low in ((0, 0, 0), (1, 63, 6)):
        hs[side, 0:8, :] = fields[block]
        hs[side, 8:9, :] = oldh[block : block + 1, :]
        hs[side, 9:10, :] = fown[block : block + 1, :].astype(F32)
        for k in range(3):
            here = ftab[k, block : block + 1, :] - (128 + 128 * block)
            hs[side, 10 + k : 11 + k, :] = here.astype(F32)
            hs[side, 13 + k : 14 + k, :] = edge[k, block : block + 1, :]
        for k in range(3):
            hs[side, 16 + 2 * k : 18 + 2 * k, :] = etab[k, 2 + low : 4 + low, :]
            hs[side, 22 + 2 * k : 24 + 2 * k, :] = cedge[k, low : low + 2, :]
        hs[side, 28:30, :] = e_d[3 + low : 5 + low, :]
        hs[side, 30:32, :] = e_o[3 + low : 5 + low, :]

    pl.semaphore_wait(bar, jnp.where(seat == 0, 14, 16))

    surf_copies = [
        pltpu.make_async_remote_copy(
            src_ref=outg.at[pl.ds(32 * j, 32)],
            dst_ref=inc.at[pl.ds(32 * j, 32)],
            send_sem=surf_ss.at[j],
            recv_sem=surf_rs.at[j],
            device_id=(1 - g, lax.rem(t + n + 2 - j, n)),
            device_id_type=MESH,
        )
        for j in range(5)
    ]

    def pair(to_left, at_right, to_right, at_left, ss, rs):
        return [
            pltpu.make_async_remote_copy(
                src_ref=to_left, dst_ref=at_right, send_sem=ss.at[0], recv_sem=rs.at[0],
                device_id=(g, left), device_id_type=MESH,
            ),
            pltpu.make_async_remote_copy(
                src_ref=to_right, dst_ref=at_left, send_sem=ss.at[1], recv_sem=rs.at[1],
                device_id=(g, right), device_id_type=MESH,
            ),
        ]

    halo_copies = pair(hs.at[0], hr.at[1], hs.at[1], hr.at[0], halo_ss, halo_rs)
    inv_copies = pair(inputs[13], invr.at[1], inputs[13], invr.at[0], inv_ss, inv_rs)
    def relayed(source, landing, ss, rs, group):
        return pltpu.make_async_remote_copy(
            src_ref=source, dst_ref=landing, send_sem=ss, recv_sem=rs,
            device_id=(group, back), device_id_type=MESH,
        )

    def handed(source, landing, ss, rs, ahead):
        return pltpu.make_async_remote_copy(
            src_ref=source, dst_ref=landing, send_sem=ss, recv_sem=rs,
            device_id=(g, lax.rem(t + ahead, n)), device_id_type=MESH,
        )

    surf_in = [
        relayed(
            outg.at[pl.ds(32 * j, 32)], rl.at[j - 3], surf_ss.at[j], rl_rs.at[j - 3], 1 - g
        )
        for j in (3, 4)
    ]
    surf_on = [
        handed(
            rl.at[j - 3], inc.at[pl.ds(32 * j, 32)], rl_ss.at[j - 3], surf_rs.at[j], 18 - j
        )
        for j in (3, 4)
    ]
    halo_in = relayed(hs.at[0], rh, halo_ss.at[0], rh_rs, g)
    halo_on = handed(rh, hr.at[1], rh_ss, halo_rs.at[0], 15)

    def either(ok, direct, other):
        pl.when(ok)(direct.start)
        pl.when(jnp.logical_not(ok))(other.start)

    either(seat >= 1, halo_copies[0], halo_in)
    halo_copies[1].start()
    either(seat >= 2, surf_copies[4], surf_in[1])
    surf_copies[0].start()
    either(seat >= 1, surf_copies[3], surf_in[0])
    surf_copies[1].start()
    surf_copies[2].start()
    for tile in ring_z:
        signal(plane_sem, g, tile)

    ready(1, 6, 7, 17, 3, 16, 13)
    def positions(i, carry):
        at = pl.ds(pl.multiple_of(i * 8, 8), 8)
        total = edge[0, at, :] + edge[1, at, :] + edge[2, at, :]
        share = 1.0 / total
        for k in range(3):
            pos[k, at, :] = ftab[k, at, :] - 128 - 128 * (i * 8 + row8)
            shares[k, at, :] = edge[k, at, :] * share
        return carry

    lax.fori_loop(0, 8, positions, 0)

    def column(ref, count):
        out = jnp.zeros((8, 128), F32)
        for level in range(count):
            out = jnp.where(row8 == level, ref[0, level], out)
        return out

    rates, weights = column(rate_s, 8), column(lw_s, 8)

    def advance(j, prev, cur, nxt):
        beside = None
        for k in range(3):
            p = spread(pos[k, pl.ds(j, 1), :])
            w = spread(shares[k, pl.ds(j, 1), :])
            term = w * pick(prev, cur, nxt, p)
            beside = term if beside is None else beside + term
        new = cur + rates * (beside - cur)
        newf[j] = new
        base[pl.ds(j, 1), :] = jnp.sum(weights * new, axis=0, keepdims=True)

    def advance8(i, carry):
        for a in range(8):
            j = i * 8 + a
            advance(j, fields[j - 1], fields[j], fields[j + 1])
        return carry

    lax.fori_loop(1, 7, advance8, 0)
    for j in (*range(1, 8), *range(56, 63)):
        advance(j, fields[j - 1], fields[j], fields[j + 1])

    lane8 = iota((8, 128), 1)
    blocks = iota((64, 160), 0)
    member[...] = jnp.where(
        blocks == jnp.broadcast_to(eblk[...], (64, 160)), 1.0, 0.0
    ).astype(BF16)

    down = iota((128, 128), 0)

    def one_hot(i, carry):
        for a in range(4):
            r = i * 4 + a
            row = fown[pl.ds(r, 1), :] & 127
            at = pl.ds(pl.multiple_of(r * 128, 128), 128)
            hot[:, at] = jnp.where(down == spread(row, 128), 1.0, 0.0).astype(BF16)
        return carry

    lax.fori_loop(0, 16, one_hot, 0)
    pl.semaphore_wait(plane_sem, 3)
    for tile in ring_x:
        signal(space_sem, g, tile)

    @pl.when(seat == 0)
    def _():
        halo_in.wait_recv()
        halo_on.start()
        surf_in[0].wait_recv()
        surf_on[0].start()

    @pl.when(seat < 2)
    def _():
        surf_in[1].wait_recv()
        surf_on[1].start()

    inv_copies[1].start()
    for c in halo_copies:
        c.wait_recv()
    advance(0, hr[0, 0:8, :], fields[0], fields[1])
    advance(63, fields[62], fields[63], hr[1, 0:8, :])
    oldp[7:8, :] = hr[0, 8:9, :]
    oldp[8:72, :] = oldh[...]
    oldp[72:73, :] = hr[1, 8:9, :]
    def neighbours(ref, r, at_ref_row):
        out = None
        prev = ref[at_ref_row - 1 : at_ref_row + 7, :]
        cur = ref[at_ref_row : at_ref_row + 8, :]
        nxt = ref[at_ref_row + 1 : at_ref_row + 9, :]
        for k in range(3):
            at = slice(8 * r, 8 * r + 8)
            term = edge[k, at, :] * pick(prev, cur, nxt, pos[k, at, :])
            out = term if out is None else out + term
        return out

    def totals(r):
        at = slice(8 * r, 8 * r + 8)
        return fdiag[at, :] + (edge[0, at, :] + edge[1, at, :] + edge[2, at, :])

    for r in range(8):
        at = slice(8 * r, 8 * r + 8)
        smp[8 + 8 * r : 16 + 8 * r, :] = neighbours(oldp, r, 8 + 8 * r)

    row16 = iota((16, 128), 0)
    def halves(at, block):
        high, low = split(block)
        invc[at : at + 16, :] = high
        invc[48 + at : 64 + at, :] = low

    halves(0, cinv[...])
    invc[96:128, :] = jnp.zeros((32, 1024), BF16)
    for k in range(3):
        etab[k, 0:2, :] = hr[0, 16 + 2 * k : 18 + 2 * k, :]
        etab[k, 10:12, :] = hr[1, 16 + 2 * k : 18 + 2 * k, :]
        eedge[k, 0:2, :] = hr[0, 22 + 2 * k : 24 + 2 * k, :]
        eedge[k, 10:12, :] = hr[1, 22 + 2 * k : 24 + 2 * k, :]
    e_d[1:3, :] = hr[0, 28:30, :]
    e_d[11:13, :] = hr[1, 28:30, :]
    e_o[1:3, :] = hr[0, 30:32, :]
    e_o[11:13, :] = hr[1, 30:32, :]
    side = jnp.where(row16 < 2, 7, jnp.where(row16 >= 10, 1, 0))
    key[...] = ((t + side) & 7) * 16 + e_o[1:17, :].astype(I32)
    for r in range(12):
        khot[:, 128 * r : 128 * r + 128] = jnp.where(
            down == spread(key[r : r + 1, :], 128), 1.0, 0.0
        ).astype(BF16)
    for i in range(2):
        owner = spread(hr[i, 9:10, :], 128).astype(I32) & 127
        hot_n[i] = jnp.where(down == owner, 1.0, 0.0).astype(BF16)
    for c in surf_copies:
        c.wait_recv()
    for c in tile_copies:
        c.wait()

    def choose(i, carry):
        for b in range(16):
            e = i * 16 + b
            picks[pl.ds(pl.multiple_of(e * 4, 4), 4), :] = inc[eslot[0, e]].astype(F32)
        return carry

    lax.fori_loop(0, 10, choose, 0)
    quarter = row16 // 4
    for i in range(40):
        at = slice(16 * i, 16 * i + 16)
        rows = picks[at, :]
        ab = jnp.where(quarter < 2, rows, 0.0).astype(BF16)
        cd = jnp.where(quarter < 2, 0.0, rows).astype(BF16)
        four = tl[4 * i : 4 * i + 4]
        out = dot(
            jnp.concatenate([ab, cd], axis=1),
            jnp.concatenate(
                [four[0:2].reshape(256, 128), four[2:4].reshape(256, 128)], axis=1
            ),
            NT,
        )
        prod[at, :] = jnp.where(quarter % 2 == 0, out[:, 0:128], out[:, 128:256])

    for f in range(4):
        high, low = split(prod[pl.ds(f, 160, stride=4), :])
        both = dot(member[...], jnp.concatenate([high, low], axis=1), NN)
        recv[pl.ds(f, 64, stride=4), :] = both[:, 0:128] + both[:, 128:256]

    for r in range(8):
        at = slice(8 * r, 8 * r + 8)
        out = base[at, :]
        for f in range(4):
            out = out + fw_s[0, f] * recv[pl.ds(32 * r + f, 8, stride=4), :]
        base[at, :] = out
        prev = oldh[at, :]
        whole = totals(r)
        smp[8 + 8 * r : 16 + 8 * r, :] = (
            prev + RELAX * (out - (whole * prev - smp[8 + 8 * r : 16 + 8 * r, :])) / whole
        )

    pl.semaphore_wait(space_sem, 3)
    sm_copies = pair(smp.at[pl.ds(8, 8)], sm_r, smp.at[pl.ds(64, 8)], sm_l, sm_ss, sm_rs)
    for c in sm_copies:
        c.start()
    inv_copies[0].start()
    smp[7:8, :] = jnp.zeros((1, 128), F32)
    smp[72:73, :] = jnp.zeros((1, 128), F32)

    def spot(row, owner):
        mine = jnp.where(spread(owner >> 7) == row8, spread(row), 0.0)
        return jnp.concatenate(list(split_f32(mine)), axis=0).astype(BF16)

    for r in range(8):
        at = slice(8 * r, 8 * r + 8)
        cur = smp[8 + 8 * r : 16 + 8 * r, :]
        res = base[at, :] - (totals(r) * cur - neighbours(smp, r, 8 + 8 * r))
        for a in range(8):
            where = slice(128 * (8 * r + a), 128 * (8 * r + a) + 128)
            lhs[:, where] = spot(res[a : a + 1], fown[8 * r + a : 8 * r + a + 1, :])
    def from_here(i, row, towards):
        row = spread(row)
        out = jnp.zeros((8, 128), F32)
        for k in range(3):
            p = spread(hr[i, 10 + k : 11 + k, :]).astype(I32)
            term = spread(hr[i, 13 + k : 14 + k, :]) * take(row, p & 127)
            out = out + jnp.where(towards(p), term, 0.0)
        both = dot(jnp.concatenate(list(split_f32(out)), axis=0).astype(BF16), hot_n[i], NT)
        return both[0:1] + both[8:9]

    extra_l = from_here(0, smp[8:9, :], lambda p: p > 127)
    extra_r = from_here(1, smp[71:72, :], lambda p: p < 0)
    for r in range(2):
        where = slice(4096 * r, 4096 * r + 4096)
        seg[r] = dot(lhs[:, where], hot[:, where], NT)
    source = (seg[0, 0:8] + seg[0, 8:16]) + (seg[1, 0:8] + seg[1, 8:16])
    cs_s[...] = source
    cs_copies = pair(cs_s, cs_r, cs_s, cs_l, cs_ss, cs_rs)
    for c in cs_copies:
        c.start()

    cs[...] = jnp.zeros((24, 128), F32)
    cs[2:3, :] = extra_l
    cs[3:11, :] = source
    cs[11:12, :] = extra_r
    cf[...] = jnp.zeros((24, 128), F32)
    cs2[...] = jnp.zeros((24, 128), F32)
    cf[0:16, :] = RELAX * cs[0:16, :] / e_d[0:16, :]

    def coarse_neighbours(ref):
        out = None
        for k in range(3):
            term = eedge[k] * pick(
                ref[0:16, :], ref[1:17, :], ref[2:18, :], etab[k].astype(I32)
            )
            out = term if out is None else out + term
        return out

    left_over = cs[1:17, :] - e_d[1:17, :] * cf[1:17, :] + coarse_neighbours(cf)
    klhs[...] = jnp.zeros((8, 1536), F32)
    for r in range(12):
        klhs[0:1, 128 * r : 128 * r + 128] = left_over[r : r + 1]
    packed = jnp.concatenate(list(split_f32(klhs[...])), axis=0).astype(BF16)
    bottoms = dot(packed, khot[...], NT)
    pay[0] = bottoms[0:1] + bottoms[8:9]
    gb[t] = pay[0]

    hops = (0, 1, 2, 1)
    others = sorted(
        ((a, b, c) for a in range(4) for b in range(4) for c in range(4)),
        key=lambda d: -(hops[d[0]] + hops[d[1]] + hops[d[2]]),
    )[:-1]
    for a, b, c in others:
        pltpu.make_async_remote_copy(
            src_ref=pay,
            dst_ref=gb.at[pl.ds(t, 1)],
            send_sem=ag_ss,
            recv_sem=ag_rs,
            device_id=(g, xs[a] + zs[b] + ys[c]),
            device_id_type=MESH,
        ).start()

    inv_copies[1].wait_recv()
    halves(16, invr[0])
    for c in sm_copies:
        c.wait_send()
        c.wait_recv()
    smp[7:8, :] = sm_l[7:8, :]
    smp[72:73, :] = sm_r[0:1, :]
    far_l, far_r = spread(sm_l[7:8, :]), spread(sm_r[0:1, :])
    more_l = more_r = jnp.zeros((8, 128), F32)
    for k in range(3):
        p = pos[k, 0:8, :]
        more_l = more_l + jnp.where(p < 0, edge[k, 0:8, :] * take(far_l, p & 127), 0.0)
        p = pos[k, 56:64, :]
        more_r = more_r + jnp.where(p > 127, edge[k, 56:64, :] * take(far_r, p & 127), 0.0)
    sums = dot(spot(more_l[0:1], fown[0:1, :]), hot[:, 0:128], NT)
    sums = sums + dot(spot(more_r[7:8], fown[63:64, :]), hot[:, 8064:8192], NT)
    more = sums[0:8] + sums[8:16]
    inv_copies[0].wait_recv()
    halves(32, invr[1])
    for c in cs_copies:
        c.wait_recv()
    cs[1:3, :] = cs_l[6:8, :] + cs[1:3, :]
    cs[3:11, :] = cs[3:11, :] + more
    cs[11:13, :] = cs_r[0:2, :] + cs[11:13, :]
    cf[0:16, :] = RELAX * cs[0:16, :] / e_d[0:16, :]

    everyone = pltpu.make_async_remote_copy(
        src_ref=gb.at[pl.ds(0, n - 1)],
        dst_ref=gb.at[pl.ds(0, n - 1)],
        send_sem=ag_ss,
        recv_sem=ag_rs,
        device_id=(g, right),
        device_id_type=MESH,
    )
    everyone.wait_recv()
    from_right = (row8 == 0) & (lane8 >= 112)
    from_left = (row8 == 7) & (lane8 < 16)
    groups = [gb[8 * j : 8 * j + 8, 0, :] for j in range(8)]
    flat = []
    for j in range(8):
        mix = jnp.where(
            from_right, groups[(j + 1) % 8], jnp.where(from_left, groups[(j - 1) % 8], groups[j])
        )
        flat.append(jnp.sum(mix, axis=0, keepdims=True))
    flat = spread_all(jnp.concatenate(flat, axis=1))
    packed = jnp.concatenate(list(split_f32(flat)), axis=0).astype(BF16)
    found = dot(packed, invc[...], NT)
    value = found[0:1] + found[8:9]
    value = value + pltpu.roll(spread(value), 128 - 48, 1)[0:1]
    value = spread(value, 16)
    shift = jnp.where(row16 < 3, 16, jnp.where(row16 < 11, 0, 32))
    cs2[0:16, :] = cf[0:16, :] + take(value, jnp.minimum(e_o[0:16, :].astype(I32), 15) + shift)
    cur = cs2[1:17, :]
    whole = e_d[1:17, :]
    t3[...] = cur + RELAX * (cs[1:17, :] - (whole * cur - coarse_neighbours(cs2))) / whole

    for r in range(8):
        at = slice(8 * r, 8 * r + 8)
        owner = fown[at, :]
        high, lane = owner >> 7, owner & 127
        out = smp[8 + 8 * r : 16 + 8 * r, :]
        for h in range(8):
            out = out + jnp.where(high == h, take(spread(t3[2 + h : 3 + h, :]), lane), 0.0)
        cop[8 + 8 * r : 16 + 8 * r, :] = out
    own_l = spread(hr[0, 9:10, :]).astype(I32) & 127
    own_r = spread(hr[1, 9:10, :]).astype(I32) & 127
    cop[7:8, :] = smp[7:8, :] + take(spread(t3[1:2, :]), own_l)[0:1]
    cop[72:73, :] = smp[72:73, :] + take(spread(t3[10:11, :]), own_r)[0:1]
    for r in range(8):
        at = slice(8 * r, 8 * r + 8)
        cur = cop[8 + 8 * r : 16 + 8 * r, :]
        whole = totals(r)
        beside = neighbours(cop, r, 8 + 8 * r)
        height[at, :] = cur + RELAX * (base[at, :] - (whole * cur - beside)) / whole

    for c in halo_copies + surf_copies + inv_copies + cs_copies:
        c.wait_send()
    everyone.wait_send()

    @pl.when(seat == 0)
    def _():
        halo_on.wait_send()
        surf_on[0].wait_send()

    @pl.when(seat < 2)
    def _():
        surf_on[1].wait_send()


def write_out(a, b, c, a_out, b_out, c_out, sems):
    copies = [
        pltpu.make_async_copy(source, target, sems.at[i])
        for i, (source, target) in enumerate(((a, a_out), (b, b_out), (c, c_out)))
    ]
    for copy in copies:
        copy.start()
    for copy in copies:
        copy.wait()


def split_f32(x):
    high = x.astype(BF16).astype(F32)
    return high, x - high


def spread_all(row):
    return jnp.broadcast_to(row, (8, row.shape[1]))


def per_device(
    fields, level_rate, edge_weight, fine_diagonal, fine_table, old_height, level_weight,
    flux_weight, fine_owner, coarse_table, coarse_edge, coarse_diagonal, coarse_owner,
    coarse_inverse, surface_out, send_blocks, entry_slot, entry_block, remap_tiles,
):
    operands = (
        fields.reshape(8, 64, 128).transpose(1, 0, 2),
        level_rate,
        edge_weight.reshape(3, 64, 128),
        fine_diagonal.reshape(64, 128),
        fine_table.reshape(3, 64, 128),
        old_height.reshape(64, 128),
        level_weight,
        flux_weight,
        fine_owner.reshape(64, 128),
        coarse_table.reshape(3, 8, 128),
        coarse_edge.reshape(3, 8, 128),
        coarse_diagonal.reshape(8, 128),
        coarse_owner.reshape(8, 128),
        coarse_inverse.reshape(16, 1024),
        surface_out.reshape(4, 64, 128).transpose(1, 0, 2),
        send_blocks.reshape(1, 160),
        entry_slot.reshape(1, 160),
        entry_block.reshape(1, 160),
        remap_tiles.reshape(160, 128, 128),
    )
    vmem = pl.BlockSpec(memory_space=pltpu.VMEM)
    specs = [pl.BlockSpec(memory_space=pltpu.HBM)] * 19
    V = pltpu.VMEM
    local = [
        (pltpu.SMEM if i in (1, 6, 7, 15, 16) else V)(x.shape, x.dtype)
        for i, x in enumerate(operands)
    ]
    D = pltpu.SemaphoreType.DMA
    new, got, high = pl.pallas_call(
        kernel,
        out_shape=(
            jax.ShapeDtypeStruct((64, 8, 128), F32),
            jax.ShapeDtypeStruct((256, 128), F32),
            jax.ShapeDtypeStruct((64, 128), F32),
        ),
        in_specs=specs,
        out_specs=(vmem, vmem, vmem),
        scratch_shapes=[
            *local,
            V((160, 4, 128), BF16),
            V((160, 4, 128), BF16),
            V((2, 32, 128), F32),
            V((2, 32, 128), F32),
            V((2, 16, 1024), F32),
            V((8, 128), F32),
            V((8, 128), F32),
            V((8, 128), F32),
            V((8, 128), F32),
            V((1, 1, 128), F32),
            V((8, 128), F32),
            V((64, 1, 128), F32),
            V((64, 160), BF16),
            V((640, 128), F32),
            V((640, 128), F32),
            V((128, 8192), BF16),
            V((16, 8192), BF16),
            V((2, 16, 128), F32),
            V((80, 128), F32),
            V((80, 128), F32),
            V((80, 128), F32),
            V((64, 128), F32),
            V((3, 64, 128), I32),
            V((3, 16, 128), F32),
            V((3, 16, 128), F32),
            V((24, 128), F32),
            V((24, 128), F32),
            V((16, 128), I32),
            V((24, 128), F32),
            V((24, 128), F32),
            V((24, 128), F32),
            V((16, 128), F32),
            V((128, 1536), BF16),
            V((8, 1536), F32),
            V((2, 128, 128), BF16),
            V((3, 64, 128), F32),
            V((128, 1024), BF16),
            V((2, 32, 4, 128), BF16),
            V((32, 128), F32),
            D((18,)),
            D((4,)),
            D((5,)), D((5,)),
            D((2,)), D((2,)),
            D((2,)), D((2,)),
            D((2,)), D((2,)),
            D((2,)), D((2,)),
            D, D,
            pltpu.SemaphoreType.REGULAR, pltpu.SemaphoreType.REGULAR,
            D((2,)), D((2,)), D, D,
        ],
        compiler_params=pltpu.CompilerParams(
            collective_id=0, has_side_effects=True, vmem_limit_bytes=48 << 20
        ),
        name="step",
    )(*[pltpu.with_memory_space_constraint(x, pltpu.HBM) for x in operands])
    new, got, high = pl.pallas_call(
        write_out,
        out_shape=tuple(jax.ShapeDtypeStruct(v.shape, v.dtype) for v in (new, got, high)),
        in_specs=[vmem] * 3,
        out_specs=[pl.BlockSpec(memory_space=pltpu.HBM)] * 3,
        scratch_shapes=[D((3,))],
        compiler_params=pltpu.CompilerParams(vmem_limit_bytes=1 << 20),
        name="write_out",
    )(new, got, high)
    return (
        new.transpose(1, 0, 2).reshape(1, 8, 8192),
        got.reshape(64, 4, 128).transpose(1, 0, 2).reshape(1, 4, 8192),
        high.reshape(1, 8192),
    )


def solution(mesh):
    in_specs = (
        P("comp", None, "tile"),
        P("comp", None),
        P("comp", None, "tile"),
        P("comp", "tile"),
        P("comp", None, "tile"),
        P("comp", "tile"),
        P("comp", None),
        P("comp", None),
        P("comp", "tile"),
        P("comp", None, "tile"),
        P("comp", None, "tile"),
        P("comp", "tile"),
        P("comp", "tile"),
        P("comp", "tile", None),
        P("comp", None, "tile"),
        P("comp", "tile", None),
        P("comp", "tile", None),
        P("comp", "tile", None),
        P("comp", "tile", None, None, None),
    )
    out_specs = (P("comp", None, "tile"), P("comp", None, "tile"), P("comp", "tile"))
    return jax.shard_map(
        per_device, mesh=mesh, in_specs=in_specs, out_specs=out_specs, check_vma=False
    )
```

```python
import functools

import jax
import jax.numpy as jnp
from jax import lax
from jax.experimental import pallas as pl
from jax.experimental.pallas import tpu as pltpu
from jax.sharding import PartitionSpec as P

MESH = pl.DeviceIdType.MESH
F32, BF16, I32 = jnp.float32, jnp.bfloat16, jnp.int32
RELAX = 0.8
NT = (((1,), (1,)), ((), ()))
NN = (((1,), (0,)), ((), ()))


def take(x, lane):
    return jnp.take_along_axis(x, lane, axis=1, mode="promise_in_bounds")


def pick(prev, cur, nxt, pos):
    lane = pos & 127
    return jnp.where(
        pos < 0, take(prev, lane), jnp.where(pos > 127, take(nxt, lane), take(cur, lane))
    )


def spread(row, count=8):
    return jnp.broadcast_to(row, (count, 128))


def iota(shape, dim):
    return lax.broadcasted_iota(I32, shape, dim)


def split(x):
    high = x.astype(BF16)
    return high, (x - high.astype(F32)).astype(BF16)


def dot(a, b, dims):
    return lax.dot_general(a, b, dims, preferred_element_type=F32)


def kernel(
    *refs,
):
    inputs, outputs, rest = refs[:19], refs[19:28], refs[28:]
    local, scratch = list(rest[:16]), rest[16:]
    for i, ref in zip((2, 3, 8), outputs[6:]):
        local.insert(i, ref)
    step(*local, *outputs[:6], inputs, local, *scratch)


def step(
    fields, rate_s, edge, fdiag, ftab, oldh, lw_s, fw_s, fown, ctab, cedge, cdiag, cown,
    cinv, surf, sendb, eslot, eblk, tl,
    newf, recv, smp, t3, base, pos, inputs, local,
    outg, inc, hs, hr, invr, sm_l, sm_r, cs_l, cs_r, pay, cs_s, gb, member, picks, prod,
    hot, lhs, seg, oldp, etab, eedge, e_d, e_o, key, cs, cf, cs2, khot, klhs, hot_n, shares,
    inv_h, inv_l, segk, rl, rh,
    in_sem, tile_sem, surf_ss, surf_rs, halo_ss, halo_rs, inv_ss, inv_rs, sm_ss, sm_rs, cs_ss, cs_rs,
    ag_ss, ag_rs, plane_sem, space_sem, rl_ss, rl_rs, rh_ss, rh_rs,
):
    g = lax.axis_index("comp")
    t = lax.axis_index("tile")
    n = lax.axis_size("tile")
    left, right = lax.rem(t + n - 1, n), lax.rem(t + 1, n)
    seat, back = lax.rem(t, 16), lax.rem(t + n - 16, n)
    y, z, x = lax.rem(t, 4), lax.rem(lax.div(t, 4), 4), lax.div(t, 16)
    ys = [lax.rem(y + d, 4) for d in range(4)]
    zs = [4 * lax.rem(z + d, 4) for d in range(4)]
    xs = [16 * lax.rem(x + d, 4) for d in range(4)]
    ring_y = [xs[0] + zs[0] + ys[d] for d in (1, 2, 3)]
    ring_z = [xs[0] + zs[d] + ys[0] for d in (1, 2, 3)]
    ring_x = [xs[d] + zs[0] + ys[0] for d in (1, 2, 3)]
    bar = pltpu.get_barrier_semaphore()

    def signal(sem, group, tile):
        pl.semaphore_signal(sem, inc=1, device_id=(group, tile), device_id_type=MESH)

    loads = [
        pltpu.make_async_copy(inputs[i], local[i], in_sem.at[i]) for i in range(18)
    ]
    for i in (15, 14, 0, 5, 8, 9, 10, 11, 12, 4, 2, 1, 6, 7, 17, 3, 16, 13):
        loads[i].start()
    def greet(ok, group, tile):
        if ok is None:
            signal(bar, group, tile)
        else:
            pl.when(ok)(functools.partial(signal, bar, group, tile))

    for d, ok in ((-2, seat < 14), (2, None), (-1, seat < 15), (1, None)):
        greet(ok, 1 - g, lax.rem(t + n - d, n))
    greet(None, g, left)
    greet(seat < 15, g, right)
    greet(seat < 2, 1 - g, lax.rem(t + 16, n))
    for tile in (*ring_y, *ring_z, *ring_x):
        signal(bar, g, tile)
    signal(bar, 1 - g, t)

    tiles = inputs[18]
    chunks = 4
    per = 160 // chunks
    tile_copies = [
        pltpu.make_async_copy(
            tiles.at[pl.ds(c * per, per)], tl.at[pl.ds(c * per, per)], tile_sem.at[c]
        )
        for c in range(chunks)
    ]
    for c in tile_copies:
        c.start()

    def ready(*which):
        for i in which:
            loads[i].wait()

    ready(15, 14)

    def gather(i, carry):
        for a in range(8):
            s = i * 8 + a
            outg[s] = surf[jnp.minimum(sendb[0, s], 63)]
        return carry

    lax.fori_loop(0, 20, gather, 0)

    ready(0, 5, 8, 9, 10, 11, 12, 4, 2)
    row8 = iota((8, 128), 0)
    cpos = [ctab[k] - 16 - 128 * row8 for k in range(3)]
    csum = cedge[0] + cedge[1] + cedge[2]
    c_d = cdiag[...] + csum
    for k in range(3):
        etab[k, 2:10, :] = cpos[k].astype(F32)
        etab[k, 12:16, :] = jnp.zeros((4, 128), F32)
        eedge[k, 2:10, :] = cedge[k]
        eedge[k, 12:16, :] = jnp.zeros((4, 128), F32)
    e_d[...] = jnp.ones((24, 128), F32)
    e_d[3:11, :] = c_d
    e_o[...] = jnp.zeros((24, 128), F32)
    e_o[3:11, :] = cown[...].astype(F32)
    for side, block, low in ((0, 0, 0), (1, 63, 6)):
        hs[side, 0:8, :] = fields[block]
        hs[side, 8:9, :] = oldh[block : block + 1, :]
        hs[side, 9:10, :] = fown[block : block + 1, :].astype(F32)
        for k in range(3):
            here = ftab[k, block : block + 1, :] - (128 + 128 * block)
            hs[side, 10 + k : 11 + k, :] = here.astype(F32)
            hs[side, 13 + k : 14 + k, :] = edge[k, block : block + 1, :]
        for k in range(3):
            hs[side, 16 + 2 * k : 18 + 2 * k, :] = etab[k, 2 + low : 4 + low, :]
            hs[side, 22 + 2 * k : 24 + 2 * k, :] = cedge[k, low : low + 2, :]
        hs[side, 28:30, :] = e_d[3 + low : 5 + low, :]
        hs[side, 30:32, :] = e_o[3 + low : 5 + low, :]

    pl.semaphore_wait(bar, jnp.where(seat == 0, 14, 16))

    surf_copies = [
        pltpu.make_async_remote_copy(
            src_ref=outg.at[pl.ds(32 * j, 32)],
            dst_ref=inc.at[pl.ds(32 * j, 32)],
            send_sem=surf_ss.at[j],
            recv_sem=surf_rs.at[j],
            device_id=(1 - g, lax.rem(t + n + 2 - j, n)),
            device_id_type=MESH,
        )
        for j in range(5)
    ]

    def pair(to_left, at_right, to_right, at_left, ss, rs):
        return [
            pltpu.make_async_remote_copy(
                src_ref=to_left, dst_ref=at_right, send_sem=ss.at[0], recv_sem=rs.at[0],
                device_id=(g, left), device_id_type=MESH,
            ),
            pltpu.make_async_remote_copy(
                src_ref=to_right, dst_ref=at_left, send_sem=ss.at[1], recv_sem=rs.at[1],
                device_id=(g, right), device_id_type=MESH,
            ),
        ]

    halo_copies = pair(hs.at[0], hr.at[1], hs.at[1], hr.at[0], halo_ss, halo_rs)
    inv_copies = pair(inputs[13], invr.at[1], inputs[13], invr.at[0], inv_ss, inv_rs)
    def relayed(source, landing, ss, rs, group):
        return pltpu.make_async_remote_copy(
            src_ref=source, dst_ref=landing, send_sem=ss, recv_sem=rs,
            device_id=(group, back), device_id_type=MESH,
        )

    def handed(source, landing, ss, rs, ahead):
        return pltpu.make_async_remote_copy(
            src_ref=source, dst_ref=landing, send_sem=ss, recv_sem=rs,
            device_id=(g, lax.rem(t + ahead, n)), device_id_type=MESH,
        )

    surf_in = [
        relayed(
            outg.at[pl.ds(32 * j, 32)], rl.at[j - 3], surf_ss.at[j], rl_rs.at[j - 3], 1 - g
        )
        for j in (3, 4)
    ]
    surf_on = [
        handed(
            rl.at[j - 3], inc.at[pl.ds(32 * j, 32)], rl_ss.at[j - 3], surf_rs.at[j], 18 - j
        )
        for j in (3, 4)
    ]
    halo_in = relayed(hs.at[0], rh, halo_ss.at[0], rh_rs, g)
    halo_on = handed(rh, hr.at[1], rh_ss, halo_rs.at[0], 15)

    def either(ok, direct, other):
        pl.when(ok)(direct.start)
        pl.when(jnp.logical_not(ok))(other.start)

    either(seat >= 1, halo_copies[0], halo_in)
    halo_copies[1].start()
    either(seat >= 2, surf_copies[4], surf_in[1])
    surf_copies[0].start()
    either(seat >= 1, surf_copies[3], surf_in[0])
    surf_copies[1].start()
    surf_copies[2].start()
    for tile in ring_z:
        signal(plane_sem, g, tile)

    ready(1, 6, 7, 17, 3, 16, 13)
    def positions(i, carry):
        at = pl.ds(pl.multiple_of(i * 8, 8), 8)
        total = edge[0, at, :] + edge[1, at, :] + edge[2, at, :]
        share = 1.0 / total
        for k in range(3):
            pos[k, at, :] = ftab[k, at, :] - 128 - 128 * (i * 8 + row8)
            shares[k, at, :] = edge[k, at, :] * share
        return carry

    lax.fori_loop(0, 8, positions, 0)

    def column(ref, count):
        out = jnp.zeros((8, 128), F32)
        for level in range(count):
            out = jnp.where(row8 == level, ref[0, level], out)
        return out

    rates, weights = column(rate_s, 8), column(lw_s, 8)

    def advance(j, prev, cur, nxt):
        beside = None
        for k in range(3):
            p = spread(pos[k, pl.ds(j, 1), :])
            w = spread(shares[k, pl.ds(j, 1), :])
            term = w * pick(prev, cur, nxt, p)
            beside = term if beside is None else beside + term
        new = cur + rates * (beside - cur)
        newf[j] = new
        base[pl.ds(j, 1), :] = jnp.sum(weights * new, axis=0, keepdims=True)

    def advance8(i, carry):
        for a in range(8):
            j = i * 8 + a
            advance(j, fields[j - 1], fields[j], fields[j + 1])
        return carry

    lax.fori_loop(1, 7, advance8, 0)
    for j in (*range(1, 8), *range(56, 63)):
        advance(j, fields[j - 1], fields[j], fields[j + 1])

    lane8 = iota((8, 128), 1)
    blocks = iota((64, 160), 0)
    member[...] = jnp.where(
        blocks == jnp.broadcast_to(eblk[...], (64, 160)), 1.0, 0.0
    ).astype(BF16)

    down = iota((128, 128), 0)

    def one_hot(i, carry):
        for a in range(4):
            r = i * 4 + a
            row = fown[pl.ds(r, 1), :] & 127
            at = pl.ds(pl.multiple_of(r * 128, 128), 128)
            hot[:, at] = jnp.where(down == spread(row, 128), 1.0, 0.0).astype(BF16)
        return carry

    lax.fori_loop(0, 16, one_hot, 0)
    pl.semaphore_wait(plane_sem, 3)
    for tile in ring_x:
        signal(space_sem, g, tile)

    @pl.when(seat == 0)
    def _():
        halo_in.wait_recv()
        halo_on.start()
        surf_in[0].wait_recv()
        surf_on[0].start()

    @pl.when(seat < 2)
    def _():
        surf_in[1].wait_recv()
        surf_on[1].start()

    inv_copies[1].start()
    for c in halo_copies:
        c.wait_recv()
    advance(0, hr[0, 0:8, :], fields[0], fields[1])
    advance(63, fields[62], fields[63], hr[1, 0:8, :])
    oldp[7:8, :] = hr[0, 8:9, :]
    oldp[8:72, :] = oldh[...]
    oldp[72:73, :] = hr[1, 8:9, :]
    def neighbours(ref, r, _):
        return beside_rows(ref, edge, pos, r)

    def totals(r):
        at = slice(8 * r, 8 * r + 8)
        return fdiag[at, :] + (edge[0, at, :] + edge[1, at, :] + edge[2, at, :])

    for r in range(8):
        at = slice(8 * r, 8 * r + 8)
        smp[8 + 8 * r : 16 + 8 * r, :] = neighbours(oldp, r, 8 + 8 * r)

    row16 = iota((16, 128), 0)
    def halves(at, block):
        inv_h[at : at + 16, :], inv_l[at : at + 16, :] = split(block)

    halves(0, cinv[...])
    for k in range(3):
        etab[k, 0:2, :] = hr[0, 16 + 2 * k : 18 + 2 * k, :]
        etab[k, 10:12, :] = hr[1, 16 + 2 * k : 18 + 2 * k, :]
        eedge[k, 0:2, :] = hr[0, 22 + 2 * k : 24 + 2 * k, :]
        eedge[k, 10:12, :] = hr[1, 22 + 2 * k : 24 + 2 * k, :]
    e_d[1:3, :] = hr[0, 28:30, :]
    e_d[11:13, :] = hr[1, 28:30, :]
    e_o[1:3, :] = hr[0, 30:32, :]
    e_o[11:13, :] = hr[1, 30:32, :]
    side = jnp.where(row16 < 2, 7, jnp.where(row16 >= 10, 1, 0))
    key[...] = ((t + side) & 7) * 16 + e_o[1:17, :].astype(I32)
    for r in range(12):
        khot[:, 128 * r : 128 * r + 128] = jnp.where(
            down == spread(key[r : r + 1, :], 128), 1.0, 0.0
        ).astype(BF16)
    for i in range(2):
        owner = spread(hr[i, 9:10, :], 128).astype(I32) & 127
        hot_n[i] = jnp.where(down == owner, 1.0, 0.0).astype(BF16)
    for c in surf_copies:
        c.wait_recv()
    for c in tile_copies:
        c.wait()

    quarter = row16 // 4
    for i in range(40):
        at = slice(16 * i, 16 * i + 16)
        for e in range(4 * i, 4 * i + 4):
            picks[4 * e : 4 * e + 4, :] = inc[eslot[0, e]].astype(F32)
        rows = picks[at, :]
        ab = jnp.where(quarter < 2, rows, 0.0).astype(BF16)
        cd = jnp.where(quarter < 2, 0.0, rows).astype(BF16)
        four = tl[4 * i : 4 * i + 4]
        out = dot(
            jnp.concatenate([ab, cd], axis=1),
            jnp.concatenate(
                [four[0:2].reshape(256, 128), four[2:4].reshape(256, 128)], axis=1
            ),
            NT,
        )
        prod[at, :] = jnp.where(quarter % 2 == 0, out[:, 0:128], out[:, 128:256])

    for f in range(4):
        high, low = split(prod[pl.ds(f, 160, stride=4), :])
        both = dot(member[...], jnp.concatenate([high, low], axis=1), NN)
        recv[pl.ds(f, 64, stride=4), :] = both[:, 0:128] + both[:, 128:256]

    for r in range(8):
        at = slice(8 * r, 8 * r + 8)
        out = base[at, :]
        for f in range(4):
            out = out + fw_s[0, f] * recv[pl.ds(32 * r + f, 8, stride=4), :]
        base[at, :] = out
        prev = oldh[at, :]
        whole = totals(r)
        smp[8 + 8 * r : 16 + 8 * r, :] = (
            prev + RELAX * (out - (whole * prev - smp[8 + 8 * r : 16 + 8 * r, :])) / whole
        )

    pl.semaphore_wait(space_sem, 3)
    sm_copies = pair(smp.at[pl.ds(8, 8)], sm_r, smp.at[pl.ds(64, 8)], sm_l, sm_ss, sm_rs)
    for c in sm_copies:
        c.start()
    inv_copies[0].start()
    smp[7:8, :] = jnp.zeros((1, 128), F32)
    smp[72:73, :] = jnp.zeros((1, 128), F32)

    def spot(row, owner):
        mine = jnp.where(spread(owner >> 7) == row8, spread(row), 0.0)
        return jnp.concatenate(list(split_f32(mine)), axis=0).astype(BF16)

    for r in range(8):
        at = slice(8 * r, 8 * r + 8)
        cur = smp[8 + 8 * r : 16 + 8 * r, :]
        res = base[at, :] - (totals(r) * cur - neighbours(smp, r, 8 + 8 * r))
        for a in range(8):
            where = slice(128 * (8 * r + a), 128 * (8 * r + a) + 128)
            lhs[:, where] = spot(res[a : a + 1], fown[8 * r + a : 8 * r + a + 1, :])
    def from_here(i, row, towards):
        row = spread(row)
        out = jnp.zeros((8, 128), F32)
        for k in range(3):
            p = spread(hr[i, 10 + k : 11 + k, :]).astype(I32)
            term = spread(hr[i, 13 + k : 14 + k, :]) * take(row, p & 127)
            out = out + jnp.where(towards(p), term, 0.0)
        both = dot(jnp.concatenate(list(split_f32(out)), axis=0).astype(BF16), hot_n[i], NT)
        return both[0:1] + both[8:9]

    extra_l = from_here(0, smp[8:9, :], lambda p: p > 127)
    extra_r = from_here(1, smp[71:72, :], lambda p: p < 0)
    for r in range(2):
        where = slice(4096 * r, 4096 * r + 4096)
        seg[r] = dot(lhs[:, where], hot[:, where], NT)
    source = (seg[0, 0:8] + seg[0, 8:16]) + (seg[1, 0:8] + seg[1, 8:16])
    cs_s[...] = source
    cs_copies = pair(cs_s, cs_r, cs_s, cs_l, cs_ss, cs_rs)
    for c in cs_copies:
        c.start()

    cs[...] = jnp.zeros((24, 128), F32)
    cs[2:3, :] = extra_l
    cs[3:11, :] = source
    cs[11:12, :] = extra_r
    cf[...] = jnp.zeros((24, 128), F32)
    cs2[...] = jnp.zeros((24, 128), F32)
    cf[0:16, :] = RELAX * cs[0:16, :] / e_d[0:16, :]

    def coarse_neighbours(ref):
        out = None
        for k in range(3):
            term = eedge[k] * pick(
                ref[0:16, :], ref[1:17, :], ref[2:18, :], etab[k].astype(I32)
            )
            out = term if out is None else out + term
        return out

    left_over = cs[1:17, :] - e_d[1:17, :] * cf[1:17, :] + coarse_neighbours(cf)
    klhs[...] = jnp.zeros((8, 1536), F32)
    for r in range(12):
        klhs[0:1, 128 * r : 128 * r + 128] = left_over[r : r + 1]
    packed = jnp.concatenate(list(split_f32(klhs[...])), axis=0).astype(BF16)
    for r in range(2):
        where = slice(768 * r, 768 * r + 768)
        segk[r] = dot(packed[:, where], khot[:, where], NT)
    pay[0] = (segk[0, 0:1] + segk[0, 8:9]) + (segk[1, 0:1] + segk[1, 8:9])
    gb[t] = pay[0]

    hops = (0, 1, 2, 1)
    others = sorted(
        ((a, b, c) for a in range(4) for b in range(4) for c in range(4)),
        key=lambda d: -(hops[d[0]] + hops[d[1]] + hops[d[2]]),
    )[:-1]
    for a, b, c in others:
        pltpu.make_async_remote_copy(
            src_ref=pay,
            dst_ref=gb.at[pl.ds(t, 1)],
            send_sem=ag_ss,
            recv_sem=ag_rs,
            device_id=(g, xs[a] + zs[b] + ys[c]),
            device_id_type=MESH,
        ).start()

    inv_copies[1].wait_recv()
    halves(16, invr[0])
    for c in sm_copies:
        c.wait_send()
        c.wait_recv()
    smp[7:8, :] = sm_l[7:8, :]
    smp[72:73, :] = sm_r[0:1, :]
    far_l, far_r = spread(sm_l[7:8, :]), spread(sm_r[0:1, :])
    more_l = more_r = jnp.zeros((8, 128), F32)
    for k in range(3):
        p = pos[k, 0:8, :]
        more_l = more_l + jnp.where(p < 0, edge[k, 0:8, :] * take(far_l, p & 127), 0.0)
        p = pos[k, 56:64, :]
        more_r = more_r + jnp.where(p > 127, edge[k, 56:64, :] * take(far_r, p & 127), 0.0)
    sums = dot(spot(more_l[0:1], fown[0:1, :]), hot[:, 0:128], NT)
    sums = sums + dot(spot(more_r[7:8], fown[63:64, :]), hot[:, 8064:8192], NT)
    more = sums[0:8] + sums[8:16]
    inv_copies[0].wait_recv()
    halves(32, invr[1])
    for c in cs_copies:
        c.wait_recv()
    cs[1:3, :] = cs_l[6:8, :] + cs[1:3, :]
    cs[3:11, :] = cs[3:11, :] + more
    cs[11:13, :] = cs_r[0:2, :] + cs[11:13, :]
    cf[0:16, :] = RELAX * cs[0:16, :] / e_d[0:16, :]

    everyone = pltpu.make_async_remote_copy(
        src_ref=gb.at[pl.ds(0, n - 1)],
        dst_ref=gb.at[pl.ds(0, n - 1)],
        send_sem=ag_ss,
        recv_sem=ag_rs,
        device_id=(g, right),
        device_id_type=MESH,
    )
    everyone.wait_recv()
    from_right = (row8 == 0) & (lane8 >= 112)
    from_left = (row8 == 7) & (lane8 < 16)
    groups = [gb[8 * j : 8 * j + 8, 0, :] for j in range(8)]
    flat = []
    for j in range(8):
        mix = jnp.where(
            from_right, groups[(j + 1) % 8], jnp.where(from_left, groups[(j - 1) % 8], groups[j])
        )
        flat.append(jnp.sum(mix, axis=0, keepdims=True))
    flat = spread_all(jnp.concatenate(flat, axis=1))
    packed = jnp.concatenate(list(split_f32(flat)), axis=0).astype(BF16)
    by_h, by_l = dot(packed, inv_h[...], NT), dot(packed, inv_l[...], NT)
    value = (by_h[0:1] + by_h[8:9]) + (by_l[0:1] + by_l[8:9])
    value = jnp.concatenate([value, jnp.zeros((1, 80), F32)], axis=1)
    value = spread(value, 16)
    shift = jnp.where(row16 < 3, 16, jnp.where(row16 < 11, 0, 32))
    cs2[0:16, :] = cf[0:16, :] + take(value, jnp.minimum(e_o[0:16, :].astype(I32), 15) + shift)
    cur = cs2[1:17, :]
    whole = e_d[1:17, :]
    t3[...] = cur + RELAX * (cs[1:17, :] - (whole * cur - coarse_neighbours(cs2))) / whole

    own_l = spread(hr[0, 9:10, :]).astype(I32) & 127
    own_r = spread(hr[1, 9:10, :]).astype(I32) & 127
    smp[7:8, :] = smp[7:8, :] + take(spread(t3[1:2, :]), own_l)[0:1]
    smp[72:73, :] = smp[72:73, :] + take(spread(t3[10:11, :]), own_r)[0:1]

    for c in halo_copies + surf_copies + inv_copies + cs_copies:
        c.wait_send()
    everyone.wait_send()

    @pl.when(seat == 0)
    def _():
        halo_on.wait_send()
        surf_on[0].wait_send()

    @pl.when(seat < 2)
    def _():
        surf_on[1].wait_send()


def finish(
    newf, recv, smp, t3, base, pos, edge, fdiag, fown, new_out, recv_out, height_out,
    cop, height, sems,
):
    copies = [
        pltpu.make_async_copy(source, target, sems.at[i])
        for i, (source, target) in enumerate(
            ((newf, new_out), (recv, recv_out), (height, height_out))
        )
    ]
    copies[0].start()
    copies[1].start()
    for r in range(8):
        at = slice(8 * r, 8 * r + 8)
        owner = fown[at, :]
        high, lane = owner >> 7, owner & 127
        out = smp[8 + 8 * r : 16 + 8 * r, :]
        for a in range(8):
            out = out + jnp.where(high == a, take(spread(t3[2 + a : 3 + a, :]), lane), 0.0)
        cop[8 + 8 * r : 16 + 8 * r, :] = out
    cop[7:8, :] = smp[7:8, :]
    cop[72:73, :] = smp[72:73, :]
    for r in range(8):
        at = slice(8 * r, 8 * r + 8)
        cur = cop[8 + 8 * r : 16 + 8 * r, :]
        whole = fdiag[at, :] + (edge[0, at, :] + edge[1, at, :] + edge[2, at, :])
        beside = beside_rows(cop, edge, pos, r)
        height[at, :] = cur + RELAX * (base[at, :] - (whole * cur - beside)) / whole
    copies[2].start()
    for copy in copies:
        copy.wait()


def beside_rows(ref, edge, pos, r):
    out = None
    row = 8 + 8 * r
    prev, cur, nxt = ref[row - 1 : row + 7, :], ref[row : row + 8, :], ref[row + 1 : row + 9, :]
    for k in range(3):
        at = slice(8 * r, 8 * r + 8)
        term = edge[k, at, :] * pick(prev, cur, nxt, pos[k, at, :])
        out = term if out is None else out + term
    return out


def split_f32(x):
    high = x.astype(BF16).astype(F32)
    return high, x - high


def spread_all(row):
    return jnp.broadcast_to(row, (8, row.shape[1]))


def per_device(
    fields, level_rate, edge_weight, fine_diagonal, fine_table, old_height, level_weight,
    flux_weight, fine_owner, coarse_table, coarse_edge, coarse_diagonal, coarse_owner,
    coarse_inverse, surface_out, send_blocks, entry_slot, entry_block, remap_tiles,
):
    operands = (
        fields.reshape(8, 64, 128).transpose(1, 0, 2),
        level_rate,
        edge_weight.reshape(3, 64, 128),
        fine_diagonal.reshape(64, 128),
        fine_table.reshape(3, 64, 128),
        old_height.reshape(64, 128),
        level_weight,
        flux_weight,
        fine_owner.reshape(64, 128),
        coarse_table.reshape(3, 8, 128),
        coarse_edge.reshape(3, 8, 128),
        coarse_diagonal.reshape(8, 128),
        coarse_owner.reshape(8, 128),
        coarse_inverse.reshape(16, 1024),
        surface_out.reshape(4, 64, 128).transpose(1, 0, 2),
        send_blocks.reshape(1, 160),
        entry_slot.reshape(1, 160),
        entry_block.reshape(1, 160),
        remap_tiles.reshape(160, 128, 128),
    )
    vmem = pl.BlockSpec(memory_space=pltpu.VMEM)
    specs = [pl.BlockSpec(memory_space=pltpu.HBM)] * 19
    V = pltpu.VMEM
    local = [
        (pltpu.SMEM if i in (1, 6, 7, 15, 16) else V)(x.shape, x.dtype)
        for i, x in enumerate(operands)
        if i not in (2, 3, 8)
    ]
    shape = jax.ShapeDtypeStruct
    D = pltpu.SemaphoreType.DMA
    made = pl.pallas_call(
        kernel,
        out_shape=(
            shape((64, 8, 128), F32),
            shape((256, 128), F32),
            shape((80, 128), F32),
            shape((16, 128), F32),
            shape((64, 128), F32),
            shape((3, 64, 128), I32),
            shape((3, 64, 128), F32),
            shape((64, 128), F32),
            shape((64, 128), I32),
        ),
        in_specs=specs,
        out_specs=(vmem,) * 9,
        scratch_shapes=[
            *local,
            V((160, 4, 128), BF16),
            V((160, 4, 128), BF16),
            V((2, 32, 128), F32),
            V((2, 32, 128), F32),
            V((2, 16, 1024), F32),
            V((8, 128), F32),
            V((8, 128), F32),
            V((8, 128), F32),
            V((8, 128), F32),
            V((1, 1, 128), F32),
            V((8, 128), F32),
            V((64, 1, 128), F32),
            V((64, 160), BF16),
            V((640, 128), F32),
            V((640, 128), F32),
            V((128, 8192), BF16),
            V((16, 8192), BF16),
            V((2, 16, 128), F32),
            V((80, 128), F32),
            V((3, 16, 128), F32),
            V((3, 16, 128), F32),
            V((24, 128), F32),
            V((24, 128), F32),
            V((16, 128), I32),
            V((24, 128), F32),
            V((24, 128), F32),
            V((24, 128), F32),
            V((128, 1536), BF16),
            V((8, 1536), F32),
            V((2, 128, 128), BF16),
            V((3, 64, 128), F32),
            V((48, 1024), BF16),
            V((48, 1024), BF16),
            V((2, 16, 128), F32),
            V((2, 32, 4, 128), BF16),
            V((32, 128), F32),
            D((18,)),
            D((4,)),
            D((5,)), D((5,)),
            D((2,)), D((2,)),
            D((2,)), D((2,)),
            D((2,)), D((2,)),
            D((2,)), D((2,)),
            D, D,
            pltpu.SemaphoreType.REGULAR, pltpu.SemaphoreType.REGULAR,
            D((2,)), D((2,)), D, D,
        ],
        compiler_params=pltpu.CompilerParams(
            collective_id=0, has_side_effects=True, vmem_limit_bytes=48 << 20
        ),
        name="step",
    )(*[pltpu.with_memory_space_constraint(x, pltpu.HBM) for x in operands])
    new, got, high = pl.pallas_call(
        finish,
        out_shape=(shape((64, 8, 128), F32), shape((256, 128), F32), shape((64, 128), F32)),
        in_specs=[vmem] * 9,
        out_specs=[pl.BlockSpec(memory_space=pltpu.HBM)] * 3,
        scratch_shapes=[V((80, 128), F32), V((64, 128), F32), D((3,))],
        compiler_params=pltpu.CompilerParams(vmem_limit_bytes=1 << 20),
        name="finish",
    )(*made)
    return (
        new.transpose(1, 0, 2).reshape(1, 8, 8192),
        got.reshape(64, 4, 128).transpose(1, 0, 2).reshape(1, 4, 8192),
        high.reshape(1, 8192),
    )


def solution(mesh):
    in_specs = (
        P("comp", None, "tile"),
        P("comp", None),
        P("comp", None, "tile"),
        P("comp", "tile"),
        P("comp", None, "tile"),
        P("comp", "tile"),
        P("comp", None),
        P("comp", None),
        P("comp", "tile"),
        P("comp", None, "tile"),
        P("comp", None, "tile"),
        P("comp", "tile"),
        P("comp", "tile"),
        P("comp", "tile", None),
        P("comp", None, "tile"),
        P("comp", "tile", None),
        P("comp", "tile", None),
        P("comp", "tile", None),
        P("comp", "tile", None, None, None),
    )
    out_specs = (P("comp", None, "tile"), P("comp", None, "tile"), P("comp", "tile"))
    return jax.shard_map(
        per_device, mesh=mesh, in_specs=in_specs, out_specs=out_specs, check_vma=False
    )
```

```python
import functools

import jax
import jax.numpy as jnp
from jax import lax
from jax.experimental import pallas as pl
from jax.experimental.pallas import tpu as pltpu
from jax.sharding import PartitionSpec as P

MESH = pl.DeviceIdType.MESH
F32, BF16, I32 = jnp.float32, jnp.bfloat16, jnp.int32
RELAX = 0.8
NT = (((1,), (1,)), ((), ()))
NN = (((1,), (0,)), ((), ()))


def take(x, lane):
    return jnp.take_along_axis(x, lane, axis=1, mode="promise_in_bounds")


def pick(prev, cur, nxt, pos):
    lane = pos & 127
    return jnp.where(
        pos < 0, take(prev, lane), jnp.where(pos > 127, take(nxt, lane), take(cur, lane))
    )


def spread(row, count=8):
    return jnp.broadcast_to(row, (count, 128))


def iota(shape, dim):
    return lax.broadcasted_iota(I32, shape, dim)


def split(x):
    high = x.astype(BF16)
    return high, (x - high.astype(F32)).astype(BF16)


def dot(a, b, dims):
    return lax.dot_general(a, b, dims, preferred_element_type=F32)


def kernel(
    *refs,
):
    inputs, outputs, rest = refs[:19], refs[19:28], refs[28:]
    local, scratch = list(rest[:16]), rest[16:]
    for i, ref in zip((2, 3, 8), outputs[6:]):
        local.insert(i, ref)
    step(*local, *outputs[:6], inputs, local, *scratch)


def step(
    fields, rate_s, edge, fdiag, ftab, oldh, lw_s, fw_s, fown, ctab, cedge, cdiag, cown,
    cinv, surf, sendb, eslot, eblk, tl,
    newf, recv, smp, t3, base, pos, inputs, local,
    outg, inc, hs, hr, invr, sm_l, sm_r, cs_l, cs_r, pay, cs_s, gb, member, picks, prod,
    hot, upper, rests, lhs, seg, oldp, etab, eedge, e_d, e_o, key, cs, cf, cs2, khot, klhs, hot_n, shares,
    inv_h, inv_l, segk, rl, rh,
    in_sem, tile_sem, surf_ss, surf_rs, halo_ss, halo_rs, inv_ss, inv_rs, sm_ss, sm_rs, cs_ss, cs_rs,
    ag_ss, ag_rs, plane_sem, space_sem, rl_ss, rl_rs, rh_ss, rh_rs,
):
    g = lax.axis_index("comp")
    t = lax.axis_index("tile")
    n = lax.axis_size("tile")
    left, right = lax.rem(t + n - 1, n), lax.rem(t + 1, n)
    seat, back = lax.rem(t, 16), lax.rem(t + n - 16, n)
    y, z, x = lax.rem(t, 4), lax.rem(lax.div(t, 4), 4), lax.div(t, 16)
    ys = [lax.rem(y + d, 4) for d in range(4)]
    zs = [4 * lax.rem(z + d, 4) for d in range(4)]
    xs = [16 * lax.rem(x + d, 4) for d in range(4)]
    ring_y = [xs[0] + zs[0] + ys[d] for d in (1, 2, 3)]
    ring_z = [xs[0] + zs[d] + ys[0] for d in (1, 2, 3)]
    ring_x = [xs[d] + zs[0] + ys[0] for d in (1, 2, 3)]
    bar = pltpu.get_barrier_semaphore()

    def signal(sem, group, tile):
        pl.semaphore_signal(sem, inc=1, device_id=(group, tile), device_id_type=MESH)

    loads = [
        pltpu.make_async_copy(inputs[i], local[i], in_sem.at[i]) for i in range(18)
    ]
    for i in (15, 14, 0, 5, 8, 9, 10, 11, 12, 4, 2, 1, 6, 7, 17, 3, 16, 13):
        loads[i].start()
    def greet(ok, group, tile):
        if ok is None:
            signal(bar, group, tile)
        else:
            pl.when(ok)(functools.partial(signal, bar, group, tile))

    for d, ok in ((-2, seat < 14), (2, None), (-1, seat < 15), (1, None)):
        greet(ok, 1 - g, lax.rem(t + n - d, n))
    greet(None, g, left)
    greet(seat < 15, g, right)
    greet(seat < 2, 1 - g, lax.rem(t + 16, n))
    for tile in (*ring_y, *ring_z, *ring_x):
        signal(bar, g, tile)
    signal(bar, 1 - g, t)

    tiles = inputs[18]
    chunks = 4
    per = 160 // chunks
    tile_copies = [
        pltpu.make_async_copy(
            tiles.at[pl.ds(c * per, per)], tl.at[pl.ds(c * per, per)], tile_sem.at[c]
        )
        for c in range(chunks)
    ]
    for c in tile_copies:
        c.start()

    def ready(*which):
        for i in which:
            loads[i].wait()

    ready(15, 14)

    def gather(i, carry):
        for a in range(8):
            s = i * 8 + a
            outg[s] = surf[jnp.minimum(sendb[0, s], 63)]
        return carry

    lax.fori_loop(0, 20, gather, 0)

    ready(0, 5, 8, 9, 10, 11, 12, 4, 2)
    row8 = iota((8, 128), 0)
    cpos = [ctab[k] - 16 - 128 * row8 for k in range(3)]
    csum = cedge[0] + cedge[1] + cedge[2]
    c_d = cdiag[...] + csum
    for k in range(3):
        etab[k, 2:10, :] = cpos[k].astype(F32)
        etab[k, 12:16, :] = jnp.zeros((4, 128), F32)
        eedge[k, 2:10, :] = cedge[k]
        eedge[k, 12:16, :] = jnp.zeros((4, 128), F32)
    e_d[...] = jnp.ones((24, 128), F32)
    e_d[3:11, :] = c_d
    e_o[...] = jnp.zeros((24, 128), F32)
    e_o[3:11, :] = cown[...].astype(F32)
    for side, block, low in ((0, 0, 0), (1, 63, 6)):
        hs[side, 0:8, :] = fields[block]
        hs[side, 8:9, :] = oldh[block : block + 1, :]
        hs[side, 9:10, :] = fown[block : block + 1, :].astype(F32)
        for k in range(3):
            here = ftab[k, block : block + 1, :] - (128 + 128 * block)
            hs[side, 10 + k : 11 + k, :] = here.astype(F32)
            hs[side, 13 + k : 14 + k, :] = edge[k, block : block + 1, :]
        for k in range(3):
            hs[side, 16 + 2 * k : 18 + 2 * k, :] = etab[k, 2 + low : 4 + low, :]
            hs[side, 22 + 2 * k : 24 + 2 * k, :] = cedge[k, low : low + 2, :]
        hs[side, 28:30, :] = e_d[3 + low : 5 + low, :]
        hs[side, 30:32, :] = e_o[3 + low : 5 + low, :]

    pl.semaphore_wait(bar, jnp.where(seat == 0, 14, 16))

    surf_copies = [
        pltpu.make_async_remote_copy(
            src_ref=outg.at[pl.ds(32 * j, 32)],
            dst_ref=inc.at[pl.ds(32 * j, 32)],
            send_sem=surf_ss.at[j],
            recv_sem=surf_rs.at[j],
            device_id=(1 - g, lax.rem(t + n + 2 - j, n)),
            device_id_type=MESH,
        )
        for j in range(5)
    ]

    def pair(to_left, at_right, to_right, at_left, ss, rs):
        return [
            pltpu.make_async_remote_copy(
                src_ref=to_left, dst_ref=at_right, send_sem=ss.at[0], recv_sem=rs.at[0],
                device_id=(g, left), device_id_type=MESH,
            ),
            pltpu.make_async_remote_copy(
                src_ref=to_right, dst_ref=at_left, send_sem=ss.at[1], recv_sem=rs.at[1],
                device_id=(g, right), device_id_type=MESH,
            ),
        ]

    halo_copies = pair(hs.at[0], hr.at[1], hs.at[1], hr.at[0], halo_ss, halo_rs)
    inv_copies = pair(inputs[13], invr.at[1], inputs[13], invr.at[0], inv_ss, inv_rs)
    def relayed(source, landing, ss, rs, group):
        return pltpu.make_async_remote_copy(
            src_ref=source, dst_ref=landing, send_sem=ss, recv_sem=rs,
            device_id=(group, back), device_id_type=MESH,
        )

    def handed(source, landing, ss, rs, ahead):
        return pltpu.make_async_remote_copy(
            src_ref=source, dst_ref=landing, send_sem=ss, recv_sem=rs,
            device_id=(g, lax.rem(t + ahead, n)), device_id_type=MESH,
        )

    surf_in = [
        relayed(
            outg.at[pl.ds(32 * j, 32)], rl.at[j - 3], surf_ss.at[j], rl_rs.at[j - 3], 1 - g
        )
        for j in (3, 4)
    ]
    surf_on = [
        handed(
            rl.at[j - 3], inc.at[pl.ds(32 * j, 32)], rl_ss.at[j - 3], surf_rs.at[j], 18 - j
        )
        for j in (3, 4)
    ]
    halo_in = relayed(hs.at[0], rh, halo_ss.at[0], rh_rs, g)
    halo_on = handed(rh, hr.at[1], rh_ss, halo_rs.at[0], 15)

    def either(ok, direct, other):
        pl.when(ok)(direct.start)
        pl.when(jnp.logical_not(ok))(other.start)

    either(seat >= 1, halo_copies[0], halo_in)
    halo_copies[1].start()
    either(seat >= 2, surf_copies[4], surf_in[1])
    surf_copies[0].start()
    either(seat >= 1, surf_copies[3], surf_in[0])
    surf_copies[1].start()
    surf_copies[2].start()
    for tile in ring_z:
        signal(plane_sem, g, tile)

    ready(1, 6, 7, 17, 3, 16, 13)
    def positions(i, carry):
        at = pl.ds(pl.multiple_of(i * 8, 8), 8)
        total = edge[0, at, :] + edge[1, at, :] + edge[2, at, :]
        share = 1.0 / total
        for k in range(3):
            pos[k, at, :] = ftab[k, at, :] - 128 - 128 * (i * 8 + row8)
            shares[k, at, :] = edge[k, at, :] * share
        return carry

    lax.fori_loop(0, 8, positions, 0)

    def column(ref, count):
        out = jnp.zeros((8, 128), F32)
        for level in range(count):
            out = jnp.where(row8 == level, ref[0, level], out)
        return out

    rates, weights = column(rate_s, 8), column(lw_s, 8)

    def advance(j, prev, cur, nxt):
        beside = None
        for k in range(3):
            p = spread(pos[k, pl.ds(j, 1), :])
            w = spread(shares[k, pl.ds(j, 1), :])
            term = w * pick(prev, cur, nxt, p)
            beside = term if beside is None else beside + term
        new = cur + rates * (beside - cur)
        newf[j] = new
        base[pl.ds(j, 1), :] = jnp.sum(weights * new, axis=0, keepdims=True)

    def advance8(i, carry):
        for a in range(8):
            j = i * 8 + a
            advance(j, fields[j - 1], fields[j], fields[j + 1])
        return carry

    lax.fori_loop(1, 7, advance8, 0)
    for j in (*range(1, 8), *range(56, 63)):
        advance(j, fields[j - 1], fields[j], fields[j + 1])

    lane8 = iota((8, 128), 1)
    blocks = iota((64, 160), 0)
    member[...] = jnp.where(
        blocks == jnp.broadcast_to(eblk[...], (64, 160)), 1.0, 0.0
    ).astype(BF16)

    down = iota((128, 128), 0)
    pl.semaphore_wait(plane_sem, 3)
    for tile in ring_x:
        signal(space_sem, g, tile)

    @pl.when(seat == 0)
    def _():
        halo_in.wait_recv()
        halo_on.start()
        surf_in[0].wait_recv()
        surf_on[0].start()

    @pl.when(seat < 2)
    def _():
        surf_in[1].wait_recv()
        surf_on[1].start()

    across = iota((128, 128), 1).astype(F32)
    lanes = (fown[...] & 127).astype(F32)
    column = jnp.transpose(jnp.concatenate([lanes, lanes], axis=0))
    for r in range(64):
        at = slice(128 * r, 128 * r + 128)
        mine = jnp.broadcast_to(column[:, r : r + 1], (128, 128))
        hot[at, :] = jnp.where(across == mine, 1.0, 0.0).astype(BF16)
        upper[8 * r : 8 * r + 8, :] = jnp.where(
            spread(fown[r : r + 1, :] >> 7) == row8, 1.0, 0.0
        )
    for c in halo_copies:
        c.wait_recv()
    advance(0, hr[0, 0:8, :], fields[0], fields[1])
    advance(63, fields[62], fields[63], hr[1, 0:8, :])
    oldp[7:8, :] = hr[0, 8:9, :]
    oldp[8:72, :] = oldh[...]
    oldp[72:73, :] = hr[1, 8:9, :]
    def neighbours(ref, r, _):
        return beside_rows(ref, edge, pos, r)

    def totals(r):
        at = slice(8 * r, 8 * r + 8)
        return fdiag[at, :] + (edge[0, at, :] + edge[1, at, :] + edge[2, at, :])

    for r in range(8):
        at = slice(8 * r, 8 * r + 8)
        smp[8 + 8 * r : 16 + 8 * r, :] = neighbours(oldp, r, 8 + 8 * r)

    row16 = iota((16, 128), 0)
    def halves(at, block):
        inv_h[at : at + 16, :], inv_l[at : at + 16, :] = split(block)

    halves(0, cinv[...])
    for k in range(3):
        etab[k, 0:2, :] = hr[0, 16 + 2 * k : 18 + 2 * k, :]
        etab[k, 10:12, :] = hr[1, 16 + 2 * k : 18 + 2 * k, :]
        eedge[k, 0:2, :] = hr[0, 22 + 2 * k : 24 + 2 * k, :]
        eedge[k, 10:12, :] = hr[1, 22 + 2 * k : 24 + 2 * k, :]
    e_d[1:3, :] = hr[0, 28:30, :]
    e_d[11:13, :] = hr[1, 28:30, :]
    e_o[1:3, :] = hr[0, 30:32, :]
    e_o[11:13, :] = hr[1, 30:32, :]
    side = jnp.where(row16 < 2, 7, jnp.where(row16 >= 10, 1, 0))
    key[...] = ((t + side) & 7) * 16 + e_o[1:17, :].astype(I32)
    for r in range(12):
        khot[:, 128 * r : 128 * r + 128] = jnp.where(
            down == spread(key[r : r + 1, :], 128), 1.0, 0.0
        ).astype(BF16)
    for i in range(2):
        owner = spread(hr[i, 9:10, :], 128).astype(I32) & 127
        hot_n[i] = jnp.where(down == owner, 1.0, 0.0).astype(BF16)
    for c in surf_copies:
        c.wait_recv()
    for c in tile_copies:
        c.wait()

    inv_copies[1].start()
    quarter = row16 // 4
    for i in range(40):
        at = slice(16 * i, 16 * i + 16)
        for e in range(4 * i, 4 * i + 4):
            picks[4 * e : 4 * e + 4, :] = inc[eslot[0, e]].astype(F32)
        rows = picks[at, :]
        ab = jnp.where(quarter < 2, rows, 0.0).astype(BF16)
        cd = jnp.where(quarter < 2, 0.0, rows).astype(BF16)
        four = tl[4 * i : 4 * i + 4]
        out = dot(
            jnp.concatenate([ab, cd], axis=1),
            jnp.concatenate(
                [four[0:2].reshape(256, 128), four[2:4].reshape(256, 128)], axis=1
            ),
            NT,
        )
        prod[at, :] = jnp.where(quarter % 2 == 0, out[:, 0:128], out[:, 128:256])

    for f in range(4):
        high, low = split(prod[pl.ds(f, 160, stride=4), :])
        both = dot(member[...], jnp.concatenate([high, low], axis=1), NN)
        recv[pl.ds(f, 64, stride=4), :] = both[:, 0:128] + both[:, 128:256]

    for r in range(8):
        at = slice(8 * r, 8 * r + 8)
        out = base[at, :]
        for f in range(4):
            out = out + fw_s[0, f] * recv[pl.ds(32 * r + f, 8, stride=4), :]
        base[at, :] = out
        prev = oldh[at, :]
        whole = totals(r)
        smp[8 + 8 * r : 16 + 8 * r, :] = (
            prev + RELAX * (out - (whole * prev - smp[8 + 8 * r : 16 + 8 * r, :])) / whole
        )

    pl.semaphore_wait(space_sem, 3)
    sm_copies = pair(smp.at[pl.ds(8, 8)], sm_r, smp.at[pl.ds(64, 8)], sm_l, sm_ss, sm_rs)
    for c in sm_copies:
        c.start()
    inv_copies[0].start()
    smp[7:8, :] = jnp.zeros((1, 128), F32)
    smp[72:73, :] = jnp.zeros((1, 128), F32)

    def spot(row, owner):
        mine = jnp.where(spread(owner >> 7) == row8, spread(row), 0.0)
        return jnp.concatenate(list(split_f32(mine)), axis=0).astype(BF16)

    for r in range(8):
        at = slice(8 * r, 8 * r + 8)
        cur = smp[8 + 8 * r : 16 + 8 * r, :]
        res = base[at, :] - (totals(r) * cur - neighbours(smp, r, 8 + 8 * r))
        rests[0, at, :], rests[1, at, :] = split_f32(res)
        for a in range(8 * r, 8 * r + 8):
            mask = upper[8 * a : 8 * a + 8, :]
            lhs[:, 128 * a : 128 * a + 128] = jnp.concatenate(
                [mask * spread(rests[i, a : a + 1, :]) for i in range(2)], axis=0
            ).astype(BF16)
    def from_here(i, row, towards):
        row = spread(row)
        out = jnp.zeros((8, 128), F32)
        for k in range(3):
            p = spread(hr[i, 10 + k : 11 + k, :]).astype(I32)
            term = spread(hr[i, 13 + k : 14 + k, :]) * take(row, p & 127)
            out = out + jnp.where(towards(p), term, 0.0)
        both = dot(jnp.concatenate(list(split_f32(out)), axis=0).astype(BF16), hot_n[i], NT)
        return both[0:1] + both[8:9]

    extra_l = from_here(0, smp[8:9, :], lambda p: p > 127)
    extra_r = from_here(1, smp[71:72, :], lambda p: p < 0)
    for r in range(2):
        where = slice(4096 * r, 4096 * r + 4096)
        seg[r] = dot(lhs[:, where], hot[where, :], NN)
    source = (seg[0, 0:8] + seg[0, 8:16]) + (seg[1, 0:8] + seg[1, 8:16])
    cs_s[...] = source
    cs_copies = pair(cs_s, cs_r, cs_s, cs_l, cs_ss, cs_rs)
    for c in cs_copies:
        c.start()

    cs[...] = jnp.zeros((24, 128), F32)
    cs[2:3, :] = extra_l
    cs[3:11, :] = source
    cs[11:12, :] = extra_r
    cf[...] = jnp.zeros((24, 128), F32)
    cs2[...] = jnp.zeros((24, 128), F32)
    cf[0:16, :] = RELAX * cs[0:16, :] / e_d[0:16, :]

    def coarse_neighbours(ref):
        out = None
        for k in range(3):
            term = eedge[k] * pick(
                ref[0:16, :], ref[1:17, :], ref[2:18, :], etab[k].astype(I32)
            )
            out = term if out is None else out + term
        return out

    left_over = cs[1:17, :] - e_d[1:17, :] * cf[1:17, :] + coarse_neighbours(cf)
    klhs[...] = jnp.zeros((8, 1536), F32)
    for r in range(12):
        klhs[0:1, 128 * r : 128 * r + 128] = left_over[r : r + 1]
    packed = jnp.concatenate(list(split_f32(klhs[...])), axis=0).astype(BF16)
    for r in range(2):
        where = slice(768 * r, 768 * r + 768)
        segk[r] = dot(packed[:, where], khot[:, where], NT)
    pay[0] = (segk[0, 0:1] + segk[0, 8:9]) + (segk[1, 0:1] + segk[1, 8:9])
    gb[t] = pay[0]

    hops = (0, 1, 2, 1)
    others = sorted(
        ((a, b, c) for a in range(4) for b in range(4) for c in range(4)),
        key=lambda d: (
            d == (0, 0, 0), (d[1], d[2]) != (1, 1), -(hops[d[0]] + hops[d[1]] + hops[d[2]])
        ),
    )[:-1]
    for a, b, c in others:
        pltpu.make_async_remote_copy(
            src_ref=pay,
            dst_ref=gb.at[pl.ds(t, 1)],
            send_sem=ag_ss,
            recv_sem=ag_rs,
            device_id=(g, xs[a] + zs[b] + ys[c]),
            device_id_type=MESH,
        ).start()

    inv_copies[1].wait_recv()
    halves(16, invr[0])
    for c in sm_copies:
        c.wait_send()
        c.wait_recv()
    smp[7:8, :] = sm_l[7:8, :]
    smp[72:73, :] = sm_r[0:1, :]
    far_l, far_r = spread(sm_l[7:8, :]), spread(sm_r[0:1, :])
    more_l = more_r = jnp.zeros((8, 128), F32)
    for k in range(3):
        p = pos[k, 0:8, :]
        more_l = more_l + jnp.where(p < 0, edge[k, 0:8, :] * take(far_l, p & 127), 0.0)
        p = pos[k, 56:64, :]
        more_r = more_r + jnp.where(p > 127, edge[k, 56:64, :] * take(far_r, p & 127), 0.0)
    sums = dot(spot(more_l[0:1], fown[0:1, :]), hot[0:128, :], NN)
    sums = sums + dot(spot(more_r[7:8], fown[63:64, :]), hot[8064:8192, :], NN)
    more = sums[0:8] + sums[8:16]
    inv_copies[0].wait_recv()
    halves(32, invr[1])
    for c in cs_copies:
        c.wait_recv()
    cs[1:3, :] = cs_l[6:8, :] + cs[1:3, :]
    cs[3:11, :] = cs[3:11, :] + more
    cs[11:13, :] = cs_r[0:2, :] + cs[11:13, :]
    cf[0:16, :] = RELAX * cs[0:16, :] / e_d[0:16, :]

    everyone = pltpu.make_async_remote_copy(
        src_ref=gb.at[pl.ds(0, n - 1)],
        dst_ref=gb.at[pl.ds(0, n - 1)],
        send_sem=ag_ss,
        recv_sem=ag_rs,
        device_id=(g, right),
        device_id_type=MESH,
    )
    everyone.wait_recv()
    from_right = (row8 == 0) & (lane8 >= 112)
    from_left = (row8 == 7) & (lane8 < 16)
    groups = [gb[8 * j : 8 * j + 8, 0, :] for j in range(8)]
    flat = []
    for j in range(8):
        mix = jnp.where(
            from_right, groups[(j + 1) % 8], jnp.where(from_left, groups[(j - 1) % 8], groups[j])
        )
        flat.append(jnp.sum(mix, axis=0, keepdims=True))
    flat = spread_all(jnp.concatenate(flat, axis=1))
    packed = jnp.concatenate(list(split_f32(flat)), axis=0).astype(BF16)
    by_h, by_l = dot(packed, inv_h[...], NT), dot(packed, inv_l[...], NT)
    value = (by_h[0:1] + by_h[8:9]) + (by_l[0:1] + by_l[8:9])
    value = jnp.concatenate([value, jnp.zeros((1, 80), F32)], axis=1)
    value = spread(value, 16)
    shift = jnp.where(row16 < 3, 16, jnp.where(row16 < 11, 0, 32))
    cs2[0:16, :] = cf[0:16, :] + take(value, jnp.minimum(e_o[0:16, :].astype(I32), 15) + shift)
    cur = cs2[1:17, :]
    whole = e_d[1:17, :]
    t3[...] = cur + RELAX * (cs[1:17, :] - (whole * cur - coarse_neighbours(cs2))) / whole

    own_l = spread(hr[0, 9:10, :]).astype(I32) & 127
    own_r = spread(hr[1, 9:10, :]).astype(I32) & 127
    smp[7:8, :] = smp[7:8, :] + take(spread(t3[1:2, :]), own_l)[0:1]
    smp[72:73, :] = smp[72:73, :] + take(spread(t3[10:11, :]), own_r)[0:1]

    for c in halo_copies + surf_copies + inv_copies + cs_copies:
        c.wait_send()
    everyone.wait_send()

    @pl.when(seat == 0)
    def _():
        halo_on.wait_send()
        surf_on[0].wait_send()

    @pl.when(seat < 2)
    def _():
        surf_on[1].wait_send()


def finish(
    newf, recv, smp, t3, base, pos, edge, fdiag, fown, new_out, recv_out, height_out,
    cop, height, sems,
):
    copies = [
        pltpu.make_async_copy(source, target, sems.at[i])
        for i, (source, target) in enumerate(
            ((newf, new_out), (recv, recv_out), (height, height_out))
        )
    ]
    copies[0].start()
    copies[1].start()
    for r in range(8):
        at = slice(8 * r, 8 * r + 8)
        owner = fown[at, :]
        high, lane = owner >> 7, owner & 127
        out = smp[8 + 8 * r : 16 + 8 * r, :]
        for a in range(8):
            out = out + jnp.where(high == a, take(spread(t3[2 + a : 3 + a, :]), lane), 0.0)
        cop[8 + 8 * r : 16 + 8 * r, :] = out
    cop[7:8, :] = smp[7:8, :]
    cop[72:73, :] = smp[72:73, :]
    for r in range(8):
        at = slice(8 * r, 8 * r + 8)
        cur = cop[8 + 8 * r : 16 + 8 * r, :]
        whole = fdiag[at, :] + (edge[0, at, :] + edge[1, at, :] + edge[2, at, :])
        beside = beside_rows(cop, edge, pos, r)
        height[at, :] = cur + RELAX * (base[at, :] - (whole * cur - beside)) / whole
    copies[2].start()
    for copy in copies:
        copy.wait()


def beside_rows(ref, edge, pos, r):
    out = None
    row = 8 + 8 * r
    prev, cur, nxt = ref[row - 1 : row + 7, :], ref[row : row + 8, :], ref[row + 1 : row + 9, :]
    for k in range(3):
        at = slice(8 * r, 8 * r + 8)
        term = edge[k, at, :] * pick(prev, cur, nxt, pos[k, at, :])
        out = term if out is None else out + term
    return out


def split_f32(x):
    high = x.astype(BF16).astype(F32)
    return high, x - high


def spread_all(row):
    return jnp.broadcast_to(row, (8, row.shape[1]))


def per_device(
    fields, level_rate, edge_weight, fine_diagonal, fine_table, old_height, level_weight,
    flux_weight, fine_owner, coarse_table, coarse_edge, coarse_diagonal, coarse_owner,
    coarse_inverse, surface_out, send_blocks, entry_slot, entry_block, remap_tiles,
):
    operands = (
        fields.reshape(8, 64, 128).transpose(1, 0, 2),
        level_rate,
        edge_weight.reshape(3, 64, 128),
        fine_diagonal.reshape(64, 128),
        fine_table.reshape(3, 64, 128),
        old_height.reshape(64, 128),
        level_weight,
        flux_weight,
        fine_owner.reshape(64, 128),
        coarse_table.reshape(3, 8, 128),
        coarse_edge.reshape(3, 8, 128),
        coarse_diagonal.reshape(8, 128),
        coarse_owner.reshape(8, 128),
        coarse_inverse.reshape(16, 1024),
        surface_out.reshape(4, 64, 128).transpose(1, 0, 2),
        send_blocks.reshape(1, 160),
        entry_slot.reshape(1, 160),
        entry_block.reshape(1, 160),
        remap_tiles.reshape(160, 128, 128),
    )
    vmem = pl.BlockSpec(memory_space=pltpu.VMEM)
    specs = [pl.BlockSpec(memory_space=pltpu.HBM)] * 19
    V = pltpu.VMEM
    local = [
        (pltpu.SMEM if i in (1, 6, 7, 15, 16) else V)(x.shape, x.dtype)
        for i, x in enumerate(operands)
        if i not in (2, 3, 8)
    ]
    shape = jax.ShapeDtypeStruct
    D = pltpu.SemaphoreType.DMA
    made = pl.pallas_call(
        kernel,
        out_shape=(
            shape((64, 8, 128), F32),
            shape((256, 128), F32),
            shape((80, 128), F32),
            shape((16, 128), F32),
            shape((64, 128), F32),
            shape((3, 64, 128), I32),
            shape((3, 64, 128), F32),
            shape((64, 128), F32),
            shape((64, 128), I32),
        ),
        in_specs=specs,
        out_specs=(vmem,) * 9,
        scratch_shapes=[
            *local,
            V((160, 4, 128), BF16),
            V((160, 4, 128), BF16),
            V((2, 32, 128), F32),
            V((2, 32, 128), F32),
            V((2, 16, 1024), F32),
            V((8, 128), F32),
            V((8, 128), F32),
            V((8, 128), F32),
            V((8, 128), F32),
            V((1, 1, 128), F32),
            V((8, 128), F32),
            V((64, 1, 128), F32),
            V((64, 160), BF16),
            V((640, 128), F32),
            V((640, 128), F32),
            V((8192, 128), BF16),
            V((512, 128), F32),
            V((2, 64, 128), F32),
            V((16, 8192), BF16),
            V((2, 16, 128), F32),
            V((80, 128), F32),
            V((3, 16, 128), F32),
            V((3, 16, 128), F32),
            V((24, 128), F32),
            V((24, 128), F32),
            V((16, 128), I32),
            V((24, 128), F32),
            V((24, 128), F32),
            V((24, 128), F32),
            V((128, 1536), BF16),
            V((8, 1536), F32),
            V((2, 128, 128), BF16),
            V((3, 64, 128), F32),
            V((48, 1024), BF16),
            V((48, 1024), BF16),
            V((2, 16, 128), F32),
            V((2, 32, 4, 128), BF16),
            V((32, 128), F32),
            D((18,)),
            D((4,)),
            D((5,)), D((5,)),
            D((2,)), D((2,)),
            D((2,)), D((2,)),
            D((2,)), D((2,)),
            D((2,)), D((2,)),
            D, D,
            pltpu.SemaphoreType.REGULAR, pltpu.SemaphoreType.REGULAR,
            D((2,)), D((2,)), D, D,
        ],
        compiler_params=pltpu.CompilerParams(
            collective_id=0, has_side_effects=True, vmem_limit_bytes=48 << 20
        ),
        name="step",
    )(*[pltpu.with_memory_space_constraint(x, pltpu.HBM) for x in operands])
    new, got, high = pl.pallas_call(
        finish,
        out_shape=(shape((64, 8, 128), F32), shape((256, 128), F32), shape((64, 128), F32)),
        in_specs=[vmem] * 9,
        out_specs=[pl.BlockSpec(memory_space=pltpu.HBM)] * 3,
        scratch_shapes=[V((80, 128), F32), V((64, 128), F32), D((3,))],
        compiler_params=pltpu.CompilerParams(vmem_limit_bytes=1 << 20),
        name="finish",
    )(*made)
    return (
        new.transpose(1, 0, 2).reshape(1, 8, 8192),
        got.reshape(64, 4, 128).transpose(1, 0, 2).reshape(1, 4, 8192),
        high.reshape(1, 8192),
    )


def solution(mesh):
    in_specs = (
        P("comp", None, "tile"),
        P("comp", None),
        P("comp", None, "tile"),
        P("comp", "tile"),
        P("comp", None, "tile"),
        P("comp", "tile"),
        P("comp", None),
        P("comp", None),
        P("comp", "tile"),
        P("comp", None, "tile"),
        P("comp", None, "tile"),
        P("comp", "tile"),
        P("comp", "tile"),
        P("comp", "tile", None),
        P("comp", None, "tile"),
        P("comp", "tile", None),
        P("comp", "tile", None),
        P("comp", "tile", None),
        P("comp", "tile", None, None, None),
    )
    out_specs = (P("comp", None, "tile"), P("comp", None, "tile"), P("comp", "tile"))
    return jax.shard_map(
        per_device, mesh=mesh, in_specs=in_specs, out_specs=out_specs, check_vma=False
    )
```

```python
import functools

import jax
import jax.numpy as jnp
from jax import lax
from jax.experimental import pallas as pl
from jax.experimental.pallas import tpu as pltpu
from jax.sharding import PartitionSpec as P

MESH = pl.DeviceIdType.MESH
F32, BF16, I32 = jnp.float32, jnp.bfloat16, jnp.int32
RELAX = 0.8
NT = (((1,), (1,)), ((), ()))
NN = (((1,), (0,)), ((), ()))


def take(x, lane):
    return jnp.take_along_axis(x, lane, axis=1, mode="promise_in_bounds")


def pick(prev, cur, nxt, pos):
    lane = pos & 127
    return jnp.where(
        pos < 0, take(prev, lane), jnp.where(pos > 127, take(nxt, lane), take(cur, lane))
    )


def spread(row, count=8):
    return jnp.broadcast_to(row, (count, 128))


def iota(shape, dim):
    return lax.broadcasted_iota(I32, shape, dim)


def split(x):
    high = x.astype(BF16)
    return high, (x - high.astype(F32)).astype(BF16)


def dot(a, b, dims):
    return lax.dot_general(a, b, dims, preferred_element_type=F32)


def kernel(
    *refs,
):
    inputs, outputs, rest = refs[:19], refs[19:29], refs[29:]
    local, scratch = list(rest[:17]), rest[17:]
    for i, ref in zip((2, 8), outputs[8:]):
        local.insert(i, ref)
    step(*local, *outputs[:8], inputs, local, *scratch)


def step(
    fields, rate_s, edge, fdiag, ftab, oldh, lw_s, fw_s, fown, ctab, cedge, cdiag, cown,
    cinv, surf, sendb, eslot, eblk, tl,
    newf, recv, smp, t3, base, pos, whole, scale, inputs, local,
    outg, inc, hs, hr, invr, sm_l, sm_r, cs_l, cs_r, pay, cs_s, gb, member, picks, prod,
    hot, upper, rests, lhs, seg, oldp, etab, eedge, e_d, e_s, e_o, key, cs, cf, cs2, khot, klhs, hot_n, shares,
    inv_h, inv_l, segk, rl, rh,
    in_sem, tile_sem, surf_ss, surf_rs, halo_ss, halo_rs, inv_ss, inv_rs, sm_ss, sm_rs, cs_ss, cs_rs,
    ag_ss, ag_rs, plane_sem, space_sem, rl_ss, rl_rs, rh_ss, rh_rs,
):
    g = lax.axis_index("comp")
    t = lax.axis_index("tile")
    n = lax.axis_size("tile")
    left, right = lax.rem(t + n - 1, n), lax.rem(t + 1, n)
    seat, back = lax.rem(t, 16), lax.rem(t + n - 16, n)
    y, z, x = lax.rem(t, 4), lax.rem(lax.div(t, 4), 4), lax.div(t, 16)
    ys = [lax.rem(y + d, 4) for d in range(4)]
    zs = [4 * lax.rem(z + d, 4) for d in range(4)]
    xs = [16 * lax.rem(x + d, 4) for d in range(4)]
    ring_y = [xs[0] + zs[0] + ys[d] for d in (1, 2, 3)]
    ring_z = [xs[0] + zs[d] + ys[0] for d in (1, 2, 3)]
    ring_x = [xs[d] + zs[0] + ys[0] for d in (1, 2, 3)]
    bar = pltpu.get_barrier_semaphore()

    def signal(sem, group, tile):
        pl.semaphore_signal(sem, inc=1, device_id=(group, tile), device_id_type=MESH)

    loads = [
        pltpu.make_async_copy(inputs[i], local[i], in_sem.at[i]) for i in range(18)
    ]
    for i in (15, 14, 0, 5, 8, 9, 10, 11, 12, 4, 2, 1, 6, 7, 17, 3, 16, 13):
        loads[i].start()
    def greet(ok, group, tile):
        if ok is None:
            signal(bar, group, tile)
        else:
            pl.when(ok)(functools.partial(signal, bar, group, tile))

    for d, ok in ((-2, seat < 14), (2, None), (-1, seat < 15), (1, None)):
        greet(ok, 1 - g, lax.rem(t + n - d, n))
    greet(None, g, left)
    greet(seat < 15, g, right)
    greet(seat < 2, 1 - g, lax.rem(t + 16, n))
    for tile in (*ring_y, *ring_z, *ring_x):
        signal(bar, g, tile)
    signal(bar, 1 - g, t)

    tiles = inputs[18]
    chunks = 4
    per = 160 // chunks
    tile_copies = [
        pltpu.make_async_copy(
            tiles.at[pl.ds(c * per, per)], tl.at[pl.ds(c * per, per)], tile_sem.at[c]
        )
        for c in range(chunks)
    ]
    for c in tile_copies:
        c.start()

    def ready(*which):
        for i in which:
            loads[i].wait()

    ready(15, 14)

    def gather(i, carry):
        for a in range(8):
            s = i * 8 + a
            outg[s] = surf[jnp.minimum(sendb[0, s], 63)]
        return carry

    lax.fori_loop(0, 20, gather, 0)

    ready(0, 5, 8, 9, 10, 11, 12, 4, 2)
    row8 = iota((8, 128), 0)
    cpos = [ctab[k] - 16 - 128 * row8 for k in range(3)]
    csum = cedge[0] + cedge[1] + cedge[2]
    c_d = cdiag[...] + csum
    for k in range(3):
        etab[k, 2:10, :] = cpos[k].astype(F32)
        etab[k, 12:16, :] = jnp.zeros((4, 128), F32)
        eedge[k, 2:10, :] = cedge[k]
        eedge[k, 12:16, :] = jnp.zeros((4, 128), F32)
    e_d[...] = jnp.ones((24, 128), F32)
    e_d[3:11, :] = c_d
    e_o[...] = jnp.zeros((24, 128), F32)
    e_o[3:11, :] = cown[...].astype(F32)
    for side, block, low in ((0, 0, 0), (1, 63, 6)):
        hs[side, 0:8, :] = fields[block]
        hs[side, 8:9, :] = oldh[block : block + 1, :]
        hs[side, 9:10, :] = fown[block : block + 1, :].astype(F32)
        for k in range(3):
            here = ftab[k, block : block + 1, :] - (128 + 128 * block)
            hs[side, 10 + k : 11 + k, :] = here.astype(F32)
            hs[side, 13 + k : 14 + k, :] = edge[k, block : block + 1, :]
        for k in range(3):
            hs[side, 16 + 2 * k : 18 + 2 * k, :] = etab[k, 2 + low : 4 + low, :]
            hs[side, 22 + 2 * k : 24 + 2 * k, :] = cedge[k, low : low + 2, :]
        hs[side, 28:30, :] = e_d[3 + low : 5 + low, :]
        hs[side, 30:32, :] = e_o[3 + low : 5 + low, :]

    pl.semaphore_wait(bar, jnp.where(seat == 0, 14, 16))

    surf_copies = [
        pltpu.make_async_remote_copy(
            src_ref=outg.at[pl.ds(32 * j, 32)],
            dst_ref=inc.at[pl.ds(32 * j, 32)],
            send_sem=surf_ss.at[j],
            recv_sem=surf_rs.at[j],
            device_id=(1 - g, lax.rem(t + n + 2 - j, n)),
            device_id_type=MESH,
        )
        for j in range(5)
    ]

    def pair(to_left, at_right, to_right, at_left, ss, rs):
        return [
            pltpu.make_async_remote_copy(
                src_ref=to_left, dst_ref=at_right, send_sem=ss.at[0], recv_sem=rs.at[0],
                device_id=(g, left), device_id_type=MESH,
            ),
            pltpu.make_async_remote_copy(
                src_ref=to_right, dst_ref=at_left, send_sem=ss.at[1], recv_sem=rs.at[1],
                device_id=(g, right), device_id_type=MESH,
            ),
        ]

    halo_copies = pair(hs.at[0], hr.at[1], hs.at[1], hr.at[0], halo_ss, halo_rs)
    inv_copies = pair(inputs[13], invr.at[1], inputs[13], invr.at[0], inv_ss, inv_rs)
    def relayed(source, landing, ss, rs, group):
        return pltpu.make_async_remote_copy(
            src_ref=source, dst_ref=landing, send_sem=ss, recv_sem=rs,
            device_id=(group, back), device_id_type=MESH,
        )

    def handed(source, landing, ss, rs, ahead):
        return pltpu.make_async_remote_copy(
            src_ref=source, dst_ref=landing, send_sem=ss, recv_sem=rs,
            device_id=(g, lax.rem(t + ahead, n)), device_id_type=MESH,
        )

    surf_in = [
        relayed(
            outg.at[pl.ds(32 * j, 32)], rl.at[j - 3], surf_ss.at[j], rl_rs.at[j - 3], 1 - g
        )
        for j in (3, 4)
    ]
    surf_on = [
        handed(
            rl.at[j - 3], inc.at[pl.ds(32 * j, 32)], rl_ss.at[j - 3], surf_rs.at[j], 18 - j
        )
        for j in (3, 4)
    ]
    halo_in = relayed(hs.at[0], rh, halo_ss.at[0], rh_rs, g)
    halo_on = handed(rh, hr.at[1], rh_ss, halo_rs.at[0], 15)

    def either(ok, direct, other):
        pl.when(ok)(direct.start)
        pl.when(jnp.logical_not(ok))(other.start)

    either(seat >= 1, halo_copies[0], halo_in)
    halo_copies[1].start()
    either(seat >= 2, surf_copies[4], surf_in[1])
    surf_copies[0].start()
    either(seat >= 1, surf_copies[3], surf_in[0])
    surf_copies[1].start()
    surf_copies[2].start()
    for tile in ring_z:
        signal(plane_sem, g, tile)

    ready(1, 6, 7, 17, 3, 16, 13)
    def positions(i, carry):
        at = pl.ds(pl.multiple_of(i * 8, 8), 8)
        total = edge[0, at, :] + edge[1, at, :] + edge[2, at, :]
        share = 1.0 / total
        whole[at, :] = fdiag[at, :] + total
        scale[at, :] = RELAX / whole[at, :]
        for k in range(3):
            pos[k, at, :] = ftab[k, at, :] - 128 - 128 * (i * 8 + row8)
            shares[k, at, :] = edge[k, at, :] * share
        return carry

    lax.fori_loop(0, 8, positions, 0)

    def column(ref, count):
        out = jnp.zeros((8, 128), F32)
        for level in range(count):
            out = jnp.where(row8 == level, ref[0, level], out)
        return out

    rates, weights = column(rate_s, 8), column(lw_s, 8)

    def advance(j, prev, cur, nxt):
        beside = None
        for k in range(3):
            p = spread(pos[k, pl.ds(j, 1), :])
            w = spread(shares[k, pl.ds(j, 1), :])
            term = w * pick(prev, cur, nxt, p)
            beside = term if beside is None else beside + term
        new = cur + rates * (beside - cur)
        newf[j] = new
        base[pl.ds(j, 1), :] = jnp.sum(weights * new, axis=0, keepdims=True)

    def advance8(i, carry):
        for a in range(8):
            j = i * 8 + a
            advance(j, fields[j - 1], fields[j], fields[j + 1])
        return carry

    lax.fori_loop(1, 7, advance8, 0)
    for j in (*range(1, 8), *range(56, 63)):
        advance(j, fields[j - 1], fields[j], fields[j + 1])

    lane8 = iota((8, 128), 1)
    blocks = iota((64, 160), 0)
    member[...] = jnp.where(
        blocks == jnp.broadcast_to(eblk[...], (64, 160)), 1.0, 0.0
    ).astype(BF16)

    down = iota((128, 128), 0)
    pl.semaphore_wait(plane_sem, 3)
    for tile in ring_x:
        signal(space_sem, g, tile)

    @pl.when(seat == 0)
    def _():
        halo_in.wait_recv()
        halo_on.start()
        surf_in[0].wait_recv()
        surf_on[0].start()

    @pl.when(seat < 2)
    def _():
        surf_in[1].wait_recv()
        surf_on[1].start()

    across = iota((128, 128), 1).astype(F32)
    lanes = (fown[...] & 127).astype(F32)
    column = jnp.transpose(jnp.concatenate([lanes, lanes], axis=0))
    for r in range(64):
        at = slice(128 * r, 128 * r + 128)
        mine = jnp.broadcast_to(column[:, r : r + 1], (128, 128))
        hot[at, :] = jnp.where(across == mine, 1.0, 0.0).astype(BF16)
        upper[8 * r : 8 * r + 8, :] = jnp.where(
            spread(fown[r : r + 1, :] >> 7) == row8, 1.0, 0.0
        )
    row16 = iota((16, 128), 0)
    side = jnp.where(row16 < 2, 7, jnp.where(row16 >= 10, 1, 0))

    def mark_owners(rows):
        key[...] = ((t + side) & 7) * 16 + e_o[1:17, :].astype(I32)
        for r in rows:
            khot[:, 128 * r : 128 * r + 128] = jnp.where(
                down == spread(key[r : r + 1, :], 128), 1.0, 0.0
            ).astype(BF16)

    mark_owners(range(2, 10))
    for c in halo_copies:
        c.wait_recv()
    for c in surf_copies:
        c.wait_recv()
    for c in tile_copies:
        c.wait()

    inv_copies[1].start()
    quarter = row16 // 4
    for i in range(40):
        at = slice(16 * i, 16 * i + 16)
        for e in range(4 * i, 4 * i + 4):
            picks[4 * e : 4 * e + 4, :] = inc[eslot[0, e]].astype(F32)
        rows = picks[at, :]
        ab = jnp.where(quarter < 2, rows, 0.0).astype(BF16)
        cd = jnp.where(quarter < 2, 0.0, rows).astype(BF16)
        four = tl[4 * i : 4 * i + 4]
        out = dot(
            jnp.concatenate([ab, cd], axis=1),
            jnp.concatenate(
                [four[0:2].reshape(256, 128), four[2:4].reshape(256, 128)], axis=1
            ),
            NT,
        )
        prod[at, :] = jnp.where(quarter % 2 == 0, out[:, 0:128], out[:, 128:256])

    advance(0, hr[0, 0:8, :], fields[0], fields[1])
    advance(63, fields[62], fields[63], hr[1, 0:8, :])
    oldp[7:8, :] = hr[0, 8:9, :]
    oldp[8:72, :] = oldh[...]
    oldp[72:73, :] = hr[1, 8:9, :]
    def neighbours(ref, r, _):
        return beside_rows(ref, edge, pos, r)

    for r in range(8):
        at = slice(8 * r, 8 * r + 8)
        smp[8 + 8 * r : 16 + 8 * r, :] = neighbours(oldp, r, 8 + 8 * r)

    def halves(at, block):
        inv_h[at : at + 16, :], inv_l[at : at + 16, :] = split(block)

    halves(0, cinv[...])
    for k in range(3):
        etab[k, 0:2, :] = hr[0, 16 + 2 * k : 18 + 2 * k, :]
        etab[k, 10:12, :] = hr[1, 16 + 2 * k : 18 + 2 * k, :]
        eedge[k, 0:2, :] = hr[0, 22 + 2 * k : 24 + 2 * k, :]
        eedge[k, 10:12, :] = hr[1, 22 + 2 * k : 24 + 2 * k, :]
    e_d[1:3, :] = hr[0, 28:30, :]
    e_d[11:13, :] = hr[1, 28:30, :]
    e_s[...] = RELAX / e_d[...]
    e_o[1:3, :] = hr[0, 30:32, :]
    e_o[11:13, :] = hr[1, 30:32, :]
    mark_owners((0, 1, 10, 11))
    for i in range(2):
        owner = spread(hr[i, 9:10, :], 128).astype(I32) & 127
        hot_n[i] = jnp.where(down == owner, 1.0, 0.0).astype(BF16)
    for f in range(4):
        high, low = split(prod[pl.ds(f, 160, stride=4), :])
        both = dot(member[...], jnp.concatenate([high, low], axis=1), NN)
        recv[pl.ds(f, 64, stride=4), :] = both[:, 0:128] + both[:, 128:256]

    for r in range(8):
        at = slice(8 * r, 8 * r + 8)
        out = base[at, :]
        for f in range(4):
            out = out + fw_s[0, f] * recv[pl.ds(32 * r + f, 8, stride=4), :]
        base[at, :] = out
        prev = oldh[at, :]
        beside = smp[8 + 8 * r : 16 + 8 * r, :]
        smp[8 + 8 * r : 16 + 8 * r, :] = (
            prev + (out - (whole[at, :] * prev - beside)) * scale[at, :]
        )

    pl.semaphore_wait(space_sem, 3)
    sm_copies = pair(smp.at[pl.ds(8, 8)], sm_r, smp.at[pl.ds(64, 8)], sm_l, sm_ss, sm_rs)
    for c in sm_copies:
        c.start()
    inv_copies[0].start()
    smp[7:8, :] = jnp.zeros((1, 128), F32)
    smp[72:73, :] = jnp.zeros((1, 128), F32)

    def spot(row, owner):
        mine = jnp.where(spread(owner >> 7) == row8, spread(row), 0.0)
        return jnp.concatenate(list(split_f32(mine)), axis=0).astype(BF16)

    for r in range(8):
        at = slice(8 * r, 8 * r + 8)
        cur = smp[8 + 8 * r : 16 + 8 * r, :]
        res = base[at, :] - (whole[at, :] * cur - neighbours(smp, r, 8 + 8 * r))
        rests[0, at, :], rests[1, at, :] = split_f32(res)
        for a in range(8 * r, 8 * r + 8):
            mask = upper[8 * a : 8 * a + 8, :]
            lhs[:, 128 * a : 128 * a + 128] = jnp.concatenate(
                [mask * spread(rests[i, a : a + 1, :]) for i in range(2)], axis=0
            ).astype(BF16)
    def from_here(i, row, towards):
        row = spread(row)
        out = jnp.zeros((8, 128), F32)
        for k in range(3):
            p = spread(hr[i, 10 + k : 11 + k, :]).astype(I32)
            term = spread(hr[i, 13 + k : 14 + k, :]) * take(row, p & 127)
            out = out + jnp.where(towards(p), term, 0.0)
        both = dot(jnp.concatenate(list(split_f32(out)), axis=0).astype(BF16), hot_n[i], NT)
        return both[0:1] + both[8:9]

    extra_l = from_here(0, smp[8:9, :], lambda p: p > 127)
    extra_r = from_here(1, smp[71:72, :], lambda p: p < 0)
    for r in range(2):
        where = slice(4096 * r, 4096 * r + 4096)
        seg[r] = dot(lhs[:, where], hot[where, :], NN)
    source = (seg[0, 0:8] + seg[0, 8:16]) + (seg[1, 0:8] + seg[1, 8:16])
    cs_s[...] = source
    cs_copies = pair(cs_s, cs_r, cs_s, cs_l, cs_ss, cs_rs)
    for c in cs_copies:
        c.start()

    cs[...] = jnp.zeros((24, 128), F32)
    cs[2:3, :] = extra_l
    cs[3:11, :] = source
    cs[11:12, :] = extra_r
    cf[...] = jnp.zeros((24, 128), F32)
    cs2[...] = jnp.zeros((24, 128), F32)
    cf[0:16, :] = cs[0:16, :] * e_s[0:16, :]

    def coarse_neighbours(ref):
        out = None
        for k in range(3):
            term = eedge[k] * pick(
                ref[0:16, :], ref[1:17, :], ref[2:18, :], etab[k].astype(I32)
            )
            out = term if out is None else out + term
        return out

    left_over = cs[1:17, :] - e_d[1:17, :] * cf[1:17, :] + coarse_neighbours(cf)
    klhs[...] = jnp.zeros((8, 1536), F32)
    for r in range(12):
        klhs[0:1, 128 * r : 128 * r + 128] = left_over[r : r + 1]
    packed = jnp.concatenate(list(split_f32(klhs[...])), axis=0).astype(BF16)
    for r in range(2):
        where = slice(768 * r, 768 * r + 768)
        segk[r] = dot(packed[:, where], khot[:, where], NT)
    pay[0] = (segk[0, 0:1] + segk[0, 8:9]) + (segk[1, 0:1] + segk[1, 8:9])
    gb[t] = pay[0]

    hops = (0, 1, 2, 1)
    others = sorted(
        ((a, b, c) for a in range(4) for b in range(4) for c in range(4)),
        key=lambda d: (
            d == (0, 0, 0), (d[1], d[2]) != (1, 1), -(hops[d[0]] + hops[d[1]] + hops[d[2]])
        ),
    )[:-1]
    for a, b, c in others:
        pltpu.make_async_remote_copy(
            src_ref=pay,
            dst_ref=gb.at[pl.ds(t, 1)],
            send_sem=ag_ss,
            recv_sem=ag_rs,
            device_id=(g, xs[a] + zs[b] + ys[c]),
            device_id_type=MESH,
        ).start()

    inv_copies[1].wait_recv()
    halves(16, invr[0])
    for c in sm_copies:
        c.wait_send()
        c.wait_recv()
    smp[7:8, :] = sm_l[7:8, :]
    smp[72:73, :] = sm_r[0:1, :]
    far_l, far_r = spread(sm_l[7:8, :]), spread(sm_r[0:1, :])
    more_l = more_r = jnp.zeros((8, 128), F32)
    for k in range(3):
        p = pos[k, 0:8, :]
        more_l = more_l + jnp.where(p < 0, edge[k, 0:8, :] * take(far_l, p & 127), 0.0)
        p = pos[k, 56:64, :]
        more_r = more_r + jnp.where(p > 127, edge[k, 56:64, :] * take(far_r, p & 127), 0.0)
    sums = dot(spot(more_l[0:1], fown[0:1, :]), hot[0:128, :], NN)
    sums = sums + dot(spot(more_r[7:8], fown[63:64, :]), hot[8064:8192, :], NN)
    more = sums[0:8] + sums[8:16]
    inv_copies[0].wait_recv()
    halves(32, invr[1])
    for c in cs_copies:
        c.wait_recv()
    cs[1:3, :] = cs_l[6:8, :] + cs[1:3, :]
    cs[3:11, :] = cs[3:11, :] + more
    cs[11:13, :] = cs_r[0:2, :] + cs[11:13, :]
    cf[0:16, :] = cs[0:16, :] * e_s[0:16, :]

    everyone = pltpu.make_async_remote_copy(
        src_ref=gb.at[pl.ds(0, n - 1)],
        dst_ref=gb.at[pl.ds(0, n - 1)],
        send_sem=ag_ss,
        recv_sem=ag_rs,
        device_id=(g, right),
        device_id_type=MESH,
    )
    everyone.wait_recv()
    from_right = (row8 == 0) & (lane8 >= 112)
    from_left = (row8 == 7) & (lane8 < 16)
    groups = [gb[8 * j : 8 * j + 8, 0, :] for j in range(8)]
    flat = []
    for j in range(8):
        mix = jnp.where(
            from_right, groups[(j + 1) % 8], jnp.where(from_left, groups[(j - 1) % 8], groups[j])
        )
        flat.append(jnp.sum(mix, axis=0, keepdims=True))
    flat = spread_all(jnp.concatenate(flat, axis=1))
    packed = jnp.concatenate(list(split_f32(flat)), axis=0).astype(BF16)
    by_h, by_l = dot(packed, inv_h[...], NT), dot(packed, inv_l[...], NT)
    value = (by_h[0:1] + by_h[8:9]) + (by_l[0:1] + by_l[8:9])
    value = jnp.concatenate([value, jnp.zeros((1, 80), F32)], axis=1)
    value = spread(value, 16)
    shift = jnp.where(row16 < 3, 16, jnp.where(row16 < 11, 0, 32))
    cs2[0:16, :] = cf[0:16, :] + take(value, jnp.minimum(e_o[0:16, :].astype(I32), 15) + shift)
    cur = cs2[1:17, :]
    rest = cs[1:17, :] - (e_d[1:17, :] * cur - coarse_neighbours(cs2))
    t3[...] = cur + rest * e_s[1:17, :]

    own_l = spread(hr[0, 9:10, :]).astype(I32) & 127
    own_r = spread(hr[1, 9:10, :]).astype(I32) & 127
    smp[7:8, :] = smp[7:8, :] + take(spread(t3[1:2, :]), own_l)[0:1]
    smp[72:73, :] = smp[72:73, :] + take(spread(t3[10:11, :]), own_r)[0:1]

    for c in halo_copies + surf_copies + inv_copies + cs_copies:
        c.wait_send()
    everyone.wait_send()

    @pl.when(seat == 0)
    def _():
        halo_on.wait_send()
        surf_on[0].wait_send()

    @pl.when(seat < 2)
    def _():
        surf_on[1].wait_send()


def finish(
    newf, recv, smp, t3, base, pos, whole, scale, edge, fown, new_out, recv_out, height_out,
    cop, height, sems,
):
    copies = [
        pltpu.make_async_copy(source, target, sems.at[i])
        for i, (source, target) in enumerate(
            ((newf, new_out), (recv, recv_out), (height, height_out))
        )
    ]
    copies[0].start()
    copies[1].start()
    for r in range(8):
        at = slice(8 * r, 8 * r + 8)
        owner = fown[at, :]
        high, lane = owner >> 7, owner & 127
        out = smp[8 + 8 * r : 16 + 8 * r, :]
        for a in range(8):
            out = out + jnp.where(high == a, take(spread(t3[2 + a : 3 + a, :]), lane), 0.0)
        cop[8 + 8 * r : 16 + 8 * r, :] = out
    cop[7:8, :] = smp[7:8, :]
    cop[72:73, :] = smp[72:73, :]
    for r in range(8):
        at = slice(8 * r, 8 * r + 8)
        cur = cop[8 + 8 * r : 16 + 8 * r, :]
        rest = base[at, :] - (whole[at, :] * cur - beside_rows(cop, edge, pos, r))
        height[at, :] = cur + rest * scale[at, :]
    copies[2].start()
    for copy in copies:
        copy.wait()


def beside_rows(ref, edge, pos, r):
    out = None
    row = 8 + 8 * r
    prev, cur, nxt = ref[row - 1 : row + 7, :], ref[row : row + 8, :], ref[row + 1 : row + 9, :]
    for k in range(3):
        at = slice(8 * r, 8 * r + 8)
        term = edge[k, at, :] * pick(prev, cur, nxt, pos[k, at, :])
        out = term if out is None else out + term
    return out


def split_f32(x):
    high = x.astype(BF16).astype(F32)
    return high, x - high


def spread_all(row):
    return jnp.broadcast_to(row, (8, row.shape[1]))


def per_device(
    fields, level_rate, edge_weight, fine_diagonal, fine_table, old_height, level_weight,
    flux_weight, fine_owner, coarse_table, coarse_edge, coarse_diagonal, coarse_owner,
    coarse_inverse, surface_out, send_blocks, entry_slot, entry_block, remap_tiles,
):
    operands = (
        fields.reshape(8, 64, 128).transpose(1, 0, 2),
        level_rate,
        edge_weight.reshape(3, 64, 128),
        fine_diagonal.reshape(64, 128),
        fine_table.reshape(3, 64, 128),
        old_height.reshape(64, 128),
        level_weight,
        flux_weight,
        fine_owner.reshape(64, 128),
        coarse_table.reshape(3, 8, 128),
        coarse_edge.reshape(3, 8, 128),
        coarse_diagonal.reshape(8, 128),
        coarse_owner.reshape(8, 128),
        coarse_inverse.reshape(16, 1024),
        surface_out.reshape(4, 64, 128).transpose(1, 0, 2),
        send_blocks.reshape(1, 160),
        entry_slot.reshape(1, 160),
        entry_block.reshape(1, 160),
        remap_tiles.reshape(160, 128, 128),
    )
    vmem = pl.BlockSpec(memory_space=pltpu.VMEM)
    specs = [pl.BlockSpec(memory_space=pltpu.HBM)] * 19
    V = pltpu.VMEM
    local = [
        (pltpu.SMEM if i in (1, 6, 7, 15, 16) else V)(x.shape, x.dtype)
        for i, x in enumerate(operands)
        if i not in (2, 8)
    ]
    shape = jax.ShapeDtypeStruct
    D = pltpu.SemaphoreType.DMA
    made = pl.pallas_call(
        kernel,
        out_shape=(
            shape((64, 8, 128), F32),
            shape((256, 128), F32),
            shape((80, 128), F32),
            shape((16, 128), F32),
            shape((64, 128), F32),
            shape((3, 64, 128), I32),
            shape((64, 128), F32),
            shape((64, 128), F32),
            shape((3, 64, 128), F32),
            shape((64, 128), I32),
        ),
        in_specs=specs,
        out_specs=(vmem,) * 10,
        scratch_shapes=[
            *local,
            V((160, 4, 128), BF16),
            V((160, 4, 128), BF16),
            V((2, 32, 128), F32),
            V((2, 32, 128), F32),
            V((2, 16, 1024), F32),
            V((8, 128), F32),
            V((8, 128), F32),
            V((8, 128), F32),
            V((8, 128), F32),
            V((1, 1, 128), F32),
            V((8, 128), F32),
            V((64, 1, 128), F32),
            V((64, 160), BF16),
            V((640, 128), F32),
            V((640, 128), F32),
            V((8192, 128), BF16),
            V((512, 128), F32),
            V((2, 64, 128), F32),
            V((16, 8192), BF16),
            V((2, 16, 128), F32),
            V((80, 128), F32),
            V((3, 16, 128), F32),
            V((3, 16, 128), F32),
            V((24, 128), F32),
            V((24, 128), F32),
            V((24, 128), F32),
            V((16, 128), I32),
            V((24, 128), F32),
            V((24, 128), F32),
            V((24, 128), F32),
            V((128, 1536), BF16),
            V((8, 1536), F32),
            V((2, 128, 128), BF16),
            V((3, 64, 128), F32),
            V((48, 1024), BF16),
            V((48, 1024), BF16),
            V((2, 16, 128), F32),
            V((2, 32, 4, 128), BF16),
            V((32, 128), F32),
            D((18,)),
            D((4,)),
            D((5,)), D((5,)),
            D((2,)), D((2,)),
            D((2,)), D((2,)),
            D((2,)), D((2,)),
            D((2,)), D((2,)),
            D, D,
            pltpu.SemaphoreType.REGULAR, pltpu.SemaphoreType.REGULAR,
            D((2,)), D((2,)), D, D,
        ],
        compiler_params=pltpu.CompilerParams(
            collective_id=0, has_side_effects=True, vmem_limit_bytes=48 << 20
        ),
        name="step",
    )(*[pltpu.with_memory_space_constraint(x, pltpu.HBM) for x in operands])
    new, got, high = pl.pallas_call(
        finish,
        out_shape=(shape((64, 8, 128), F32), shape((256, 128), F32), shape((64, 128), F32)),
        in_specs=[vmem] * 10,
        out_specs=[pl.BlockSpec(memory_space=pltpu.HBM)] * 3,
        scratch_shapes=[V((80, 128), F32), V((64, 128), F32), D((3,))],
        compiler_params=pltpu.CompilerParams(vmem_limit_bytes=1 << 20),
        name="finish",
    )(*made)
    return (
        new.transpose(1, 0, 2).reshape(1, 8, 8192),
        got.reshape(64, 4, 128).transpose(1, 0, 2).reshape(1, 4, 8192),
        high.reshape(1, 8192),
    )


def solution(mesh):
    in_specs = (
        P("comp", None, "tile"),
        P("comp", None),
        P("comp", None, "tile"),
        P("comp", "tile"),
        P("comp", None, "tile"),
        P("comp", "tile"),
        P("comp", None),
        P("comp", None),
        P("comp", "tile"),
        P("comp", None, "tile"),
        P("comp", None, "tile"),
        P("comp", "tile"),
        P("comp", "tile"),
        P("comp", "tile", None),
        P("comp", None, "tile"),
        P("comp", "tile", None),
        P("comp", "tile", None),
        P("comp", "tile", None),
        P("comp", "tile", None, None, None),
    )
    out_specs = (P("comp", None, "tile"), P("comp", None, "tile"), P("comp", "tile"))
    return jax.shard_map(
        per_device, mesh=mesh, in_specs=in_specs, out_specs=out_specs, check_vma=False
    )
```

```python
import functools

import jax
import jax.numpy as jnp
from jax import lax
from jax.experimental import pallas as pl
from jax.experimental.pallas import tpu as pltpu
from jax.sharding import PartitionSpec as P

MESH = pl.DeviceIdType.MESH
F32, BF16, I32 = jnp.float32, jnp.bfloat16, jnp.int32
RELAX = 0.8
NT = (((1,), (1,)), ((), ()))
NN = (((1,), (0,)), ((), ()))


def take(x, lane):
    return jnp.take_along_axis(x, lane, axis=1, mode="promise_in_bounds")


def pick(prev, cur, nxt, pos):
    lane = pos & 127
    return jnp.where(
        pos < 0, take(prev, lane), jnp.where(pos > 127, take(nxt, lane), take(cur, lane))
    )


def spread(row, count=8):
    return jnp.broadcast_to(row, (count, 128))


def iota(shape, dim):
    return lax.broadcasted_iota(I32, shape, dim)


def split(x):
    high = x.astype(BF16)
    return high, (x - high.astype(F32)).astype(BF16)


def dot(a, b, dims):
    return lax.dot_general(a, b, dims, preferred_element_type=F32)


def kernel(
    *refs,
):
    inputs, outputs, rest = refs[:19], refs[19:29], refs[29:]
    local, scratch = list(rest[:17]), rest[17:]
    for i, ref in zip((2, 8), outputs[8:]):
        local.insert(i, ref)
    step(*local, *outputs[:8], inputs, local, *scratch)


def step(
    fields, rate_s, edge, fdiag, ftab, oldh, lw_s, fw_s, fown, ctab, cedge, cdiag, cown,
    cinv, surf, sendb, eslot, eblk, tl,
    newf, recv, smp, t3, base, pos, whole, scale, inputs, local,
    outg, inc, hs, hr, invr, sm_l, sm_r, cs_l, cs_r, pay, cs_s, gb, member, picks, prod,
    hot, upper, rests, lhs, seg, oldp, etab, eedge, e_d, e_s, e_o, key, cs, cf, cs2, khot, klhs, hot_n, shares,
    inv_h, inv_l, segk, rl, rh,
    in_sem, tile_sem, surf_ss, surf_rs, halo_ss, halo_rs, inv_ss, inv_rs, sm_ss, sm_rs, cs_ss, cs_rs,
    ag_ss, ag_rs, plane_sem, space_sem, rl_ss, rl_rs, rh_ss, rh_rs,
):
    g = lax.axis_index("comp")
    t = lax.axis_index("tile")
    n = lax.axis_size("tile")
    left, right = lax.rem(t + n - 1, n), lax.rem(t + 1, n)
    seat = lax.rem(t, 16)
    y, z, x = lax.rem(t, 4), lax.rem(lax.div(t, 4), 4), lax.div(t, 16)
    ys = [lax.rem(y + d, 4) for d in range(4)]
    zs = [4 * lax.rem(z + d, 4) for d in range(4)]
    xs = [16 * lax.rem(x + d, 4) for d in range(4)]
    ring_y = [xs[0] + zs[0] + ys[d] for d in (1, 2, 3)]
    ring_z = [xs[0] + zs[d] + ys[0] for d in (1, 2, 3)]
    ring_x = [xs[d] + zs[0] + ys[0] for d in (1, 2, 3)]
    bar = pltpu.get_barrier_semaphore()

    def signal(sem, group, tile):
        pl.semaphore_signal(sem, inc=1, device_id=(group, tile), device_id_type=MESH)

    loads = [
        pltpu.make_async_copy(inputs[i], local[i], in_sem.at[i]) for i in range(18)
    ]
    for i in (15, 14, 0, 5, 8, 9, 10, 11, 12, 4, 2, 1, 6, 7, 17, 3, 16, 13):
        loads[i].start()
    def greet(ok, group, tile):
        if ok is None:
            signal(bar, group, tile)
        else:
            pl.when(ok)(functools.partial(signal, bar, group, tile))

    for d, ok in ((-2, seat < 14), (2, None), (-1, seat < 15), (1, None)):
        greet(ok, 1 - g, lax.rem(t + n - d, n))
    greet(None, g, left)
    greet(seat < 15, g, right)
    hands_on = jnp.logical_and(seat >= 2, seat < 4)
    greet(hands_on, 1 - g, lax.rem(t + 14, n))
    greet(seat == 3, 1 - g, lax.rem(t + 13, n))
    greet(seat == 3, g, lax.rem(t + 13, n))
    for tile in (*ring_y, *ring_z, *ring_x):
        signal(bar, g, tile)
    signal(bar, 1 - g, t)

    tiles = inputs[18]
    chunks = 4
    per = 160 // chunks
    tile_copies = [
        pltpu.make_async_copy(
            tiles.at[pl.ds(c * per, per)], tl.at[pl.ds(c * per, per)], tile_sem.at[c]
        )
        for c in range(chunks)
    ]
    for c in tile_copies:
        c.start()

    def ready(*which):
        for i in which:
            loads[i].wait()

    ready(15, 14)

    def gather(i, carry):
        for a in range(8):
            s = i * 8 + a
            outg[s] = surf[jnp.minimum(sendb[0, s], 63)]
        return carry

    lax.fori_loop(0, 20, gather, 0)

    ready(0, 5, 8, 9, 10, 11, 12, 4, 2)
    row8 = iota((8, 128), 0)
    cpos = [ctab[k] - 16 - 128 * row8 for k in range(3)]
    csum = cedge[0] + cedge[1] + cedge[2]
    c_d = cdiag[...] + csum
    for k in range(3):
        etab[k, 2:10, :] = cpos[k].astype(F32)
        etab[k, 12:16, :] = jnp.zeros((4, 128), F32)
        eedge[k, 2:10, :] = cedge[k]
        eedge[k, 12:16, :] = jnp.zeros((4, 128), F32)
    e_d[...] = jnp.ones((24, 128), F32)
    e_d[3:11, :] = c_d
    e_o[...] = jnp.zeros((24, 128), F32)
    e_o[3:11, :] = cown[...].astype(F32)
    for side, block, low in ((0, 0, 0), (1, 63, 6)):
        hs[side, 0:8, :] = fields[block]
        hs[side, 8:9, :] = oldh[block : block + 1, :]
        hs[side, 9:10, :] = fown[block : block + 1, :].astype(F32)
        for k in range(3):
            here = ftab[k, block : block + 1, :] - (128 + 128 * block)
            hs[side, 10 + k : 11 + k, :] = here.astype(F32)
            hs[side, 13 + k : 14 + k, :] = edge[k, block : block + 1, :]
        for k in range(3):
            hs[side, 16 + 2 * k : 18 + 2 * k, :] = etab[k, 2 + low : 4 + low, :]
            hs[side, 22 + 2 * k : 24 + 2 * k, :] = cedge[k, low : low + 2, :]
        hs[side, 28:30, :] = e_d[3 + low : 5 + low, :]
        hs[side, 30:32, :] = e_o[3 + low : 5 + low, :]

    pl.semaphore_wait(bar, 16)

    surf_copies = [
        pltpu.make_async_remote_copy(
            src_ref=outg.at[pl.ds(32 * j, 32)],
            dst_ref=inc.at[pl.ds(32 * j, 32)],
            send_sem=surf_ss.at[j],
            recv_sem=surf_rs.at[j],
            device_id=(1 - g, lax.rem(t + n + 2 - j, n)),
            device_id_type=MESH,
        )
        for j in range(5)
    ]

    def pair(to_left, at_right, to_right, at_left, ss, rs):
        return [
            pltpu.make_async_remote_copy(
                src_ref=to_left, dst_ref=at_right, send_sem=ss.at[0], recv_sem=rs.at[0],
                device_id=(g, left), device_id_type=MESH,
            ),
            pltpu.make_async_remote_copy(
                src_ref=to_right, dst_ref=at_left, send_sem=ss.at[1], recv_sem=rs.at[1],
                device_id=(g, right), device_id_type=MESH,
            ),
        ]

    halo_copies = pair(hs.at[0], hr.at[1], hs.at[1], hr.at[0], halo_ss, halo_rs)
    inv_copies = pair(inputs[13], invr.at[1], inputs[13], invr.at[0], inv_ss, inv_rs)
    def relayed(source, landing, ss, rs, group, back):
        return pltpu.make_async_remote_copy(
            src_ref=source, dst_ref=landing, send_sem=ss, recv_sem=rs,
            device_id=(group, lax.rem(t + n - back, n)), device_id_type=MESH,
        )

    def handed(source, landing, ss, rs):
        return pltpu.make_async_remote_copy(
            src_ref=source, dst_ref=landing, send_sem=ss, recv_sem=rs,
            device_id=(g, lax.rem(t + 12, n)), device_id_type=MESH,
        )

    surf_in = [
        relayed(
            outg.at[pl.ds(32 * j, 32)],
            rl.at[j - 3],
            surf_ss.at[j],
            rl_rs.at[j - 3],
            1 - g,
            10 + j,
        )
        for j in (3, 4)
    ]
    surf_on = [
        handed(rl.at[j - 3], inc.at[pl.ds(32 * j, 32)], rl_ss.at[j - 3], surf_rs.at[j])
        for j in (3, 4)
    ]
    halo_in = relayed(hs.at[0], rh, halo_ss.at[0], rh_rs, g, 13)
    halo_on = handed(rh, hr.at[1], rh_ss, halo_rs.at[0])

    def either(ok, direct, other):
        pl.when(ok)(direct.start)
        pl.when(jnp.logical_not(ok))(other.start)

    either(seat >= 1, halo_copies[0], halo_in)
    halo_copies[1].start()
    either(seat >= 2, surf_copies[4], surf_in[1])
    surf_copies[0].start()
    either(seat >= 1, surf_copies[3], surf_in[0])
    surf_copies[1].start()
    surf_copies[2].start()
    for tile in ring_z:
        signal(plane_sem, g, tile)

    ready(1, 6, 7, 17, 3, 16, 13)
    def positions(i, carry):
        at = pl.ds(pl.multiple_of(i * 8, 8), 8)
        total = edge[0, at, :] + edge[1, at, :] + edge[2, at, :]
        share = 1.0 / total
        whole[at, :] = fdiag[at, :] + total
        scale[at, :] = RELAX / whole[at, :]
        for k in range(3):
            pos[k, at, :] = ftab[k, at, :] - 128 - 128 * (i * 8 + row8)
            shares[k, at, :] = edge[k, at, :] * share
        return carry

    lax.fori_loop(0, 8, positions, 0)

    def column(ref, count):
        out = jnp.zeros((8, 128), F32)
        for level in range(count):
            out = jnp.where(row8 == level, ref[0, level], out)
        return out

    rates, weights = column(rate_s, 8), column(lw_s, 8)

    def advance(j, prev, cur, nxt):
        beside = None
        for k in range(3):
            p = spread(pos[k, pl.ds(j, 1), :])
            w = spread(shares[k, pl.ds(j, 1), :])
            term = w * pick(prev, cur, nxt, p)
            beside = term if beside is None else beside + term
        new = cur + rates * (beside - cur)
        newf[j] = new
        base[pl.ds(j, 1), :] = jnp.sum(weights * new, axis=0, keepdims=True)

    def advance8(i, carry):
        for a in range(8):
            j = i * 8 + a
            advance(j, fields[j - 1], fields[j], fields[j + 1])
        return carry

    lax.fori_loop(1, 7, advance8, 0)
    for j in (*range(1, 8), *range(56, 63)):
        advance(j, fields[j - 1], fields[j], fields[j + 1])

    lane8 = iota((8, 128), 1)
    blocks = iota((64, 160), 0)
    member[...] = jnp.where(
        blocks == jnp.broadcast_to(eblk[...], (64, 160)), 1.0, 0.0
    ).astype(BF16)

    down = iota((128, 128), 0)
    @pl.when(seat == 3)
    def _():
        halo_in.wait_recv()
        halo_on.start()
        surf_in[0].wait_recv()
        surf_on[0].start()

    @pl.when(hands_on)
    def _():
        surf_in[1].wait_recv()
        surf_on[1].start()

    pl.semaphore_wait(plane_sem, 3)
    for tile in ring_x:
        signal(space_sem, g, tile)

    across = iota((128, 128), 1).astype(F32)
    lanes = (fown[...] & 127).astype(F32)
    column = jnp.transpose(jnp.concatenate([lanes, lanes], axis=0))
    for r in range(64):
        at = slice(128 * r, 128 * r + 128)
        mine = jnp.broadcast_to(column[:, r : r + 1], (128, 128))
        hot[at, :] = jnp.where(across == mine, 1.0, 0.0).astype(BF16)
        upper[8 * r : 8 * r + 8, :] = jnp.where(
            spread(fown[r : r + 1, :] >> 7) == row8, 1.0, 0.0
        )
    row16 = iota((16, 128), 0)
    side = jnp.where(row16 < 2, 7, jnp.where(row16 >= 10, 1, 0))

    def mark_owners(rows):
        key[...] = ((t + side) & 7) * 16 + e_o[1:17, :].astype(I32)
        for r in rows:
            khot[:, 128 * r : 128 * r + 128] = jnp.where(
                down == spread(key[r : r + 1, :], 128), 1.0, 0.0
            ).astype(BF16)

    mark_owners(range(2, 10))
    for c in halo_copies:
        c.wait_recv()
    for c in surf_copies:
        c.wait_recv()
    for c in tile_copies:
        c.wait()

    inv_copies[1].start()
    quarter = row16 // 4
    for i in range(40):
        at = slice(16 * i, 16 * i + 16)
        for e in range(4 * i, 4 * i + 4):
            picks[4 * e : 4 * e + 4, :] = inc[eslot[0, e]].astype(F32)
        rows = picks[at, :]
        ab = jnp.where(quarter < 2, rows, 0.0).astype(BF16)
        cd = jnp.where(quarter < 2, 0.0, rows).astype(BF16)
        four = tl[4 * i : 4 * i + 4]
        out = dot(
            jnp.concatenate([ab, cd], axis=1),
            jnp.concatenate(
                [four[0:2].reshape(256, 128), four[2:4].reshape(256, 128)], axis=1
            ),
            NT,
        )
        prod[at, :] = jnp.where(quarter % 2 == 0, out[:, 0:128], out[:, 128:256])

    advance(0, hr[0, 0:8, :], fields[0], fields[1])
    advance(63, fields[62], fields[63], hr[1, 0:8, :])
    oldp[7:8, :] = hr[0, 8:9, :]
    oldp[8:72, :] = oldh[...]
    oldp[72:73, :] = hr[1, 8:9, :]
    def neighbours(ref, r, _):
        return beside_rows(ref, edge, pos, r)

    for r in range(8):
        at = slice(8 * r, 8 * r + 8)
        smp[8 + 8 * r : 16 + 8 * r, :] = neighbours(oldp, r, 8 + 8 * r)

    def halves(at, block):
        inv_h[at : at + 16, :], inv_l[at : at + 16, :] = split(block)

    halves(0, cinv[...])
    for k in range(3):
        etab[k, 0:2, :] = hr[0, 16 + 2 * k : 18 + 2 * k, :]
        etab[k, 10:12, :] = hr[1, 16 + 2 * k : 18 + 2 * k, :]
        eedge[k, 0:2, :] = hr[0, 22 + 2 * k : 24 + 2 * k, :]
        eedge[k, 10:12, :] = hr[1, 22 + 2 * k : 24 + 2 * k, :]
    e_d[1:3, :] = hr[0, 28:30, :]
    e_d[11:13, :] = hr[1, 28:30, :]
    e_s[...] = RELAX / e_d[...]
    e_o[1:3, :] = hr[0, 30:32, :]
    e_o[11:13, :] = hr[1, 30:32, :]
    mark_owners((0, 1, 10, 11))
    for i in range(2):
        owner = spread(hr[i, 9:10, :], 128).astype(I32) & 127
        hot_n[i] = jnp.where(down == owner, 1.0, 0.0).astype(BF16)
    for f in range(4):
        high, low = split(prod[pl.ds(f, 160, stride=4), :])
        both = dot(member[...], jnp.concatenate([high, low], axis=1), NN)
        recv[pl.ds(f, 64, stride=4), :] = both[:, 0:128] + both[:, 128:256]

    for r in range(8):
        at = slice(8 * r, 8 * r + 8)
        out = base[at, :]
        for f in range(4):
            out = out + fw_s[0, f] * recv[pl.ds(32 * r + f, 8, stride=4), :]
        base[at, :] = out
        prev = oldh[at, :]
        beside = smp[8 + 8 * r : 16 + 8 * r, :]
        smp[8 + 8 * r : 16 + 8 * r, :] = (
            prev + (out - (whole[at, :] * prev - beside)) * scale[at, :]
        )

    pl.semaphore_wait(space_sem, 3)
    sm_copies = pair(smp.at[pl.ds(8, 8)], sm_r, smp.at[pl.ds(64, 8)], sm_l, sm_ss, sm_rs)
    for c in sm_copies:
        c.start()
    inv_copies[0].start()
    smp[7:8, :] = jnp.zeros((1, 128), F32)
    smp[72:73, :] = jnp.zeros((1, 128), F32)

    def spot(row, owner):
        mine = jnp.where(spread(owner >> 7) == row8, spread(row), 0.0)
        return jnp.concatenate(list(split_f32(mine)), axis=0).astype(BF16)

    for r in range(8):
        at = slice(8 * r, 8 * r + 8)
        cur = smp[8 + 8 * r : 16 + 8 * r, :]
        res = base[at, :] - (whole[at, :] * cur - neighbours(smp, r, 8 + 8 * r))
        rests[0, at, :], rests[1, at, :] = split_f32(res)
        for a in range(8 * r, 8 * r + 8):
            mask = upper[8 * a : 8 * a + 8, :]
            lhs[:, 128 * a : 128 * a + 128] = jnp.concatenate(
                [mask * spread(rests[i, a : a + 1, :]) for i in range(2)], axis=0
            ).astype(BF16)
    def from_here(i, row, towards):
        row = spread(row)
        out = jnp.zeros((8, 128), F32)
        for k in range(3):
            p = spread(hr[i, 10 + k : 11 + k, :]).astype(I32)
            term = spread(hr[i, 13 + k : 14 + k, :]) * take(row, p & 127)
            out = out + jnp.where(towards(p), term, 0.0)
        both = dot(jnp.concatenate(list(split_f32(out)), axis=0).astype(BF16), hot_n[i], NT)
        return both[0:1] + both[8:9]

    extra_l = from_here(0, smp[8:9, :], lambda p: p > 127)
    extra_r = from_here(1, smp[71:72, :], lambda p: p < 0)
    for r in range(2):
        where = slice(4096 * r, 4096 * r + 4096)
        seg[r] = dot(lhs[:, where], hot[where, :], NN)
    source = (seg[0, 0:8] + seg[0, 8:16]) + (seg[1, 0:8] + seg[1, 8:16])
    cs_s[...] = source
    cs_copies = pair(cs_s, cs_r, cs_s, cs_l, cs_ss, cs_rs)
    for c in cs_copies:
        c.start()

    cs[...] = jnp.zeros((24, 128), F32)
    cs[2:3, :] = extra_l
    cs[3:11, :] = source
    cs[11:12, :] = extra_r
    cf[...] = jnp.zeros((24, 128), F32)
    cs2[...] = jnp.zeros((24, 128), F32)
    cf[0:16, :] = cs[0:16, :] * e_s[0:16, :]

    def coarse_neighbours(ref):
        out = None
        for k in range(3):
            term = eedge[k] * pick(
                ref[0:16, :], ref[1:17, :], ref[2:18, :], etab[k].astype(I32)
            )
            out = term if out is None else out + term
        return out

    left_over = cs[1:17, :] - e_d[1:17, :] * cf[1:17, :] + coarse_neighbours(cf)
    klhs[...] = jnp.zeros((8, 1536), F32)
    for r in range(12):
        klhs[0:1, 128 * r : 128 * r + 128] = left_over[r : r + 1]
    packed = jnp.concatenate(list(split_f32(klhs[...])), axis=0).astype(BF16)
    for r in range(2):
        where = slice(768 * r, 768 * r + 768)
        segk[r] = dot(packed[:, where], khot[:, where], NT)
    pay[0] = (segk[0, 0:1] + segk[0, 8:9]) + (segk[1, 0:1] + segk[1, 8:9])
    gb[t] = pay[0]

    hops = (0, 1, 2, 1)
    others = sorted(
        ((a, b, c) for a in range(4) for b in range(4) for c in range(4)),
        key=lambda d: (
            d == (0, 0, 0), (d[1], d[2]) != (1, 1), -(hops[d[0]] + hops[d[1]] + hops[d[2]])
        ),
    )[:-1]
    for a, b, c in others:
        pltpu.make_async_remote_copy(
            src_ref=pay,
            dst_ref=gb.at[pl.ds(t, 1)],
            send_sem=ag_ss,
            recv_sem=ag_rs,
            device_id=(g, xs[a] + zs[b] + ys[c]),
            device_id_type=MESH,
        ).start()

    inv_copies[1].wait_recv()
    halves(16, invr[0])
    for c in sm_copies:
        c.wait_send()
        c.wait_recv()
    smp[7:8, :] = sm_l[7:8, :]
    smp[72:73, :] = sm_r[0:1, :]
    far_l, far_r = spread(sm_l[7:8, :]), spread(sm_r[0:1, :])
    more_l = more_r = jnp.zeros((8, 128), F32)
    for k in range(3):
        p = pos[k, 0:8, :]
        more_l = more_l + jnp.where(p < 0, edge[k, 0:8, :] * take(far_l, p & 127), 0.0)
        p = pos[k, 56:64, :]
        more_r = more_r + jnp.where(p > 127, edge[k, 56:64, :] * take(far_r, p & 127), 0.0)
    sums = dot(spot(more_l[0:1], fown[0:1, :]), hot[0:128, :], NN)
    sums = sums + dot(spot(more_r[7:8], fown[63:64, :]), hot[8064:8192, :], NN)
    more = sums[0:8] + sums[8:16]
    inv_copies[0].wait_recv()
    halves(32, invr[1])
    for c in cs_copies:
        c.wait_recv()
    cs[1:3, :] = cs_l[6:8, :] + cs[1:3, :]
    cs[3:11, :] = cs[3:11, :] + more
    cs[11:13, :] = cs_r[0:2, :] + cs[11:13, :]
    cf[0:16, :] = cs[0:16, :] * e_s[0:16, :]

    everyone = pltpu.make_async_remote_copy(
        src_ref=gb.at[pl.ds(0, n - 1)],
        dst_ref=gb.at[pl.ds(0, n - 1)],
        send_sem=ag_ss,
        recv_sem=ag_rs,
        device_id=(g, right),
        device_id_type=MESH,
    )
    everyone.wait_recv()
    from_right = (row8 == 0) & (lane8 >= 112)
    from_left = (row8 == 7) & (lane8 < 16)
    groups = [gb[8 * j : 8 * j + 8, 0, :] for j in range(8)]
    flat = []
    for j in range(8):
        mix = jnp.where(
            from_right, groups[(j + 1) % 8], jnp.where(from_left, groups[(j - 1) % 8], groups[j])
        )
        flat.append(jnp.sum(mix, axis=0, keepdims=True))
    flat = spread_all(jnp.concatenate(flat, axis=1))
    packed = jnp.concatenate(list(split_f32(flat)), axis=0).astype(BF16)
    by_h, by_l = dot(packed, inv_h[...], NT), dot(packed, inv_l[...], NT)
    value = (by_h[0:1] + by_h[8:9]) + (by_l[0:1] + by_l[8:9])
    value = jnp.concatenate([value, jnp.zeros((1, 80), F32)], axis=1)
    value = spread(value, 16)
    shift = jnp.where(row16 < 3, 16, jnp.where(row16 < 11, 0, 32))
    cs2[0:16, :] = cf[0:16, :] + take(value, jnp.minimum(e_o[0:16, :].astype(I32), 15) + shift)
    cur = cs2[1:17, :]
    rest = cs[1:17, :] - (e_d[1:17, :] * cur - coarse_neighbours(cs2))
    t3[...] = cur + rest * e_s[1:17, :]

    own_l = spread(hr[0, 9:10, :]).astype(I32) & 127
    own_r = spread(hr[1, 9:10, :]).astype(I32) & 127
    smp[7:8, :] = smp[7:8, :] + take(spread(t3[1:2, :]), own_l)[0:1]
    smp[72:73, :] = smp[72:73, :] + take(spread(t3[10:11, :]), own_r)[0:1]

    for c in halo_copies + surf_copies + inv_copies + cs_copies:
        c.wait_send()
    everyone.wait_send()

    @pl.when(seat == 3)
    def _():
        halo_on.wait_send()
        surf_on[0].wait_send()

    @pl.when(hands_on)
    def _():
        surf_on[1].wait_send()


def finish(
    newf, recv, smp, t3, base, pos, whole, scale, edge, fown, new_out, recv_out, height_out,
    cop, height, sems,
):
    copies = [
        pltpu.make_async_copy(source, target, sems.at[i])
        for i, (source, target) in enumerate(
            ((newf, new_out), (recv, recv_out), (height, height_out))
        )
    ]
    copies[0].start()
    copies[1].start()
    for r in range(8):
        at = slice(8 * r, 8 * r + 8)
        owner = fown[at, :]
        high, lane = owner >> 7, owner & 127
        out = smp[8 + 8 * r : 16 + 8 * r, :]
        for a in range(8):
            out = out + jnp.where(high == a, take(spread(t3[2 + a : 3 + a, :]), lane), 0.0)
        cop[8 + 8 * r : 16 + 8 * r, :] = out
    cop[7:8, :] = smp[7:8, :]
    cop[72:73, :] = smp[72:73, :]
    for r in range(8):
        at = slice(8 * r, 8 * r + 8)
        cur = cop[8 + 8 * r : 16 + 8 * r, :]
        rest = base[at, :] - (whole[at, :] * cur - beside_rows(cop, edge, pos, r))
        height[at, :] = cur + rest * scale[at, :]
    copies[2].start()
    for copy in copies:
        copy.wait()


def beside_rows(ref, edge, pos, r):
    out = None
    row = 8 + 8 * r
    prev, cur, nxt = ref[row - 1 : row + 7, :], ref[row : row + 8, :], ref[row + 1 : row + 9, :]
    for k in range(3):
        at = slice(8 * r, 8 * r + 8)
        term = edge[k, at, :] * pick(prev, cur, nxt, pos[k, at, :])
        out = term if out is None else out + term
    return out


def split_f32(x):
    high = x.astype(BF16).astype(F32)
    return high, x - high


def spread_all(row):
    return jnp.broadcast_to(row, (8, row.shape[1]))


def per_device(
    fields, level_rate, edge_weight, fine_diagonal, fine_table, old_height, level_weight,
    flux_weight, fine_owner, coarse_table, coarse_edge, coarse_diagonal, coarse_owner,
    coarse_inverse, surface_out, send_blocks, entry_slot, entry_block, remap_tiles,
):
    operands = (
        fields.reshape(8, 64, 128).transpose(1, 0, 2),
        level_rate,
        edge_weight.reshape(3, 64, 128),
        fine_diagonal.reshape(64, 128),
        fine_table.reshape(3, 64, 128),
        old_height.reshape(64, 128),
        level_weight,
        flux_weight,
        fine_owner.reshape(64, 128),
        coarse_table.reshape(3, 8, 128),
        coarse_edge.reshape(3, 8, 128),
        coarse_diagonal.reshape(8, 128),
        coarse_owner.reshape(8, 128),
        coarse_inverse.reshape(16, 1024),
        surface_out.reshape(4, 64, 128).transpose(1, 0, 2),
        send_blocks.reshape(1, 160),
        entry_slot.reshape(1, 160),
        entry_block.reshape(1, 160),
        remap_tiles.reshape(160, 128, 128),
    )
    vmem = pl.BlockSpec(memory_space=pltpu.VMEM)
    specs = [pl.BlockSpec(memory_space=pltpu.HBM)] * 19
    V = pltpu.VMEM
    local = [
        (pltpu.SMEM if i in (1, 6, 7, 15, 16) else V)(x.shape, x.dtype)
        for i, x in enumerate(operands)
        if i not in (2, 8)
    ]
    shape = jax.ShapeDtypeStruct
    D = pltpu.SemaphoreType.DMA
    made = pl.pallas_call(
        kernel,
        out_shape=(
            shape((64, 8, 128), F32),
            shape((256, 128), F32),
            shape((80, 128), F32),
            shape((16, 128), F32),
            shape((64, 128), F32),
            shape((3, 64, 128), I32),
            shape((64, 128), F32),
            shape((64, 128), F32),
            shape((3, 64, 128), F32),
            shape((64, 128), I32),
        ),
        in_specs=specs,
        out_specs=(vmem,) * 10,
        scratch_shapes=[
            *local,
            V((160, 4, 128), BF16),
            V((160, 4, 128), BF16),
            V((2, 32, 128), F32),
            V((2, 32, 128), F32),
            V((2, 16, 1024), F32),
            V((8, 128), F32),
            V((8, 128), F32),
            V((8, 128), F32),
            V((8, 128), F32),
            V((1, 1, 128), F32),
            V((8, 128), F32),
            V((64, 1, 128), F32),
            V((64, 160), BF16),
            V((640, 128), F32),
            V((640, 128), F32),
            V((8192, 128), BF16),
            V((512, 128), F32),
            V((2, 64, 128), F32),
            V((16, 8192), BF16),
            V((2, 16, 128), F32),
            V((80, 128), F32),
            V((3, 16, 128), F32),
            V((3, 16, 128), F32),
            V((24, 128), F32),
            V((24, 128), F32),
            V((24, 128), F32),
            V((16, 128), I32),
            V((24, 128), F32),
            V((24, 128), F32),
            V((24, 128), F32),
            V((128, 1536), BF16),
            V((8, 1536), F32),
            V((2, 128, 128), BF16),
            V((3, 64, 128), F32),
            V((48, 1024), BF16),
            V((48, 1024), BF16),
            V((2, 16, 128), F32),
            V((2, 32, 4, 128), BF16),
            V((32, 128), F32),
            D((18,)),
            D((4,)),
            D((5,)), D((5,)),
            D((2,)), D((2,)),
            D((2,)), D((2,)),
            D((2,)), D((2,)),
            D((2,)), D((2,)),
            D, D,
            pltpu.SemaphoreType.REGULAR, pltpu.SemaphoreType.REGULAR,
            D((2,)), D((2,)), D, D,
        ],
        compiler_params=pltpu.CompilerParams(
            collective_id=0, has_side_effects=True, vmem_limit_bytes=48 << 20
        ),
        name="step",
    )(*[pltpu.with_memory_space_constraint(x, pltpu.HBM) for x in operands])
    new, got, high = pl.pallas_call(
        finish,
        out_shape=(shape((64, 8, 128), F32), shape((256, 128), F32), shape((64, 128), F32)),
        in_specs=[vmem] * 10,
        out_specs=[pl.BlockSpec(memory_space=pltpu.HBM)] * 3,
        scratch_shapes=[V((80, 128), F32), V((64, 128), F32), D((3,))],
        compiler_params=pltpu.CompilerParams(vmem_limit_bytes=1 << 20),
        name="finish",
    )(*made)
    return (
        new.transpose(1, 0, 2).reshape(1, 8, 8192),
        got.reshape(64, 4, 128).transpose(1, 0, 2).reshape(1, 4, 8192),
        high.reshape(1, 8192),
    )


def solution(mesh):
    in_specs = (
        P("comp", None, "tile"),
        P("comp", None),
        P("comp", None, "tile"),
        P("comp", "tile"),
        P("comp", None, "tile"),
        P("comp", "tile"),
        P("comp", None),
        P("comp", None),
        P("comp", "tile"),
        P("comp", None, "tile"),
        P("comp", None, "tile"),
        P("comp", "tile"),
        P("comp", "tile"),
        P("comp", "tile", None),
        P("comp", None, "tile"),
        P("comp", "tile", None),
        P("comp", "tile", None),
        P("comp", "tile", None),
        P("comp", "tile", None, None, None),
    )
    out_specs = (P("comp", None, "tile"), P("comp", None, "tile"), P("comp", "tile"))
    return jax.shard_map(
        per_device, mesh=mesh, in_specs=in_specs, out_specs=out_specs, check_vma=False
    )
```

```python
import functools

import jax
import jax.numpy as jnp
from jax import lax
from jax.experimental import pallas as pl
from jax.experimental.pallas import tpu as pltpu
from jax.sharding import PartitionSpec as P

MESH = pl.DeviceIdType.MESH
F32, BF16, I32 = jnp.float32, jnp.bfloat16, jnp.int32
RELAX = 0.8
NT = (((1,), (1,)), ((), ()))
NN = (((1,), (0,)), ((), ()))


def take(x, lane):
    return jnp.take_along_axis(x, lane, axis=1, mode="promise_in_bounds")


def pick(prev, cur, nxt, pos):
    lane = pos & 127
    return jnp.where(
        pos < 0, take(prev, lane), jnp.where(pos > 127, take(nxt, lane), take(cur, lane))
    )


def spread(row, count=8):
    return jnp.broadcast_to(row, (count, 128))


def iota(shape, dim):
    return lax.broadcasted_iota(I32, shape, dim)


def split(x):
    high = x.astype(BF16)
    return high, (x - high.astype(F32)).astype(BF16)


def dot(a, b, dims):
    return lax.dot_general(a, b, dims, preferred_element_type=F32)


def kernel(
    *refs,
):
    inputs, outputs, rest = refs[:19], refs[19:29], refs[29:]
    local, scratch = list(rest[:17]), rest[17:]
    for i, ref in zip((2, 8), outputs[8:]):
        local.insert(i, ref)
    step(*local, *outputs[:8], inputs, local, *scratch)


def step(
    fields, rate_s, edge, fdiag, ftab, oldh, lw_s, fw_s, fown, ctab, cedge, cdiag, cown,
    cinv, surf, sendb, eslot, eblk, tl,
    newf, recv, smp, t3, base, pos, whole, scale, inputs, local,
    outg, inc, hs, hr, invr, sm_l, sm_r, cs_l, cs_r, pay, cs_s, gb, member, picks, prod,
    hot, upper, rests, lhs, seg, oldp, etab, eedge, e_d, e_s, e_o, key, cs, cf, cs2, khot, klhs, hot_n, shares,
    inv_h, inv_l, segk, rl, rh,
    in_sem, tile_sem, surf_ss, surf_rs, halo_ss, halo_rs, inv_ss, inv_rs, sm_ss, sm_rs, cs_ss, cs_rs,
    ag_ss, ag_rs, plane_sem, space_sem, rl_ss, rl_rs, rh_ss, rh_rs,
):
    g = lax.axis_index("comp")
    t = lax.axis_index("tile")
    n = lax.axis_size("tile")
    left, right = lax.rem(t + n - 1, n), lax.rem(t + 1, n)
    seat, back = lax.rem(t, 16), lax.rem(t + n - 16, n)
    y, z, x = lax.rem(t, 4), lax.rem(lax.div(t, 4), 4), lax.div(t, 16)
    ys = [lax.rem(y + d, 4) for d in range(4)]
    zs = [4 * lax.rem(z + d, 4) for d in range(4)]
    xs = [16 * lax.rem(x + d, 4) for d in range(4)]
    ring_y = [xs[0] + zs[0] + ys[d] for d in (1, 2, 3)]
    ring_z = [xs[0] + zs[d] + ys[0] for d in (1, 2, 3)]
    ring_x = [xs[d] + zs[0] + ys[0] for d in (1, 2, 3)]
    bar = pltpu.get_barrier_semaphore()

    def signal(sem, group, tile):
        pl.semaphore_signal(sem, inc=1, device_id=(group, tile), device_id_type=MESH)

    loads = [
        pltpu.make_async_copy(inputs[i], local[i], in_sem.at[i]) for i in range(18)
    ]
    for i in (15, 14, 0, 5, 8, 9, 10, 11, 12, 4, 2, 1, 6, 7, 17, 3, 16, 13):
        loads[i].start()
    def greet(ok, group, tile):
        if ok is None:
            signal(bar, group, tile)
        else:
            pl.when(ok)(functools.partial(signal, bar, group, tile))

    for d, ok in ((-2, seat < 14), (2, None), (-1, seat < 15), (1, None)):
        greet(ok, 1 - g, lax.rem(t + n - d, n))
    greet(None, g, left)
    greet(seat < 15, g, right)
    greet(seat < 2, 1 - g, lax.rem(t + 16, n))
    for tile in (*ring_y, *ring_z, *ring_x):
        signal(bar, g, tile)
    signal(bar, 1 - g, t)

    tiles = inputs[18]
    chunks = 4
    per = 160 // chunks
    tile_copies = [
        pltpu.make_async_copy(
            tiles.at[pl.ds(c * per, per)], tl.at[pl.ds(c * per, per)], tile_sem.at[c]
        )
        for c in range(chunks)
    ]
    for c in tile_copies:
        c.start()

    def ready(*which):
        for i in which:
            loads[i].wait()

    ready(15, 14)

    def gather(i, carry):
        for a in range(8):
            s = i * 8 + a
            outg[s] = surf[jnp.minimum(sendb[0, s], 63)]
        return carry

    lax.fori_loop(0, 20, gather, 0)

    ready(0, 5, 8, 9, 10, 11, 12, 4, 2)
    row8 = iota((8, 128), 0)
    cpos = [ctab[k] - 16 - 128 * row8 for k in range(3)]
    csum = cedge[0] + cedge[1] + cedge[2]
    c_d = cdiag[...] + csum
    for k in range(3):
        etab[k, 2:10, :] = cpos[k].astype(F32)
        etab[k, 12:16, :] = jnp.zeros((4, 128), F32)
        eedge[k, 2:10, :] = cedge[k]
        eedge[k, 12:16, :] = jnp.zeros((4, 128), F32)
    e_d[...] = jnp.ones((24, 128), F32)
    e_d[3:11, :] = c_d
    e_o[...] = jnp.zeros((24, 128), F32)
    e_o[3:11, :] = cown[...].astype(F32)
    for side, block, low in ((0, 0, 0), (1, 63, 6)):
        hs[side, 0:8, :] = fields[block]
        hs[side, 8:9, :] = oldh[block : block + 1, :]
        hs[side, 9:10, :] = fown[block : block + 1, :].astype(F32)
        for k in range(3):
            here = ftab[k, block : block + 1, :] - (128 + 128 * block)
            hs[side, 10 + k : 11 + k, :] = here.astype(F32)
            hs[side, 13 + k : 14 + k, :] = edge[k, block : block + 1, :]
        for k in range(3):
            hs[side, 16 + 2 * k : 18 + 2 * k, :] = etab[k, 2 + low : 4 + low, :]
            hs[side, 22 + 2 * k : 24 + 2 * k, :] = cedge[k, low : low + 2, :]
        hs[side, 28:30, :] = e_d[3 + low : 5 + low, :]
        hs[side, 30:32, :] = e_o[3 + low : 5 + low, :]

    pl.semaphore_wait(bar, jnp.where(seat == 0, 14, 16))

    surf_copies = [
        pltpu.make_async_remote_copy(
            src_ref=outg.at[pl.ds(32 * j, 32)],
            dst_ref=inc.at[pl.ds(32 * j, 32)],
            send_sem=surf_ss.at[j],
            recv_sem=surf_rs.at[j],
            device_id=(1 - g, lax.rem(t + n + 2 - j, n)),
            device_id_type=MESH,
        )
        for j in range(5)
    ]

    def pair(to_left, at_right, to_right, at_left, ss, rs):
        return [
            pltpu.make_async_remote_copy(
                src_ref=to_left, dst_ref=at_right, send_sem=ss.at[0], recv_sem=rs.at[0],
                device_id=(g, left), device_id_type=MESH,
            ),
            pltpu.make_async_remote_copy(
                src_ref=to_right, dst_ref=at_left, send_sem=ss.at[1], recv_sem=rs.at[1],
                device_id=(g, right), device_id_type=MESH,
            ),
        ]

    halo_copies = pair(hs.at[0], hr.at[1], hs.at[1], hr.at[0], halo_ss, halo_rs)
    inv_copies = pair(inputs[13], invr.at[1], inputs[13], invr.at[0], inv_ss, inv_rs)
    def relayed(source, landing, ss, rs, group):
        return pltpu.make_async_remote_copy(
            src_ref=source, dst_ref=landing, send_sem=ss, recv_sem=rs,
            device_id=(group, back), device_id_type=MESH,
        )

    def handed(source, landing, ss, rs, ahead):
        return pltpu.make_async_remote_copy(
            src_ref=source, dst_ref=landing, send_sem=ss, recv_sem=rs,
            device_id=(g, lax.rem(t + ahead, n)), device_id_type=MESH,
        )

    surf_in = [
        relayed(
            outg.at[pl.ds(32 * j, 32)], rl.at[j - 3], surf_ss.at[j], rl_rs.at[j - 3], 1 - g
        )
        for j in (3, 4)
    ]
    surf_on = [
        handed(
            rl.at[j - 3], inc.at[pl.ds(32 * j, 32)], rl_ss.at[j - 3], surf_rs.at[j], 18 - j
        )
        for j in (3, 4)
    ]
    halo_in = relayed(hs.at[0], rh, halo_ss.at[0], rh_rs, g)
    halo_on = handed(rh, hr.at[1], rh_ss, halo_rs.at[0], 15)

    def either(ok, direct, other):
        pl.when(ok)(direct.start)
        pl.when(jnp.logical_not(ok))(other.start)

    either(seat >= 1, halo_copies[0], halo_in)
    halo_copies[1].start()
    either(seat >= 2, surf_copies[4], surf_in[1])
    surf_copies[0].start()
    either(seat >= 1, surf_copies[3], surf_in[0])
    surf_copies[1].start()
    surf_copies[2].start()
    for tile in ring_z:
        signal(plane_sem, g, tile)

    ready(1, 6, 7, 17, 3, 16, 13)
    def positions(i, carry):
        at = pl.ds(pl.multiple_of(i * 8, 8), 8)
        total = edge[0, at, :] + edge[1, at, :] + edge[2, at, :]
        share = 1.0 / total
        whole[at, :] = fdiag[at, :] + total
        scale[at, :] = RELAX / whole[at, :]
        for k in range(3):
            pos[k, at, :] = ftab[k, at, :] - 128 - 128 * (i * 8 + row8)
            shares[k, at, :] = edge[k, at, :] * share
        return carry

    lax.fori_loop(0, 8, positions, 0)

    def column(ref, count):
        out = jnp.zeros((8, 128), F32)
        for level in range(count):
            out = jnp.where(row8 == level, ref[0, level], out)
        return out

    rates, weights = column(rate_s, 8), column(lw_s, 8)

    def advance(j, prev, cur, nxt):
        beside = None
        for k in range(3):
            p = spread(pos[k, pl.ds(j, 1), :])
            w = spread(shares[k, pl.ds(j, 1), :])
            term = w * pick(prev, cur, nxt, p)
            beside = term if beside is None else beside + term
        new = cur + rates * (beside - cur)
        newf[j] = new
        base[pl.ds(j, 1), :] = jnp.sum(weights * new, axis=0, keepdims=True)

    def advance8(i, carry):
        for a in range(8):
            j = i * 8 + a
            advance(j, fields[j - 1], fields[j], fields[j + 1])
        return carry

    lax.fori_loop(1, 7, advance8, 0)
    for j in (*range(1, 8), *range(56, 63)):
        advance(j, fields[j - 1], fields[j], fields[j + 1])

    lane8 = iota((8, 128), 1)
    blocks = iota((64, 160), 0)
    member[...] = jnp.where(
        blocks == jnp.broadcast_to(eblk[...], (64, 160)), 1.0, 0.0
    ).astype(BF16)

    down = iota((128, 128), 0)
    pl.semaphore_wait(plane_sem, 3)
    for tile in ring_x:
        signal(space_sem, g, tile)

    @pl.when(seat == 0)
    def _():
        halo_in.wait_recv()
        halo_on.start()
        surf_in[0].wait_recv()
        surf_on[0].start()

    @pl.when(seat < 2)
    def _():
        surf_in[1].wait_recv()
        surf_on[1].start()

    across = iota((128, 128), 1).astype(F32)
    lanes = (fown[...] & 127).astype(F32)
    column = jnp.transpose(jnp.concatenate([lanes, lanes], axis=0))
    for r in range(64):
        at = slice(128 * r, 128 * r + 128)
        mine = jnp.broadcast_to(column[:, r : r + 1], (128, 128))
        hot[at, :] = jnp.where(across == mine, 1.0, 0.0).astype(BF16)
        upper[8 * r : 8 * r + 8, :] = jnp.where(
            spread(fown[r : r + 1, :] >> 7) == row8, 1.0, 0.0
        )
    row16 = iota((16, 128), 0)
    side = jnp.where(row16 < 2, 7, jnp.where(row16 >= 10, 1, 0))

    def mark_owners(rows):
        key[...] = ((t + side) & 7) * 16 + e_o[1:17, :].astype(I32)
        for r in rows:
            khot[:, 128 * r : 128 * r + 128] = jnp.where(
                down == spread(key[r : r + 1, :], 128), 1.0, 0.0
            ).astype(BF16)

    mark_owners(range(2, 10))
    for c in halo_copies:
        c.wait_recv()
    for c in surf_copies:
        c.wait_recv()
    for c in tile_copies:
        c.wait()

    quarter = row16 // 4
    for i in range(40):
        at = slice(16 * i, 16 * i + 16)
        for e in range(4 * i, 4 * i + 4):
            picks[4 * e : 4 * e + 4, :] = inc[eslot[0, e]].astype(F32)
        rows = picks[at, :]
        ab = jnp.where(quarter < 2, rows, 0.0).astype(BF16)
        cd = jnp.where(quarter < 2, 0.0, rows).astype(BF16)
        four = tl[4 * i : 4 * i + 4]
        out = dot(
            jnp.concatenate([ab, cd], axis=1),
            jnp.concatenate(
                [four[0:2].reshape(256, 128), four[2:4].reshape(256, 128)], axis=1
            ),
            NT,
        )
        prod[at, :] = jnp.where(quarter % 2 == 0, out[:, 0:128], out[:, 128:256])

    advance(0, hr[0, 0:8, :], fields[0], fields[1])
    advance(63, fields[62], fields[63], hr[1, 0:8, :])
    oldp[7:8, :] = hr[0, 8:9, :]
    oldp[8:72, :] = oldh[...]
    oldp[72:73, :] = hr[1, 8:9, :]
    def neighbours(ref, r, _):
        return beside_rows(ref, edge, pos, r)

    for r in range(8):
        at = slice(8 * r, 8 * r + 8)
        smp[8 + 8 * r : 16 + 8 * r, :] = neighbours(oldp, r, 8 + 8 * r)

    def halves(at, block):
        inv_h[at : at + 16, :], inv_l[at : at + 16, :] = split(block)

    halves(0, cinv[...])
    for k in range(3):
        etab[k, 0:2, :] = hr[0, 16 + 2 * k : 18 + 2 * k, :]
        etab[k, 10:12, :] = hr[1, 16 + 2 * k : 18 + 2 * k, :]
        eedge[k, 0:2, :] = hr[0, 22 + 2 * k : 24 + 2 * k, :]
        eedge[k, 10:12, :] = hr[1, 22 + 2 * k : 24 + 2 * k, :]
    e_d[1:3, :] = hr[0, 28:30, :]
    e_d[11:13, :] = hr[1, 28:30, :]
    e_s[...] = RELAX / e_d[...]
    e_o[1:3, :] = hr[0, 30:32, :]
    e_o[11:13, :] = hr[1, 30:32, :]
    mark_owners((0, 1, 10, 11))
    for i in range(2):
        owner = spread(hr[i, 9:10, :], 128).astype(I32) & 127
        hot_n[i] = jnp.where(down == owner, 1.0, 0.0).astype(BF16)
    for f in range(4):
        high, low = split(prod[pl.ds(f, 160, stride=4), :])
        both = dot(member[...], jnp.concatenate([high, low], axis=1), NN)
        recv[pl.ds(f, 64, stride=4), :] = both[:, 0:128] + both[:, 128:256]

    for r in range(8):
        at = slice(8 * r, 8 * r + 8)
        out = base[at, :]
        for f in range(4):
            out = out + fw_s[0, f] * recv[pl.ds(32 * r + f, 8, stride=4), :]
        base[at, :] = out
        prev = oldh[at, :]
        beside = smp[8 + 8 * r : 16 + 8 * r, :]
        smp[8 + 8 * r : 16 + 8 * r, :] = (
            prev + (out - (whole[at, :] * prev - beside)) * scale[at, :]
        )

    pl.semaphore_wait(space_sem, 3)
    sm_copies = pair(smp.at[pl.ds(8, 8)], sm_r, smp.at[pl.ds(64, 8)], sm_l, sm_ss, sm_rs)
    for c in sm_copies:
        c.start()
    for c in inv_copies:
        c.start()
    smp[7:8, :] = jnp.zeros((1, 128), F32)
    smp[72:73, :] = jnp.zeros((1, 128), F32)

    def spot(row, owner):
        mine = jnp.where(spread(owner >> 7) == row8, spread(row), 0.0)
        return jnp.concatenate(list(split_f32(mine)), axis=0).astype(BF16)

    for r in range(8):
        at = slice(8 * r, 8 * r + 8)
        cur = smp[8 + 8 * r : 16 + 8 * r, :]
        res = base[at, :] - (whole[at, :] * cur - neighbours(smp, r, 8 + 8 * r))
        rests[0, at, :], rests[1, at, :] = split_f32(res)
        for a in range(8 * r, 8 * r + 8):
            mask = upper[8 * a : 8 * a + 8, :]
            lhs[:, 128 * a : 128 * a + 128] = jnp.concatenate(
                [mask * spread(rests[i, a : a + 1, :]) for i in range(2)], axis=0
            ).astype(BF16)
    def from_here(i, row, towards):
        row = spread(row)
        out = jnp.zeros((8, 128), F32)
        for k in range(3):
            p = spread(hr[i, 10 + k : 11 + k, :]).astype(I32)
            term = spread(hr[i, 13 + k : 14 + k, :]) * take(row, p & 127)
            out = out + jnp.where(towards(p), term, 0.0)
        both = dot(jnp.concatenate(list(split_f32(out)), axis=0).astype(BF16), hot_n[i], NT)
        return both[0:1] + both[8:9]

    extra_l = from_here(0, smp[8:9, :], lambda p: p > 127)
    extra_r = from_here(1, smp[71:72, :], lambda p: p < 0)
    for r in range(2):
        where = slice(4096 * r, 4096 * r + 4096)
        seg[r] = dot(lhs[:, where], hot[where, :], NN)
    source = (seg[0, 0:8] + seg[0, 8:16]) + (seg[1, 0:8] + seg[1, 8:16])
    cs_s[...] = source
    cs_copies = pair(cs_s, cs_r, cs_s, cs_l, cs_ss, cs_rs)
    for c in cs_copies:
        c.start()

    cs[...] = jnp.zeros((24, 128), F32)
    cs[2:3, :] = extra_l
    cs[3:11, :] = source
    cs[11:12, :] = extra_r
    cf[...] = jnp.zeros((24, 128), F32)
    cs2[...] = jnp.zeros((24, 128), F32)
    cf[0:16, :] = cs[0:16, :] * e_s[0:16, :]

    def coarse_neighbours(ref):
        out = None
        for k in range(3):
            term = eedge[k] * pick(
                ref[0:16, :], ref[1:17, :], ref[2:18, :], etab[k].astype(I32)
            )
            out = term if out is None else out + term
        return out

    left_over = cs[1:17, :] - e_d[1:17, :] * cf[1:17, :] + coarse_neighbours(cf)
    klhs[...] = jnp.zeros((8, 1536), F32)
    for r in range(12):
        klhs[0:1, 128 * r : 128 * r + 128] = left_over[r : r + 1]
    packed = jnp.concatenate(list(split_f32(klhs[...])), axis=0).astype(BF16)
    for r in range(2):
        where = slice(768 * r, 768 * r + 768)
        segk[r] = dot(packed[:, where], khot[:, where], NT)
    pay[0] = (segk[0, 0:1] + segk[0, 8:9]) + (segk[1, 0:1] + segk[1, 8:9])
    gb[t] = pay[0]

    hops = (0, 1, 2, 1)
    others = sorted(
        ((a, b, c) for a in range(4) for b in range(4) for c in range(4)),
        key=lambda d: (
            d == (0, 0, 0), (d[1], d[2]) != (1, 1), -(hops[d[0]] + hops[d[1]] + hops[d[2]])
        ),
    )[:-1]
    for a, b, c in others:
        pltpu.make_async_remote_copy(
            src_ref=pay,
            dst_ref=gb.at[pl.ds(t, 1)],
            send_sem=ag_ss,
            recv_sem=ag_rs,
            device_id=(g, xs[a] + zs[b] + ys[c]),
            device_id_type=MESH,
        ).start()

    for c in sm_copies:
        c.wait_send()
        c.wait_recv()
    smp[7:8, :] = sm_l[7:8, :]
    smp[72:73, :] = sm_r[0:1, :]
    far_l, far_r = spread(sm_l[7:8, :]), spread(sm_r[0:1, :])
    more_l = more_r = jnp.zeros((8, 128), F32)
    for k in range(3):
        p = pos[k, 0:8, :]
        more_l = more_l + jnp.where(p < 0, edge[k, 0:8, :] * take(far_l, p & 127), 0.0)
        p = pos[k, 56:64, :]
        more_r = more_r + jnp.where(p > 127, edge[k, 56:64, :] * take(far_r, p & 127), 0.0)
    sums = dot(spot(more_l[0:1], fown[0:1, :]), hot[0:128, :], NN)
    sums = sums + dot(spot(more_r[7:8], fown[63:64, :]), hot[8064:8192, :], NN)
    more = sums[0:8] + sums[8:16]
    for c in cs_copies:
        c.wait_recv()
    cs[1:3, :] = cs_l[6:8, :] + cs[1:3, :]
    cs[3:11, :] = cs[3:11, :] + more
    cs[11:13, :] = cs_r[0:2, :] + cs[11:13, :]
    cf[0:16, :] = cs[0:16, :] * e_s[0:16, :]

    inv_copies[0].wait_recv()
    halves(32, invr[1])
    inv_copies[1].wait_recv()
    halves(16, invr[0])
    everyone = pltpu.make_async_remote_copy(
        src_ref=gb.at[pl.ds(0, n - 1)],
        dst_ref=gb.at[pl.ds(0, n - 1)],
        send_sem=ag_ss,
        recv_sem=ag_rs,
        device_id=(g, right),
        device_id_type=MESH,
    )
    everyone.wait_recv()
    from_right = (row8 == 0) & (lane8 >= 112)
    from_left = (row8 == 7) & (lane8 < 16)
    groups = [gb[8 * j : 8 * j + 8, 0, :] for j in range(8)]
    flat = []
    for j in range(8):
        mix = jnp.where(
            from_right, groups[(j + 1) % 8], jnp.where(from_left, groups[(j - 1) % 8], groups[j])
        )
        flat.append(jnp.sum(mix, axis=0, keepdims=True))
    flat = spread_all(jnp.concatenate(flat, axis=1))
    packed = jnp.concatenate(list(split_f32(flat)), axis=0).astype(BF16)
    by_h, by_l = dot(packed, inv_h[...], NT), dot(packed, inv_l[...], NT)
    value = (by_h[0:1] + by_h[8:9]) + (by_l[0:1] + by_l[8:9])
    value = jnp.concatenate([value, jnp.zeros((1, 80), F32)], axis=1)
    value = spread(value, 16)
    shift = jnp.where(row16 < 3, 16, jnp.where(row16 < 11, 0, 32))
    cs2[0:16, :] = cf[0:16, :] + take(value, jnp.minimum(e_o[0:16, :].astype(I32), 15) + shift)
    cur = cs2[1:17, :]
    rest = cs[1:17, :] - (e_d[1:17, :] * cur - coarse_neighbours(cs2))
    t3[...] = cur + rest * e_s[1:17, :]

    own_l = spread(hr[0, 9:10, :]).astype(I32) & 127
    own_r = spread(hr[1, 9:10, :]).astype(I32) & 127
    smp[7:8, :] = smp[7:8, :] + take(spread(t3[1:2, :]), own_l)[0:1]
    smp[72:73, :] = smp[72:73, :] + take(spread(t3[10:11, :]), own_r)[0:1]

    for c in halo_copies + surf_copies + inv_copies + cs_copies:
        c.wait_send()
    everyone.wait_send()

    @pl.when(seat == 0)
    def _():
        halo_on.wait_send()
        surf_on[0].wait_send()

    @pl.when(seat < 2)
    def _():
        surf_on[1].wait_send()


def finish(
    newf, recv, smp, t3, base, pos, whole, scale, edge, fown, new_out, recv_out, height_out,
    cop, height, sems,
):
    copies = [
        pltpu.make_async_copy(source, target, sems.at[i])
        for i, (source, target) in enumerate(
            ((newf, new_out), (recv, recv_out), (height, height_out))
        )
    ]
    copies[0].start()
    copies[1].start()
    for r in range(8):
        at = slice(8 * r, 8 * r + 8)
        owner = fown[at, :]
        high, lane = owner >> 7, owner & 127
        out = smp[8 + 8 * r : 16 + 8 * r, :]
        for a in range(8):
            out = out + jnp.where(high == a, take(spread(t3[2 + a : 3 + a, :]), lane), 0.0)
        cop[8 + 8 * r : 16 + 8 * r, :] = out
    cop[7:8, :] = smp[7:8, :]
    cop[72:73, :] = smp[72:73, :]
    for r in range(8):
        at = slice(8 * r, 8 * r + 8)
        cur = cop[8 + 8 * r : 16 + 8 * r, :]
        rest = base[at, :] - (whole[at, :] * cur - beside_rows(cop, edge, pos, r))
        height[at, :] = cur + rest * scale[at, :]
    copies[2].start()
    for copy in copies:
        copy.wait()


def beside_rows(ref, edge, pos, r):
    out = None
    row = 8 + 8 * r
    prev, cur, nxt = ref[row - 1 : row + 7, :], ref[row : row + 8, :], ref[row + 1 : row + 9, :]
    for k in range(3):
        at = slice(8 * r, 8 * r + 8)
        term = edge[k, at, :] * pick(prev, cur, nxt, pos[k, at, :])
        out = term if out is None else out + term
    return out


def split_f32(x):
    high = x.astype(BF16).astype(F32)
    return high, x - high


def spread_all(row):
    return jnp.broadcast_to(row, (8, row.shape[1]))


def per_device(
    fields, level_rate, edge_weight, fine_diagonal, fine_table, old_height, level_weight,
    flux_weight, fine_owner, coarse_table, coarse_edge, coarse_diagonal, coarse_owner,
    coarse_inverse, surface_out, send_blocks, entry_slot, entry_block, remap_tiles,
):
    operands = (
        fields.reshape(8, 64, 128).transpose(1, 0, 2),
        level_rate,
        edge_weight.reshape(3, 64, 128),
        fine_diagonal.reshape(64, 128),
        fine_table.reshape(3, 64, 128),
        old_height.reshape(64, 128),
        level_weight,
        flux_weight,
        fine_owner.reshape(64, 128),
        coarse_table.reshape(3, 8, 128),
        coarse_edge.reshape(3, 8, 128),
        coarse_diagonal.reshape(8, 128),
        coarse_owner.reshape(8, 128),
        coarse_inverse.reshape(16, 1024),
        surface_out.reshape(4, 64, 128).transpose(1, 0, 2),
        send_blocks.reshape(1, 160),
        entry_slot.reshape(1, 160),
        entry_block.reshape(1, 160),
        remap_tiles.reshape(160, 128, 128),
    )
    vmem = pl.BlockSpec(memory_space=pltpu.VMEM)
    specs = [pl.BlockSpec(memory_space=pltpu.HBM)] * 19
    V = pltpu.VMEM
    local = [
        (pltpu.SMEM if i in (1, 6, 7, 15, 16) else V)(x.shape, x.dtype)
        for i, x in enumerate(operands)
        if i not in (2, 8)
    ]
    shape = jax.ShapeDtypeStruct
    D = pltpu.SemaphoreType.DMA
    made = pl.pallas_call(
        kernel,
        out_shape=(
            shape((64, 8, 128), F32),
            shape((256, 128), F32),
            shape((80, 128), F32),
            shape((16, 128), F32),
            shape((64, 128), F32),
            shape((3, 64, 128), I32),
            shape((64, 128), F32),
            shape((64, 128), F32),
            shape((3, 64, 128), F32),
            shape((64, 128), I32),
        ),
        in_specs=specs,
        out_specs=(vmem,) * 10,
        scratch_shapes=[
            *local,
            V((160, 4, 128), BF16),
            V((160, 4, 128), BF16),
            V((2, 32, 128), F32),
            V((2, 32, 128), F32),
            V((2, 16, 1024), F32),
            V((8, 128), F32),
            V((8, 128), F32),
            V((8, 128), F32),
            V((8, 128), F32),
            V((1, 1, 128), F32),
            V((8, 128), F32),
            V((64, 1, 128), F32),
            V((64, 160), BF16),
            V((640, 128), F32),
            V((640, 128), F32),
            V((8192, 128), BF16),
            V((512, 128), F32),
            V((2, 64, 128), F32),
            V((16, 8192), BF16),
            V((2, 16, 128), F32),
            V((80, 128), F32),
            V((3, 16, 128), F32),
            V((3, 16, 128), F32),
            V((24, 128), F32),
            V((24, 128), F32),
            V((24, 128), F32),
            V((16, 128), I32),
            V((24, 128), F32),
            V((24, 128), F32),
            V((24, 128), F32),
            V((128, 1536), BF16),
            V((8, 1536), F32),
            V((2, 128, 128), BF16),
            V((3, 64, 128), F32),
            V((48, 1024), BF16),
            V((48, 1024), BF16),
            V((2, 16, 128), F32),
            V((2, 32, 4, 128), BF16),
            V((32, 128), F32),
            D((18,)),
            D((4,)),
            D((5,)), D((5,)),
            D((2,)), D((2,)),
            D((2,)), D((2,)),
            D((2,)), D((2,)),
            D((2,)), D((2,)),
            D, D,
            pltpu.SemaphoreType.REGULAR, pltpu.SemaphoreType.REGULAR,
            D((2,)), D((2,)), D, D,
        ],
        compiler_params=pltpu.CompilerParams(
            collective_id=0, has_side_effects=True, vmem_limit_bytes=48 << 20
        ),
        name="step",
    )(*[pltpu.with_memory_space_constraint(x, pltpu.HBM) for x in operands])
    new, got, high = pl.pallas_call(
        finish,
        out_shape=(shape((64, 8, 128), F32), shape((256, 128), F32), shape((64, 128), F32)),
        in_specs=[vmem] * 10,
        out_specs=[pl.BlockSpec(memory_space=pltpu.HBM)] * 3,
        scratch_shapes=[V((80, 128), F32), V((64, 128), F32), D((3,))],
        compiler_params=pltpu.CompilerParams(vmem_limit_bytes=1 << 20),
        name="finish",
    )(*made)
    return (
        new.transpose(1, 0, 2).reshape(1, 8, 8192),
        got.reshape(64, 4, 128).transpose(1, 0, 2).reshape(1, 4, 8192),
        high.reshape(1, 8192),
    )


def solution(mesh):
    in_specs = (
        P("comp", None, "tile"),
        P("comp", None),
        P("comp", None, "tile"),
        P("comp", "tile"),
        P("comp", None, "tile"),
        P("comp", "tile"),
        P("comp", None),
        P("comp", None),
        P("comp", "tile"),
        P("comp", None, "tile"),
        P("comp", None, "tile"),
        P("comp", "tile"),
        P("comp", "tile"),
        P("comp", "tile", None),
        P("comp", None, "tile"),
        P("comp", "tile", None),
        P("comp", "tile", None),
        P("comp", "tile", None),
        P("comp", "tile", None, None, None),
    )
    out_specs = (P("comp", None, "tile"), P("comp", None, "tile"), P("comp", "tile"))
    return jax.shard_map(
        per_device, mesh=mesh, in_specs=in_specs, out_specs=out_specs, check_vma=False
    )
```

```python
import functools

import jax
import jax.numpy as jnp
from jax import lax
from jax.experimental import pallas as pl
from jax.experimental.pallas import tpu as pltpu
from jax.sharding import PartitionSpec as P

MESH = pl.DeviceIdType.MESH
F32, BF16, I32 = jnp.float32, jnp.bfloat16, jnp.int32
RELAX = 0.8
NT = (((1,), (1,)), ((), ()))
NN = (((1,), (0,)), ((), ()))


def take(x, lane):
    return jnp.take_along_axis(x, lane, axis=1, mode="promise_in_bounds")


def pick(prev, cur, nxt, pos):
    lane = pos & 127
    return jnp.where(
        pos < 0, take(prev, lane), jnp.where(pos > 127, take(nxt, lane), take(cur, lane))
    )


def spread(row, count=8):
    return jnp.broadcast_to(row, (count, 128))


def iota(shape, dim):
    return lax.broadcasted_iota(I32, shape, dim)


def split(x):
    high = x.astype(BF16)
    return high, (x - high.astype(F32)).astype(BF16)


def dot(a, b, dims):
    return lax.dot_general(a, b, dims, preferred_element_type=F32)


def kernel(
    *refs,
):
    inputs, outputs, rest = refs[:19], refs[19:29], refs[29:]
    local, scratch = list(rest[:17]), rest[17:]
    for i, ref in zip((2, 8), outputs[8:]):
        local.insert(i, ref)
    step(*local, *outputs[:8], inputs, local, *scratch)


def step(
    fields, rate_s, edge, fdiag, ftab, oldh, lw_s, fw_s, fown, ctab, cedge, cdiag, cown,
    cinv, surf, sendb, eslot, eblk, tl,
    newf, recv, smp, t3, base, pos, whole, scale, inputs, local,
    outg, inc, hs, hr, invr, sm_l, sm_r, cs_l, cs_r, pay, cs_s, gb, member, picks, prod,
    hot, upper, rests, lhs, seg, oldp, etab, eedge, e_d, e_s, e_o, key, cs, cf, cs2, khot, klhs, hot_n, shares,
    inv_h, inv_l, segk, rl, rh,
    in_sem, tile_sem, surf_ss, surf_rs, halo_ss, halo_rs, inv_ss, inv_rs, sm_ss, sm_rs, cs_ss, cs_rs,
    ag_ss, ag_rs, plane_sem, space_sem, rl_ss, rl_rs, rh_ss, rh_rs,
):
    g = lax.axis_index("comp")
    t = lax.axis_index("tile")
    n = lax.axis_size("tile")
    left, right = lax.rem(t + n - 1, n), lax.rem(t + 1, n)
    seat, back = lax.rem(t, 16), lax.rem(t + n - 16, n)
    y, z, x = lax.rem(t, 4), lax.rem(lax.div(t, 4), 4), lax.div(t, 16)
    ys = [lax.rem(y + d, 4) for d in range(4)]
    zs = [4 * lax.rem(z + d, 4) for d in range(4)]
    xs = [16 * lax.rem(x + d, 4) for d in range(4)]
    ring_y = [xs[0] + zs[0] + ys[d] for d in (1, 2, 3)]
    ring_z = [xs[0] + zs[d] + ys[0] for d in (1, 2, 3)]
    ring_x = [xs[d] + zs[0] + ys[0] for d in (1, 2, 3)]
    bar = pltpu.get_barrier_semaphore()

    def signal(sem, group, tile):
        pl.semaphore_signal(sem, inc=1, device_id=(group, tile), device_id_type=MESH)

    loads = [
        pltpu.make_async_copy(inputs[i], local[i], in_sem.at[i]) for i in range(18)
    ]
    for i in (15, 14, 0, 5, 8, 9, 10, 11, 12, 4, 2, 1, 6, 7, 17, 3, 16, 13):
        loads[i].start()
    def greet(ok, group, tile):
        if ok is None:
            signal(bar, group, tile)
        else:
            pl.when(ok)(functools.partial(signal, bar, group, tile))

    for d, ok in ((-2, seat < 14), (2, None), (-1, seat < 15), (1, None)):
        greet(ok, 1 - g, lax.rem(t + n - d, n))
    greet(None, g, left)
    greet(seat < 15, g, right)
    greet(seat < 2, 1 - g, lax.rem(t + 16, n))
    for tile in (*ring_y, *ring_z, *ring_x):
        signal(bar, g, tile)
    signal(bar, 1 - g, t)

    tiles = inputs[18]
    chunks = 4
    per = 160 // chunks
    tile_copies = [
        pltpu.make_async_copy(
            tiles.at[pl.ds(c * per, per)], tl.at[pl.ds(c * per, per)], tile_sem.at[c]
        )
        for c in range(chunks)
    ]
    for c in tile_copies:
        c.start()

    def ready(*which):
        for i in which:
            loads[i].wait()

    ready(15, 14)

    def gather(i, carry):
        for a in range(8):
            s = i * 8 + a
            outg[s] = surf[jnp.minimum(sendb[0, s], 63)]
        return carry

    lax.fori_loop(0, 20, gather, 0)

    ready(0, 5, 8, 9, 10, 11, 12, 4, 2)
    row8 = iota((8, 128), 0)
    cpos = [ctab[k] - 16 - 128 * row8 for k in range(3)]
    csum = cedge[0] + cedge[1] + cedge[2]
    c_d = cdiag[...] + csum
    for k in range(3):
        etab[k, 2:10, :] = cpos[k].astype(F32)
        etab[k, 12:16, :] = jnp.zeros((4, 128), F32)
        eedge[k, 2:10, :] = cedge[k]
        eedge[k, 12:16, :] = jnp.zeros((4, 128), F32)
    e_d[...] = jnp.ones((24, 128), F32)
    e_d[3:11, :] = c_d
    e_o[...] = jnp.zeros((24, 128), F32)
    e_o[3:11, :] = cown[...].astype(F32)
    for side, block, low in ((0, 0, 0), (1, 63, 6)):
        hs[side, 0:8, :] = fields[block]
        hs[side, 8:9, :] = oldh[block : block + 1, :]
        hs[side, 9:10, :] = fown[block : block + 1, :].astype(F32)
        for k in range(3):
            here = ftab[k, block : block + 1, :] - (128 + 128 * block)
            hs[side, 10 + k : 11 + k, :] = here.astype(F32)
            hs[side, 13 + k : 14 + k, :] = edge[k, block : block + 1, :]
        for k in range(3):
            hs[side, 16 + 2 * k : 18 + 2 * k, :] = etab[k, 2 + low : 4 + low, :]
            hs[side, 22 + 2 * k : 24 + 2 * k, :] = cedge[k, low : low + 2, :]
        hs[side, 28:30, :] = e_d[3 + low : 5 + low, :]
        hs[side, 30:32, :] = e_o[3 + low : 5 + low, :]

    pl.semaphore_wait(bar, jnp.where(seat == 0, 14, 16))

    surf_copies = [
        pltpu.make_async_remote_copy(
            src_ref=outg.at[pl.ds(32 * j, 32)],
            dst_ref=inc.at[pl.ds(32 * j, 32)],
            send_sem=surf_ss.at[j],
            recv_sem=surf_rs.at[j],
            device_id=(1 - g, lax.rem(t + n + 2 - j, n)),
            device_id_type=MESH,
        )
        for j in range(5)
    ]

    def pair(to_left, at_right, to_right, at_left, ss, rs):
        return [
            pltpu.make_async_remote_copy(
                src_ref=to_left, dst_ref=at_right, send_sem=ss.at[0], recv_sem=rs.at[0],
                device_id=(g, left), device_id_type=MESH,
            ),
            pltpu.make_async_remote_copy(
                src_ref=to_right, dst_ref=at_left, send_sem=ss.at[1], recv_sem=rs.at[1],
                device_id=(g, right), device_id_type=MESH,
            ),
        ]

    halo_copies = pair(hs.at[0], hr.at[1], hs.at[1], hr.at[0], halo_ss, halo_rs)
    inv_copies = pair(inputs[13], invr.at[1], inputs[13], invr.at[0], inv_ss, inv_rs)
    def relayed(source, landing, ss, rs, group):
        return pltpu.make_async_remote_copy(
            src_ref=source, dst_ref=landing, send_sem=ss, recv_sem=rs,
            device_id=(group, back), device_id_type=MESH,
        )

    def handed(source, landing, ss, rs, ahead):
        return pltpu.make_async_remote_copy(
            src_ref=source, dst_ref=landing, send_sem=ss, recv_sem=rs,
            device_id=(g, lax.rem(t + ahead, n)), device_id_type=MESH,
        )

    surf_in = [
        relayed(
            outg.at[pl.ds(32 * j, 32)], rl.at[j - 3], surf_ss.at[j], rl_rs.at[j - 3], 1 - g
        )
        for j in (3, 4)
    ]
    surf_on = [
        handed(
            rl.at[j - 3], inc.at[pl.ds(32 * j, 32)], rl_ss.at[j - 3], surf_rs.at[j], 18 - j
        )
        for j in (3, 4)
    ]
    halo_in = relayed(hs.at[0], rh, halo_ss.at[0], rh_rs, g)
    halo_on = handed(rh, hr.at[1], rh_ss, halo_rs.at[0], 15)

    def either(ok, direct, other):
        pl.when(ok)(direct.start)
        pl.when(jnp.logical_not(ok))(other.start)

    either(seat >= 1, halo_copies[0], halo_in)
    halo_copies[1].start()
    either(seat >= 2, surf_copies[4], surf_in[1])
    surf_copies[0].start()
    either(seat >= 1, surf_copies[3], surf_in[0])
    surf_copies[1].start()
    surf_copies[2].start()
    for tile in ring_z:
        signal(plane_sem, g, tile)

    ready(1, 6, 7, 17, 3, 16, 13)
    def positions(i, carry):
        at = pl.ds(pl.multiple_of(i * 8, 8), 8)
        total = edge[0, at, :] + edge[1, at, :] + edge[2, at, :]
        share = 1.0 / total
        whole[at, :] = fdiag[at, :] + total
        scale[at, :] = RELAX / whole[at, :]
        for k in range(3):
            pos[k, at, :] = ftab[k, at, :] - 128 - 128 * (i * 8 + row8)
            shares[k, at, :] = edge[k, at, :] * share
        return carry

    lax.fori_loop(0, 8, positions, 0)

    def column(ref, count):
        out = jnp.zeros((8, 128), F32)
        for level in range(count):
            out = jnp.where(row8 == level, ref[0, level], out)
        return out

    rates, weights = column(rate_s, 8), column(lw_s, 8)

    def advance(j, prev, cur, nxt):
        beside = None
        for k in range(3):
            p = spread(pos[k, pl.ds(j, 1), :])
            w = spread(shares[k, pl.ds(j, 1), :])
            term = w * pick(prev, cur, nxt, p)
            beside = term if beside is None else beside + term
        new = cur + rates * (beside - cur)
        newf[j] = new
        base[pl.ds(j, 1), :] = jnp.sum(weights * new, axis=0, keepdims=True)

    def advance8(i, carry):
        for a in range(8):
            j = i * 8 + a
            advance(j, fields[j - 1], fields[j], fields[j + 1])
        return carry

    lax.fori_loop(1, 7, advance8, 0)
    for j in (*range(1, 8), *range(56, 63)):
        advance(j, fields[j - 1], fields[j], fields[j + 1])

    lane8 = iota((8, 128), 1)
    blocks = iota((64, 160), 0)
    member[...] = jnp.where(
        blocks == jnp.broadcast_to(eblk[...], (64, 160)), 1.0, 0.0
    ).astype(BF16)

    down = iota((128, 128), 0)
    pl.semaphore_wait(plane_sem, 3)
    for tile in ring_x:
        signal(space_sem, g, tile)

    @pl.when(seat == 0)
    def _():
        halo_in.wait_recv()
        halo_on.start()
        surf_in[0].wait_recv()
        surf_on[0].start()

    @pl.when(seat < 2)
    def _():
        surf_in[1].wait_recv()
        surf_on[1].start()

    across = iota((128, 128), 1).astype(F32)
    lanes = (fown[...] & 127).astype(F32)
    column = jnp.transpose(jnp.concatenate([lanes, lanes], axis=0))
    for r in range(64):
        at = slice(128 * r, 128 * r + 128)
        mine = jnp.broadcast_to(column[:, r : r + 1], (128, 128))
        hot[at, :] = jnp.where(across == mine, 1.0, 0.0).astype(BF16)
        upper[8 * r : 8 * r + 8, :] = jnp.where(
            spread(fown[r : r + 1, :] >> 7) == row8, 1.0, 0.0
        )
    row16 = iota((16, 128), 0)
    side = jnp.where(row16 < 2, 7, jnp.where(row16 >= 10, 1, 0))

    def mark_owners(rows):
        key[...] = ((t + side) & 7) * 16 + e_o[1:17, :].astype(I32)
        for r in rows:
            khot[:, 128 * r : 128 * r + 128] = jnp.where(
                down == spread(key[r : r + 1, :], 128), 1.0, 0.0
            ).astype(BF16)

    mark_owners(range(2, 10))
    for c in halo_copies:
        c.wait_recv()
    for c in surf_copies:
        c.wait_recv()
    for c in tile_copies:
        c.wait()

    inv_copies[1].start()
    quarter = row16 // 4
    for i in range(40):
        at = slice(16 * i, 16 * i + 16)
        for e in range(4 * i, 4 * i + 4):
            picks[4 * e : 4 * e + 4, :] = inc[eslot[0, e]].astype(F32)
        rows = picks[at, :]
        ab = jnp.where(quarter < 2, rows, 0.0).astype(BF16)
        cd = jnp.where(quarter < 2, 0.0, rows).astype(BF16)
        four = tl[4 * i : 4 * i + 4]
        out = dot(
            jnp.concatenate([ab, cd], axis=1),
            jnp.concatenate(
                [four[0:2].reshape(256, 128), four[2:4].reshape(256, 128)], axis=1
            ),
            NT,
        )
        prod[at, :] = jnp.where(quarter % 2 == 0, out[:, 0:128], out[:, 128:256])

    advance(0, hr[0, 0:8, :], fields[0], fields[1])
    advance(63, fields[62], fields[63], hr[1, 0:8, :])
    oldp[7:8, :] = hr[0, 8:9, :]
    oldp[8:72, :] = oldh[...]
    oldp[72:73, :] = hr[1, 8:9, :]
    def neighbours(ref, r, _):
        return beside_rows(ref, edge, pos, r)

    for r in range(8):
        at = slice(8 * r, 8 * r + 8)
        smp[8 + 8 * r : 16 + 8 * r, :] = neighbours(oldp, r, 8 + 8 * r)

    def halves(at, block):
        inv_h[at : at + 16, :], inv_l[at : at + 16, :] = split(block)

    halves(0, cinv[...])
    for k in range(3):
        etab[k, 0:2, :] = hr[0, 16 + 2 * k : 18 + 2 * k, :]
        etab[k, 10:12, :] = hr[1, 16 + 2 * k : 18 + 2 * k, :]
        eedge[k, 0:2, :] = hr[0, 22 + 2 * k : 24 + 2 * k, :]
        eedge[k, 10:12, :] = hr[1, 22 + 2 * k : 24 + 2 * k, :]
    e_d[1:3, :] = hr[0, 28:30, :]
    e_d[11:13, :] = hr[1, 28:30, :]
    e_s[...] = RELAX / e_d[...]
    e_o[1:3, :] = hr[0, 30:32, :]
    e_o[11:13, :] = hr[1, 30:32, :]
    mark_owners((0, 1, 10, 11))
    for i in range(2):
        owner = spread(hr[i, 9:10, :], 128).astype(I32) & 127
        hot_n[i] = jnp.where(down == owner, 1.0, 0.0).astype(BF16)
    for f in range(4):
        high, low = split(prod[pl.ds(f, 160, stride=4), :])
        both = dot(member[...], jnp.concatenate([high, low], axis=1), NN)
        recv[pl.ds(f, 64, stride=4), :] = both[:, 0:128] + both[:, 128:256]

    for r in range(8):
        at = slice(8 * r, 8 * r + 8)
        out = base[at, :]
        for f in range(4):
            out = out + fw_s[0, f] * recv[pl.ds(32 * r + f, 8, stride=4), :]
        base[at, :] = out
        prev = oldh[at, :]
        beside = smp[8 + 8 * r : 16 + 8 * r, :]
        smp[8 + 8 * r : 16 + 8 * r, :] = (
            prev + (out - (whole[at, :] * prev - beside)) * scale[at, :]
        )

    pl.semaphore_wait(space_sem, 3)
    sm_copies = pair(smp.at[pl.ds(8, 8)], sm_r, smp.at[pl.ds(64, 8)], sm_l, sm_ss, sm_rs)
    for c in sm_copies:
        c.start()
    inv_copies[0].start()
    smp[7:8, :] = jnp.zeros((1, 128), F32)
    smp[72:73, :] = jnp.zeros((1, 128), F32)

    def spot(row, owner):
        mine = jnp.where(spread(owner >> 7) == row8, spread(row), 0.0)
        return jnp.concatenate(list(split_f32(mine)), axis=0).astype(BF16)

    for r in range(8):
        at = slice(8 * r, 8 * r + 8)
        cur = smp[8 + 8 * r : 16 + 8 * r, :]
        res = base[at, :] - (whole[at, :] * cur - neighbours(smp, r, 8 + 8 * r))
        rests[0, at, :], rests[1, at, :] = split_f32(res)
        for a in range(8 * r, 8 * r + 8):
            mask = upper[8 * a : 8 * a + 8, :]
            lhs[:, 128 * a : 128 * a + 128] = jnp.concatenate(
                [mask * spread(rests[i, a : a + 1, :]) for i in range(2)], axis=0
            ).astype(BF16)
    def from_here(i, row, towards):
        row = spread(row)
        out = jnp.zeros((8, 128), F32)
        for k in range(3):
            p = spread(hr[i, 10 + k : 11 + k, :]).astype(I32)
            term = spread(hr[i, 13 + k : 14 + k, :]) * take(row, p & 127)
            out = out + jnp.where(towards(p), term, 0.0)
        both = dot(jnp.concatenate(list(split_f32(out)), axis=0).astype(BF16), hot_n[i], NT)
        return both[0:1] + both[8:9]

    extra_l = from_here(0, smp[8:9, :], lambda p: p > 127)
    extra_r = from_here(1, smp[71:72, :], lambda p: p < 0)
    for r in range(2):
        where = slice(4096 * r, 4096 * r + 4096)
        seg[r] = dot(lhs[:, where], hot[where, :], NN)
    source = (seg[0, 0:8] + seg[0, 8:16]) + (seg[1, 0:8] + seg[1, 8:16])
    cs_s[...] = source
    cs_copies = pair(cs_s, cs_r, cs_s, cs_l, cs_ss, cs_rs)
    for c in cs_copies:
        c.start()

    cs[...] = jnp.zeros((24, 128), F32)
    cs[2:3, :] = extra_l
    cs[3:11, :] = source
    cs[11:12, :] = extra_r
    cf[...] = jnp.zeros((24, 128), F32)
    cs2[...] = jnp.zeros((24, 128), F32)
    cf[0:16, :] = cs[0:16, :] * e_s[0:16, :]

    def coarse_neighbours(ref):
        out = None
        for k in range(3):
            term = eedge[k] * pick(
                ref[0:16, :], ref[1:17, :], ref[2:18, :], etab[k].astype(I32)
            )
            out = term if out is None else out + term
        return out

    left_over = cs[1:17, :] - e_d[1:17, :] * cf[1:17, :] + coarse_neighbours(cf)
    klhs[...] = jnp.zeros((8, 1536), F32)
    for r in range(12):
        klhs[0:1, 128 * r : 128 * r + 128] = left_over[r : r + 1]
    packed = jnp.concatenate(list(split_f32(klhs[...])), axis=0).astype(BF16)
    for r in range(2):
        where = slice(768 * r, 768 * r + 768)
        segk[r] = dot(packed[:, where], khot[:, where], NT)
    pay[0] = (segk[0, 0:1] + segk[0, 8:9]) + (segk[1, 0:1] + segk[1, 8:9])
    gb[t] = pay[0]

    hops = (0, 1, 2, 1)
    others = sorted(
        ((a, b, c) for a in range(4) for b in range(4) for c in range(4)),
        key=lambda d: (
            d == (0, 0, 0), -(hops[d[0]] + hops[d[1]] + hops[d[2]]), (d[1], d[2]) != (1, 1)
        ),
    )[:-1]
    for a, b, c in others:
        pltpu.make_async_remote_copy(
            src_ref=pay,
            dst_ref=gb.at[pl.ds(t, 1)],
            send_sem=ag_ss,
            recv_sem=ag_rs,
            device_id=(g, xs[a] + zs[b] + ys[c]),
            device_id_type=MESH,
        ).start()

    inv_copies[1].wait_recv()
    halves(16, invr[0])
    for c in sm_copies:
        c.wait_send()
        c.wait_recv()
    smp[7:8, :] = sm_l[7:8, :]
    smp[72:73, :] = sm_r[0:1, :]
    far_l, far_r = spread(sm_l[7:8, :]), spread(sm_r[0:1, :])
    more_l = more_r = jnp.zeros((8, 128), F32)
    for k in range(3):
        p = pos[k, 0:8, :]
        more_l = more_l + jnp.where(p < 0, edge[k, 0:8, :] * take(far_l, p & 127), 0.0)
        p = pos[k, 56:64, :]
        more_r = more_r + jnp.where(p > 127, edge[k, 56:64, :] * take(far_r, p & 127), 0.0)
    sums = dot(spot(more_l[0:1], fown[0:1, :]), hot[0:128, :], NN)
    sums = sums + dot(spot(more_r[7:8], fown[63:64, :]), hot[8064:8192, :], NN)
    more = sums[0:8] + sums[8:16]
    inv_copies[0].wait_recv()
    halves(32, invr[1])
    for c in cs_copies:
        c.wait_recv()
    cs[1:3, :] = cs_l[6:8, :] + cs[1:3, :]
    cs[3:11, :] = cs[3:11, :] + more
    cs[11:13, :] = cs_r[0:2, :] + cs[11:13, :]
    cf[0:16, :] = cs[0:16, :] * e_s[0:16, :]

    everyone = pltpu.make_async_remote_copy(
        src_ref=gb.at[pl.ds(0, n - 1)],
        dst_ref=gb.at[pl.ds(0, n - 1)],
        send_sem=ag_ss,
        recv_sem=ag_rs,
        device_id=(g, right),
        device_id_type=MESH,
    )
    everyone.wait_recv()
    from_right = (row8 == 0) & (lane8 >= 112)
    from_left = (row8 == 7) & (lane8 < 16)
    groups = [gb[8 * j : 8 * j + 8, 0, :] for j in range(8)]
    flat = []
    for j in range(8):
        mix = jnp.where(
            from_right, groups[(j + 1) % 8], jnp.where(from_left, groups[(j - 1) % 8], groups[j])
        )
        flat.append(jnp.sum(mix, axis=0, keepdims=True))
    flat = spread_all(jnp.concatenate(flat, axis=1))
    packed = jnp.concatenate(list(split_f32(flat)), axis=0).astype(BF16)
    by_h, by_l = dot(packed, inv_h[...], NT), dot(packed, inv_l[...], NT)
    value = (by_h[0:1] + by_h[8:9]) + (by_l[0:1] + by_l[8:9])
    value = jnp.concatenate([value, jnp.zeros((1, 80), F32)], axis=1)
    value = spread(value, 16)
    shift = jnp.where(row16 < 3, 16, jnp.where(row16 < 11, 0, 32))
    cs2[0:16, :] = cf[0:16, :] + take(value, jnp.minimum(e_o[0:16, :].astype(I32), 15) + shift)
    cur = cs2[1:17, :]
    rest = cs[1:17, :] - (e_d[1:17, :] * cur - coarse_neighbours(cs2))
    t3[...] = cur + rest * e_s[1:17, :]

    own_l = spread(hr[0, 9:10, :]).astype(I32) & 127
    own_r = spread(hr[1, 9:10, :]).astype(I32) & 127
    smp[7:8, :] = smp[7:8, :] + take(spread(t3[1:2, :]), own_l)[0:1]
    smp[72:73, :] = smp[72:73, :] + take(spread(t3[10:11, :]), own_r)[0:1]

    for c in halo_copies + surf_copies + inv_copies + cs_copies:
        c.wait_send()
    everyone.wait_send()

    @pl.when(seat == 0)
    def _():
        halo_on.wait_send()
        surf_on[0].wait_send()

    @pl.when(seat < 2)
    def _():
        surf_on[1].wait_send()


def finish(
    newf, recv, smp, t3, base, pos, whole, scale, edge, fown, new_out, recv_out, height_out,
    cop, height, sems,
):
    copies = [
        pltpu.make_async_copy(source, target, sems.at[i])
        for i, (source, target) in enumerate(
            ((newf, new_out), (recv, recv_out), (height, height_out))
        )
    ]
    copies[0].start()
    copies[1].start()
    for r in range(8):
        at = slice(8 * r, 8 * r + 8)
        owner = fown[at, :]
        high, lane = owner >> 7, owner & 127
        out = smp[8 + 8 * r : 16 + 8 * r, :]
        for a in range(8):
            out = out + jnp.where(high == a, take(spread(t3[2 + a : 3 + a, :]), lane), 0.0)
        cop[8 + 8 * r : 16 + 8 * r, :] = out
    cop[7:8, :] = smp[7:8, :]
    cop[72:73, :] = smp[72:73, :]
    for r in range(8):
        at = slice(8 * r, 8 * r + 8)
        cur = cop[8 + 8 * r : 16 + 8 * r, :]
        rest = base[at, :] - (whole[at, :] * cur - beside_rows(cop, edge, pos, r))
        height[at, :] = cur + rest * scale[at, :]
    copies[2].start()
    for copy in copies:
        copy.wait()


def beside_rows(ref, edge, pos, r):
    out = None
    row = 8 + 8 * r
    prev, cur, nxt = ref[row - 1 : row + 7, :], ref[row : row + 8, :], ref[row + 1 : row + 9, :]
    for k in range(3):
        at = slice(8 * r, 8 * r + 8)
        term = edge[k, at, :] * pick(prev, cur, nxt, pos[k, at, :])
        out = term if out is None else out + term
    return out


def split_f32(x):
    high = x.astype(BF16).astype(F32)
    return high, x - high


def spread_all(row):
    return jnp.broadcast_to(row, (8, row.shape[1]))


def per_device(
    fields, level_rate, edge_weight, fine_diagonal, fine_table, old_height, level_weight,
    flux_weight, fine_owner, coarse_table, coarse_edge, coarse_diagonal, coarse_owner,
    coarse_inverse, surface_out, send_blocks, entry_slot, entry_block, remap_tiles,
):
    operands = (
        fields.reshape(8, 64, 128).transpose(1, 0, 2),
        level_rate,
        edge_weight.reshape(3, 64, 128),
        fine_diagonal.reshape(64, 128),
        fine_table.reshape(3, 64, 128),
        old_height.reshape(64, 128),
        level_weight,
        flux_weight,
        fine_owner.reshape(64, 128),
        coarse_table.reshape(3, 8, 128),
        coarse_edge.reshape(3, 8, 128),
        coarse_diagonal.reshape(8, 128),
        coarse_owner.reshape(8, 128),
        coarse_inverse.reshape(16, 1024),
        surface_out.reshape(4, 64, 128).transpose(1, 0, 2),
        send_blocks.reshape(1, 160),
        entry_slot.reshape(1, 160),
        entry_block.reshape(1, 160),
        remap_tiles.reshape(160, 128, 128),
    )
    vmem = pl.BlockSpec(memory_space=pltpu.VMEM)
    specs = [pl.BlockSpec(memory_space=pltpu.HBM)] * 19
    V = pltpu.VMEM
    local = [
        (pltpu.SMEM if i in (1, 6, 7, 15, 16) else V)(x.shape, x.dtype)
        for i, x in enumerate(operands)
        if i not in (2, 8)
    ]
    shape = jax.ShapeDtypeStruct
    D = pltpu.SemaphoreType.DMA
    made = pl.pallas_call(
        kernel,
        out_shape=(
            shape((64, 8, 128), F32),
            shape((256, 128), F32),
            shape((80, 128), F32),
            shape((16, 128), F32),
            shape((64, 128), F32),
            shape((3, 64, 128), I32),
            shape((64, 128), F32),
            shape((64, 128), F32),
            shape((3, 64, 128), F32),
            shape((64, 128), I32),
        ),
        in_specs=specs,
        out_specs=(vmem,) * 10,
        scratch_shapes=[
            *local,
            V((160, 4, 128), BF16),
            V((160, 4, 128), BF16),
            V((2, 32, 128), F32),
            V((2, 32, 128), F32),
            V((2, 16, 1024), F32),
            V((8, 128), F32),
            V((8, 128), F32),
            V((8, 128), F32),
            V((8, 128), F32),
            V((1, 1, 128), F32),
            V((8, 128), F32),
            V((64, 1, 128), F32),
            V((64, 160), BF16),
            V((640, 128), F32),
            V((640, 128), F32),
            V((8192, 128), BF16),
            V((512, 128), F32),
            V((2, 64, 128), F32),
            V((16, 8192), BF16),
            V((2, 16, 128), F32),
            V((80, 128), F32),
            V((3, 16, 128), F32),
            V((3, 16, 128), F32),
            V((24, 128), F32),
            V((24, 128), F32),
            V((24, 128), F32),
            V((16, 128), I32),
            V((24, 128), F32),
            V((24, 128), F32),
            V((24, 128), F32),
            V((128, 1536), BF16),
            V((8, 1536), F32),
            V((2, 128, 128), BF16),
            V((3, 64, 128), F32),
            V((48, 1024), BF16),
            V((48, 1024), BF16),
            V((2, 16, 128), F32),
            V((2, 32, 4, 128), BF16),
            V((32, 128), F32),
            D((18,)),
            D((4,)),
            D((5,)), D((5,)),
            D((2,)), D((2,)),
            D((2,)), D((2,)),
            D((2,)), D((2,)),
            D((2,)), D((2,)),
            D, D,
            pltpu.SemaphoreType.REGULAR, pltpu.SemaphoreType.REGULAR,
            D((2,)), D((2,)), D, D,
        ],
        compiler_params=pltpu.CompilerParams(
            collective_id=0, has_side_effects=True, vmem_limit_bytes=48 << 20
        ),
        name="step",
    )(*[pltpu.with_memory_space_constraint(x, pltpu.HBM) for x in operands])
    new, got, high = pl.pallas_call(
        finish,
        out_shape=(shape((64, 8, 128), F32), shape((256, 128), F32), shape((64, 128), F32)),
        in_specs=[vmem] * 10,
        out_specs=[pl.BlockSpec(memory_space=pltpu.HBM)] * 3,
        scratch_shapes=[V((80, 128), F32), V((64, 128), F32), D((3,))],
        compiler_params=pltpu.CompilerParams(vmem_limit_bytes=1 << 20),
        name="finish",
    )(*made)
    return (
        new.transpose(1, 0, 2).reshape(1, 8, 8192),
        got.reshape(64, 4, 128).transpose(1, 0, 2).reshape(1, 4, 8192),
        high.reshape(1, 8192),
    )


def solution(mesh):
    in_specs = (
        P("comp", None, "tile"),
        P("comp", None),
        P("comp", None, "tile"),
        P("comp", "tile"),
        P("comp", None, "tile"),
        P("comp", "tile"),
        P("comp", None),
        P("comp", None),
        P("comp", "tile"),
        P("comp", None, "tile"),
        P("comp", None, "tile"),
        P("comp", "tile"),
        P("comp", "tile"),
        P("comp", "tile", None),
        P("comp", None, "tile"),
        P("comp", "tile", None),
        P("comp", "tile", None),
        P("comp", "tile", None),
        P("comp", "tile", None, None, None),
    )
    out_specs = (P("comp", None, "tile"), P("comp", None, "tile"), P("comp", "tile"))
    return jax.shard_map(
        per_device, mesh=mesh, in_specs=in_specs, out_specs=out_specs, check_vma=False
    )
```
